128 devices in a mesh: gx: 4 (over z_lo, core), gy: 8 (over x, z_hi), gz: 4 (over y).
Axes of the slice: x: 4, y: 4, z: 4 (z_hi: 2, z_lo: 2; z = z_hi * 2 + z_lo), core: 2. Of those that a mesh axis runs over, the one named last changes fastest.
Arguments:
- factor: bfloat16 [4096, 4096], P(None, ('gx', 'gy')), may hold values from -1 to 1, as said below
- kriging: bfloat16 [768, 4096], replicated, may hold values from -0.75 to 0.75
- normals: bfloat16 [4, 8, 4, 8, 8, 4096], P('gx', 'gy', 'gz'), may hold values from -6 to 6
- visit_order: int32 [4, 8, 4, 8], P('gx', 'gy', 'gz'), may hold values from 0 to 7, each once within a row
Outputs:
- evolved: float32 [8, 16, 8, 8, 4096], P('gx', 'gy', 'gz')
The draws below stay inside these ranges and needn't reach their ends.
Inputs may be any that keep to these rules, and one draw needn't show every extreme that they name: `visit_order`: each device block's 8 entries name each of its draws once. `factor`: zero below the diagonal; diagonal entries between 0.5 and 1.
All inputs are finite; a program needn't handle non-finite values.
Results may differ from the reference program's by a relative error of at most 0.013.
Values may be sent and summed in bfloat16 or wider, within the bound.
No kernel may reach another device: no remote copies, remote signals or barrier semaphores. Data moves between devices by JAX's collectives and lax.ppermute only.
A program may use at most 128 MiB of HBM per device.

```python
import math
import jax
import jax.numpy as jnp
from jax import lax

TILE = 16
CELLS = 4096
FACE = 256
BX = 2
BY = 2
BZ = 2
TILES_DEV = 8
REALIZATIONS = 8
N_GX = 4
N_GY = 8
N_GZ = 4


def draw_factor(key, part):
    key_entries = jax.random.fold_in(key, 11)
    key_diagonal = jax.random.fold_in(key, 23)
    entries = jnp.clip(jax.random.normal(key_entries, (CELLS, CELLS), jnp.float32), -4.0, 4.0)
    diagonal = jax.random.uniform(key_diagonal, (CELLS,), jnp.float32, 0.5, 1.0)
    upper_part = jnp.triu(entries / math.sqrt(CELLS), 1)
    return (upper_part + jnp.diag(diagonal)).astype(jnp.bfloat16)


def draw_kriging(key, part):
    key_entries = jax.random.fold_in(key, 37)
    side_scale = math.sqrt(0.15 / FACE)
    chain_scale = math.sqrt(0.5 / FACE)
    row_scale = jnp.concatenate([jnp.full((FACE, 1), side_scale, jnp.float32), jnp.full((FACE, 1), chain_scale, jnp.float32), jnp.full((FACE, 1), side_scale, jnp.float32)], 0)
    entries = jnp.clip(jax.random.normal(key_entries, (3 * FACE, CELLS), jnp.float32), -4.0, 4.0)
    return (entries * row_scale).astype(jnp.bfloat16)


def steps_of(own_key, dims, pieces, low, largest):
    loudness = 1.0
    for position, blocks in pieces:
        steps = jax.random.uniform(jax.random.fold_in(jax.random.fold_in(own_key, 6), position), (blocks,), jnp.float32, low / len(pieces), largest / len(pieces))
        loudness = loudness * jnp.repeat(jnp.exp(steps), dims[position] // blocks).reshape((-1,) + (1,) * (len(dims) - 1 - position))
    return loudness


def normal_values(stream_key, shape, deviation, bound, shards=(), dtype=jnp.bfloat16):
    values = deviation * jax.random.normal(stream_key, shape, jnp.float32)
    if shards:
        values = values * steps_of(stream_key, shape, shards, -0.22, 0.18)
    return jnp.clip(values, -bound, bound).astype(dtype)


def setup_inputs(seed: int = 0) -> dict:
    arg_keys = jax.random.split(jax.random.key(seed), 5)
    return {
        "factor": draw_factor(jax.random.fold_in(arg_keys[4], 71), 0),
        "kriging": draw_kriging(jax.random.fold_in(arg_keys[4], 71), 0),
        "normals": normal_values(arg_keys[2], (N_GX, N_GY, N_GZ, TILES_DEV, REALIZATIONS, CELLS), 1.0, 6.0, ((0, 4), (1, 8), (2, 4))),
        "visit_order": jax.vmap(lambda own: jax.random.permutation(own, TILES_DEV))(jax.random.split(arg_keys[3], N_GX * N_GY * N_GZ)).reshape((N_GX, N_GY, N_GZ, TILES_DEV)).astype(jnp.int32),
    }


def cube_of(values):
    return values.reshape(values.shape[:-1] + (TILE, TILE, TILE))


def face_x(values):
    return cube_of(values)[..., TILE - 1, :, :].reshape(values.shape[:-1] + (FACE,))


def face_y(values):
    return cube_of(values)[..., :, TILE - 1, :].reshape(values.shape[:-1] + (FACE,))


def face_z(values):
    return cube_of(values)[..., :, :, TILE - 1].reshape(values.shape[:-1] + (FACE,))


def reference(factor, kriging, normals, visit_order):
    blocks = N_GX * N_GY * N_GZ
    tiles_dev = BX * BY * BZ
    ensemble = normals.shape[4]
    drawn_rows = normals.reshape(blocks, tiles_dev, ensemble, CELLS)
    indices = visit_order.reshape(blocks, tiles_dev).astype(jnp.int32)
    ordered = jax.vmap(lambda source, picked: jnp.take(source, picked, axis=0))(drawn_rows, indices)
    flat_rows = ordered.reshape(blocks * tiles_dev * ensemble, CELLS)
    noise_term = jnp.dot(flat_rows, factor, preferred_element_type=jnp.float32)
    noise_term = noise_term.reshape(N_GX, N_GY, N_GZ, BX, BY, BZ, ensemble, CELLS)
    noise_term = noise_term.transpose(0, 3, 1, 4, 2, 5, 6, 7)
    span_x = N_GX * BX
    span_y = N_GY * BY
    span_z = N_GZ * BZ
    noise_term = noise_term.reshape(span_x, span_y, span_z, ensemble, CELLS)
    padded = jnp.zeros((span_x + 1, span_y + 1, span_z + 1, ensemble, CELLS), jnp.float32)
    zero_index = jnp.zeros((), jnp.int32)

    def tile_at(grid, first, second, third):
        return lax.dynamic_slice(grid, (first, second, third, zero_index, zero_index), (1, 1, 1, ensemble, CELLS))[0, 0, 0]

    def visit_tile(number, grid):
        number = jnp.asarray(number).astype(jnp.int32)
        i = (number // (span_y * span_z)).astype(jnp.int32)
        j = ((number // span_z) % span_y).astype(jnp.int32)
        k = (number % span_z).astype(jnp.int32)
        up_x = tile_at(grid, i, j + 1, k + 1)
        up_y = tile_at(grid, i + 1, j, k + 1)
        up_z = tile_at(grid, i + 1, j + 1, k)
        upstream = jnp.concatenate([face_x(up_x), face_y(up_y), face_z(up_z)], -1).astype(jnp.bfloat16)
        own_term = tile_at(noise_term, i, j, k)
        result = jnp.dot(upstream, kriging, preferred_element_type=jnp.float32) + own_term
        return lax.dynamic_update_slice(grid, result[None, None, None], (i + 1, j + 1, k + 1, zero_index, zero_index))

    padded = lax.fori_loop(0, span_x * span_y * span_z, visit_tile, padded)
    return padded[1:, 1:, 1:]
```

```python
import functools

import jax
import jax.numpy as jnp
import numpy as np
from jax import lax
from jax.experimental import pallas as pl
from jax.experimental.pallas import tpu as pltpu
from jax.sharding import PartitionSpec as P

TILE = 16
CELLS = 4096
FACE = 256
BX = 2
BY = 2
BZ = 2
TILES = 8
ENS = 8
N_GX = 4
N_GY = 8
N_GZ = 4
SPAN_X = N_GX * BX
SPAN_Y = N_GY * BY
SPAN_Z = N_GZ * BZ
LEVELS = SPAN_X + SPAN_Y + SPAN_Z - 2
COLS_DEV = CELLS // (N_GX * N_GY)
PART = COLS_DEV // N_GZ
HALF = PART // 2
STATE = 3 * FACE
PLANES = STATE // 128
SLOTS = SPAN_Y + SPAN_X - 1 + SPAN_Z - 1 + 14

BF = jnp.bfloat16
F32 = jnp.float32


def part_column(q, part):
    rows = q // 4
    return rows * TILE + 4 * ((part - rows) % 4) + q % 4


def state_order():
    rows = np.zeros(STATE, np.int32)
    cells = np.zeros(STATE, np.int32)
    for f in range(STATE):
        plane, lane = divmod(f, 128)
        if plane < 4:
            s, slot = plane, lane % 64
            if lane < 64:
                i, q = 30 + slot // 32, slot % 32
                v, w = 8 * (i % 2) + q // 4, 4 * ((s - q // 4) % 4) + q % 4
                rows[f], cells[f] = v * 16 + w, (15 * 16 + v) * 16 + w
            else:
                u, w = slot // 4, 4 * ((s - 15) % 4) + slot % 4
                rows[f], cells[f] = FACE + u * 16 + w, (u * 16 + 15) * 16 + w
        else:
            s, slot = 2 * (plane - 4) + lane // 64, lane % 64
            i, e = slot // 2, slot % 2
            u, v = i // 2, 8 * (i % 2) + 4 * e + (s + 1) % 4
            rows[f], cells[f] = 2 * FACE + u * 16 + v, (u * 16 + v) * 16 + 15
    return rows, cells


STATE_ROWS, STATE_CELLS = state_order()


def one_hot(condition):
    return condition.astype(BF)


def iota(shape, axis):
    return lax.broadcasted_iota(jnp.int32, shape, axis)


def to_bf16_dot(left, right):
    return jnp.dot(left, right, preferred_element_type=F32).astype(BF)


def plane_shift(value, dx, dz, dc):
    pairs = []
    for gx in range(N_GX):
        for gy in range(N_GY):
            x, z, core = gy // 2, (gy % 2) * 2 + gx // 2, gx % 2
            x, z, core = (x + dx) % 4, (z + dz) % 4, core ^ dc
            pairs.append((gx * N_GY + gy, ((z % 2) * 2 + core) * N_GY + x * 2 + z // 2))
    return lax.ppermute(value, ("gx", "gy"), pairs)


def line_shift(value, steps):
    return lax.ppermute(value, "gz", [(s, (s + steps) % N_GZ) for s in range(N_GZ)])


def noise_kernel(place, select, row_order, *refs):
    row_refs = refs[:4]
    piece_refs = refs[4:20]
    noise_out, face_out = refs[20:22]
    rows, factors, acc, sums, sem_rows, sem_factor = refs[22:]
    x, z, core, gz = place[0], place[1], place[2], place[3]
    copies = []
    for back in range(N_GZ):
        copies.append(
            pltpu.make_async_copy(
                row_refs[back], rows.at[lax.rem(gz - back + N_GZ, N_GZ)], sem_rows
            )
        )
    for half in range(2):
        for outer in range(4):
            for swap in range(2):
                ref = piece_refs[half * 8 + outer * 2 + swap]
                for inner in range(4):
                    dx, dz = (inner, outer) if half == 0 else (outer, inner)
                    sx = lax.rem(x - dx + 4, 4)
                    sz = lax.rem(z - dz + 4, 4)
                    sc = core if swap == 0 else 1 - core
                    sgx = lax.rem(sz, 2) * 2 + sc
                    sgy = sx * 2 + sz // 2
                    copies.append(
                        pltpu.make_async_copy(
                            ref.at[pl.ds(inner * HALF, HALF)],
                            factors.at[(sgx * N_GY + sgy) * 2 + half],
                            sem_factor.at[sgx],
                        )
                    )
    for copy in copies:
        copy.start()
    pltpu.make_async_copy(rows, rows, sem_rows).wait()
    sums[...] = jnp.zeros_like(sums)
    per = N_GY * 2
    wide = N_GY * PART
    for g in range(N_GX):
        block = factors.at[pl.ds(g * per, per)]
        pltpu.make_async_copy(block, block, sem_factor.at[g]).wait()
        acc[...] = jnp.zeros_like(acc)

        @pl.loop(0, g + 1)
        def _(chunk):
            span = pl.ds(pl.multiple_of(chunk * 1024, 1024), 1024)
            acc[...] += lax.dot_general(
                rows[:, :, span].reshape(N_GZ * 64, 1024),
                factors[g * per : (g + 1) * per, :, span].reshape(wide, 1024),
                (((1,), (1,)), ((), ())),
                preferred_element_type=F32,
            )

        rounded = acc[...].astype(BF)
        noise_out[:, g * wide : (g + 1) * wide] = rounded
        sums[...] += jnp.dot(
            rounded, select[g * wide : (g + 1) * wide, :], preferred_element_type=F32
        )
    faces = jnp.dot(row_order[...], sums[...].astype(BF), preferred_element_type=F32)
    low = iota((16, 128), 1) < 64
    for r in range(ENS):
        face_out[r, 0:32, :] = faces[r * 32 : (r + 1) * 32, :128].astype(BF)
        first = faces[r * 32 : r * 32 + 16, 128:]
        second = faces[r * 32 + 16 : r * 32 + 32, 128:]
        face_out[r, 32:48, :] = jnp.where(low, first, second).astype(BF)


def sweep_kernel(place, received, step, out, noise, history, state, picked):
    gx, gz = place[0], place[3]
    low8 = iota((8, 128), 1) < 64

    noise[...] = jnp.zeros_like(noise)

    @pl.loop(0, N_GX * N_GY)
    def _(block):
        bx = block // N_GY
        by = lax.rem(block, N_GY)
        for a in range(BX):
            planes = []
            for s in range(N_GZ):
                planes.append(received[block * N_GZ + s, a * 16 : (a + 1) * 16, :].astype(F32))
            zs = [received[block * N_GZ + s, 32:48, :].astype(F32) for s in range(N_GZ)]
            for pair in range(2):
                first, second = zs[2 * pair], zs[2 * pair + 1]
                if a == 0:
                    second = pltpu.roll(second, 64, 1)
                else:
                    first = pltpu.roll(first, 64, 1)
                planes.append(jnp.where(iota((16, 128), 1) < 64, first, second))
            for b in range(BY):
                start = ((bx * BX + a) * SLOTS + by * BY + b + 14) * 8
                start = pl.multiple_of(start, 8)
                for p in range(PLANES):
                    noise[p, pl.ds(start, 8), :] = planes[p][b * 8 : (b + 1) * 8]

    state[...] = jnp.zeros_like(state)
    low = iota((64, 128), 1) < 64
    has_below = (iota((64, 128), 0) % 8) != 7

    @pl.loop(0, LEVELS)
    def _(level):
        upstream = []
        for p in range(PLANES):
            here = state[p]
            if p < 4:
                west = jnp.concatenate([jnp.zeros((8, 128), F32), here[:56]], 0)
                value = jnp.where(low, west, here)
            else:
                value = jnp.where(has_below, pltpu.roll(here, 63, 0), 0.0)
            history[p, pl.ds(pl.multiple_of(level * 64, 64), 64), :] = value
            upstream.append(value.astype(BF))
        result = jnp.dot(jnp.concatenate(upstream, 1), step[...], preferred_element_type=F32)
        for p in range(PLANES):
            rows = []
            for i in range(SPAN_X):
                start = (i * SLOTS + level - i + 7) * 8
                rows.append(noise[p, pl.ds(start, 8, stride=9), :])
            state[p] = result[:, p * 128 : (p + 1) * 128] + jnp.concatenate(rows, 0)

    for a in range(BX):
        for b in range(BY):
            for c in range(BZ):
                i = gx * BX + a
                k = gz * BZ + c
                start = (i + k + b) * 64 + i * 8 + 7 - k
                for p in range(PLANES):
                    picked[p, pl.ds((a * BY + b) * BZ + c, 8, stride=8), :] = history[
                        p, pl.ds(start, 8, stride=128), :
                    ]
    for p in range(PLANES):
        out[:, p * 128 : (p + 1) * 128] = picked[p].astype(BF)


def final_kernel(faces, swap_rows, kriging, noise, spread, out):
    upstream = jnp.dot(swap_rows[...], faces[...], preferred_element_type=F32).astype(BF)
    total = jnp.dot(upstream, kriging[...], preferred_element_type=F32)
    for s in range(N_GZ):
        total += jnp.dot(noise[s], spread[s], preferred_element_type=F32)
    out[...] = total


def local(factor, kriging, normals, visit_order):
    gx = lax.axis_index("gx")
    gy = lax.axis_index("gy")
    gz = lax.axis_index("gz")
    place = jnp.stack([gy // 2, (gy % 2) * 2 + gx // 2, gx % 2, gz]).astype(jnp.int32)
    sweep_place = jnp.stack([gx, gy, gx, gz]).astype(jnp.int32)
    vmem = pl.BlockSpec(memory_space=pltpu.VMEM)
    smem = pl.BlockSpec(memory_space=pltpu.SMEM)
    anywhere = pl.BlockSpec(memory_space=pl.ANY)

    drawn = normals.reshape(TILES, ENS, CELLS)
    ordered = drawn.at[visit_order.reshape(TILES)].get(mode="promise_in_bounds")
    ordered = ordered.reshape(TILES * ENS, CELLS)
    row_pieces = [ordered] + [line_shift(ordered, s) for s in (1, 2, 3)]

    own = one_hot(iota((PART, COLS_DEV), 1) == part_column(iota((PART, COLS_DEV), 0), gz))
    shard = lax.dot_general(
        own, factor, (((1,), (1,)), ((), ())), preferred_element_type=F32
    ).astype(BF)
    first, second = shard[:HALF], shard[HALF:]
    along_x = jnp.concatenate([first] + [plane_shift(first, d, 0, 0) for d in (1, 2, 3)], 0)
    along_z = jnp.concatenate([second] + [plane_shift(second, 0, d, 0) for d in (1, 2, 3)], 0)
    pieces = []
    for piece in [along_x] + [plane_shift(along_x, 0, d, 0) for d in (1, 2, 3)]:
        pieces += [piece, plane_shift(piece, 0, 0, 1)]
    for piece in [along_z] + [plane_shift(along_z, d, 0, 0) for d in (1, 2, 3)]:
        pieces += [piece, plane_shift(piece, 0, 0, 1)]

    number = iota((N_GX * N_GY * PART, 256), 0)
    lane = iota((N_GX * N_GY * PART, 256), 1)
    i, q = number // PART, number % PART
    is_x = (lane < 64) & (i >= 30) & (lane == (i - 30) * 32 + q)
    is_y = (lane >= 64) & (lane < 128) & (i % 2 == 1) & (q >= 28)
    is_y = is_y & (lane - 64 == (i // 2) * 4 + q % 4)
    z_slot = i * 2 + q // 16
    is_z = (lane >= 128) & (q % 4 == 3) & ((gz - q // 4) % 4 == 3) & (lane % 64 == z_slot)
    select = one_hot(is_x | is_y | is_z)

    target, source = iota((256, 256), 0), iota((256, 256), 1)
    k = 7 - target % 8
    tile = (target // 8 % 4) * 2 + k % 2
    row_order = one_hot(source == (k // 2) * 64 + tile * 8 + target // 32)

    noise_part, faces = pl.pallas_call(
        noise_kernel,
        out_shape=(
            jax.ShapeDtypeStruct((N_GZ * 64, N_GX * N_GY * PART), BF),
            jax.ShapeDtypeStruct((ENS, 48, 128), BF),
        ),
        in_specs=[smem, vmem, vmem] + [anywhere] * 20,
        out_specs=(vmem, vmem),
        scratch_shapes=[
            pltpu.VMEM((N_GZ, 64, CELLS), BF),
            pltpu.VMEM((N_GX * N_GY * 2, HALF, CELLS), BF),
            pltpu.VMEM((256, 256), F32),
            pltpu.VMEM((256, 256), F32),
            pltpu.SemaphoreType.DMA,
            pltpu.SemaphoreType.DMA((N_GX,)),
        ],
        name="noise_part",
    )(place, select, row_order, *row_pieces, *pieces)

    copies = jnp.broadcast_to(faces[None, :, None], (N_GX, ENS, N_GZ, 48, 128))
    received = lax.all_to_all(
        copies.reshape(128, 48, 128), ("gx", "gy", "gz"), 0, 0, tiled=True
    )
    own_noise = lax.all_to_all(
        noise_part.reshape(N_GZ, 64, N_GX * N_GY * PART), "gz", 0, 0, tiled=True
    )

    rows_index = jnp.asarray(STATE_ROWS)
    cells_index = jnp.asarray(STATE_CELLS)
    reorder = one_hot(rows_index[:, None] == iota((STATE, STATE), 1))
    kriging_state = to_bf16_dot(reorder, kriging)
    to_state = one_hot(iota((CELLS, STATE), 0) == cells_index[None, :])
    step = to_bf16_dot(kriging_state, to_state)

    chosen = pl.pallas_call(
        sweep_kernel,
        out_shape=jax.ShapeDtypeStruct((64, STATE), BF),
        in_specs=[smem, vmem, vmem],
        out_specs=vmem,
        scratch_shapes=[
            pltpu.VMEM((PLANES, SPAN_X * SLOTS * 8, 128), F32),
            pltpu.VMEM((PLANES, LEVELS * 64, 128), F32),
            pltpu.VMEM((PLANES, 64, 128), F32),
            pltpu.VMEM((PLANES, 64, 128), F32),
        ],
        name="sweep",
    )(sweep_place, received, step)

    upstream = lax.all_to_all(
        chosen.reshape(N_GY, TILES, STATE), "gy", 0, 0, tiled=True
    ).reshape(ENS * TILES, STATE)

    target, source = iota((64, 64), 0), iota((64, 64), 1)
    swap_rows = one_hot(source == (target % 8) * 8 + target // 8)
    part, number, cell = (iota((N_GZ, 128, 512), axis) for axis in range(3))
    spread = one_hot(cell == (number // PART) * COLS_DEV + part_column(number % PART, part))

    out = pl.pallas_call(
        final_kernel,
        grid=(CELLS // 512,),
        out_shape=jax.ShapeDtypeStruct((TILES * ENS, CELLS), F32),
        in_specs=[
            pl.BlockSpec((64, STATE), lambda g: (0, 0)),
            pl.BlockSpec((64, 64), lambda g: (0, 0)),
            pl.BlockSpec((STATE, 512), lambda g: (0, g)),
            pl.BlockSpec((N_GZ, 64, 128), lambda g: (0, 0, g)),
            pl.BlockSpec((N_GZ, 128, 512), lambda g: (0, 0, 0)),
        ],
        out_specs=pl.BlockSpec((64, 512), lambda g: (0, g)),
        name="evolve",
    )(upstream, swap_rows, kriging_state, own_noise, spread)
    return out.reshape(BX, BY, BZ, ENS, CELLS)


def solution(mesh):
    placed = (
        P(None, ("gx", "gy")),
        P(),
        P("gx", "gy", "gz", None, None, None),
        P("gx", "gy", "gz", None),
    )
    return jax.shard_map(
        local,
        mesh=mesh,
        in_specs=placed,
        out_specs=P("gx", "gy", "gz", None, None),
        check_vma=False,
    )
```

```python
import functools

import jax
import jax.numpy as jnp
import numpy as np
from jax import lax
from jax.experimental import pallas as pl
from jax.experimental.pallas import tpu as pltpu
from jax.sharding import PartitionSpec as P

TILE = 16
CELLS = 4096
FACE = 256
BX = 2
BY = 2
BZ = 2
TILES = 8
ENS = 8
N_GX = 4
N_GY = 8
N_GZ = 4
SPAN_X = N_GX * BX
SPAN_Y = N_GY * BY
SPAN_Z = N_GZ * BZ
LEVELS = SPAN_X + SPAN_Y + SPAN_Z - 2
COLS_DEV = CELLS // (N_GX * N_GY)
PART = COLS_DEV // N_GZ
HALF = PART // 2
STATE = 3 * FACE
PLANES = STATE // 128
SLOTS = SPAN_Y + SPAN_X - 1 + SPAN_Z - 1 + 14

BF = jnp.bfloat16
F32 = jnp.float32


def part_column(q, part):
    rows = q // 4
    return rows * TILE + 4 * ((part - rows) % 4) + q % 4


def state_order():
    rows = np.zeros(STATE, np.int32)
    cells = np.zeros(STATE, np.int32)
    for f in range(STATE):
        plane, lane = divmod(f, 128)
        if plane < 4:
            s, slot = plane, lane % 64
            if lane < 64:
                i, q = 30 + slot // 32, slot % 32
                v, w = 8 * (i % 2) + q // 4, 4 * ((s - q // 4) % 4) + q % 4
                rows[f], cells[f] = v * 16 + w, (15 * 16 + v) * 16 + w
            else:
                u, w = slot // 4, 4 * ((s - 15) % 4) + slot % 4
                rows[f], cells[f] = FACE + u * 16 + w, (u * 16 + 15) * 16 + w
        else:
            s, slot = 2 * (plane - 4) + lane // 64, lane % 64
            i, e = slot // 2, slot % 2
            u, v = i // 2, 8 * (i % 2) + 4 * e + (s + 1) % 4
            rows[f], cells[f] = 2 * FACE + u * 16 + v, (u * 16 + v) * 16 + 15
    return rows, cells


STATE_ROWS, STATE_CELLS = state_order()


def one_hot(condition):
    return condition.astype(BF)


def iota(shape, axis):
    return lax.broadcasted_iota(jnp.int32, shape, axis)


def to_bf16_dot(left, right):
    return jnp.dot(left, right, preferred_element_type=F32).astype(BF)


def plane_shift(value, dx, dz, dc):
    pairs = []
    for gx in range(N_GX):
        for gy in range(N_GY):
            x, z, core = gy // 2, (gy % 2) * 2 + gx // 2, gx % 2
            x, z, core = (x + dx) % 4, (z + dz) % 4, core ^ dc
            pairs.append((gx * N_GY + gy, ((z % 2) * 2 + core) * N_GY + x * 2 + z // 2))
    return lax.ppermute(value, ("gx", "gy"), pairs)


def line_shift(value, steps):
    return lax.ppermute(value, "gz", [(s, (s + steps) % N_GZ) for s in range(N_GZ)])


def noise_kernel(place, select, row_order, *refs):
    row_refs = refs[:4]
    piece_refs = refs[4:20]
    noise_out, face_out = refs[20:22]
    rows, factors, acc, sums, sem_rows, sem_factor = refs[22:]
    x, z, core, gz = place[0], place[1], place[2], place[3]
    copies = []
    for back in range(N_GZ):
        copies.append(
            pltpu.make_async_copy(
                row_refs[back], rows.at[lax.rem(gz - back + N_GZ, N_GZ)], sem_rows
            )
        )
    for half in range(2):
        for outer in range(4):
            for swap in range(2):
                ref = piece_refs[half * 8 + outer * 2 + swap]
                for inner in range(4):
                    dx, dz = (inner, outer) if half == 0 else (outer, inner)
                    sx = lax.rem(x - dx + 4, 4)
                    sz = lax.rem(z - dz + 4, 4)
                    sc = core if swap == 0 else 1 - core
                    sgx = lax.rem(sz, 2) * 2 + sc
                    sgy = sx * 2 + sz // 2
                    copies.append(
                        pltpu.make_async_copy(
                            ref.at[pl.ds(inner * HALF, HALF)],
                            factors.at[(sgx * N_GY + sgy) * 2 + half],
                            sem_factor.at[sgx],
                        )
                    )
    for copy in copies:
        copy.start()
    pltpu.make_async_copy(rows, rows, sem_rows).wait()
    sums[...] = jnp.zeros_like(sums)
    per = N_GY * 2
    wide = N_GY * PART
    for g in range(N_GX):
        block = factors.at[pl.ds(g * per, per)]
        pltpu.make_async_copy(block, block, sem_factor.at[g]).wait()
        acc[...] = jnp.zeros_like(acc)

        @pl.loop(0, g + 1)
        def _(chunk):
            span = pl.ds(pl.multiple_of(chunk * 1024, 1024), 1024)
            acc[...] += lax.dot_general(
                rows[:, :, span].reshape(N_GZ * 64, 1024),
                factors[g * per : (g + 1) * per, :, span].reshape(wide, 1024),
                (((1,), (1,)), ((), ())),
                preferred_element_type=F32,
            )

        rounded = acc[...].astype(BF)
        noise_out[:, g * wide : (g + 1) * wide] = rounded
        sums[...] += jnp.dot(
            rounded, select[g * wide : (g + 1) * wide, :], preferred_element_type=F32
        )
    faces = jnp.dot(row_order[...], sums[...].astype(BF), preferred_element_type=F32)
    low = iota((8, 128), 1) < 64
    for r in range(ENS):
        for a in range(BX):
            base = r * 32 + a * 16
            face_out[a, r, 0:16, :] = faces[base : base + 16, :128].astype(BF)
            first = faces[base : base + 8, 128:]
            second = faces[base + 8 : base + 16, 128:]
            face_out[a, r, 16:24, :] = jnp.where(low, first, second).astype(BF)


def sweep_kernel(place, own_half, other_half, step, out, noise, history, state, picked):
    gx, core, gz = place[0], place[2], place[3]
    low8 = iota((8, 128), 1) < 64

    noise[...] = jnp.zeros_like(noise)

    @pl.loop(0, N_GX * N_GY)
    def _(block):
        bx = block // N_GY
        by = lax.rem(block, N_GY)
        for a, half in ((core, own_half), (1 - core, other_half)):
            planes = [half[block * N_GZ + s, 0:16, :].astype(F32) for s in range(N_GZ)]
            zs = [half[block * N_GZ + s, 16:24, :].astype(F32) for s in range(N_GZ)]
            for b in range(BY):
                start = ((bx * BX + a) * SLOTS + by * BY + b + 14) * 8
                start = pl.multiple_of(start, 8)
                for p in range(4):
                    noise[p, pl.ds(start, 8), :] = planes[p][b * 8 : (b + 1) * 8]
                for pair in range(2):
                    first, second = zs[2 * pair], zs[2 * pair + 1]
                    if b == 0:
                        second = pltpu.roll(second, 64, 1)
                    else:
                        first = pltpu.roll(first, 64, 1)
                    noise[4 + pair, pl.ds(start, 8), :] = jnp.where(low8, first, second)

    state[...] = jnp.zeros_like(state)
    low = iota((64, 128), 1) < 64
    has_below = (iota((64, 128), 0) % 8) != 7

    @pl.loop(0, LEVELS)
    def _(level):
        upstream = []
        for p in range(PLANES):
            here = state[p]
            if p < 4:
                west = jnp.concatenate([jnp.zeros((8, 128), F32), here[:56]], 0)
                value = jnp.where(low, west, here)
            else:
                value = jnp.where(has_below, pltpu.roll(here, 63, 0), 0.0)
            history[p, pl.ds(pl.multiple_of(level * 64, 64), 64), :] = value
            upstream.append(value.astype(BF))
        result = jnp.dot(jnp.concatenate(upstream, 1), step[...], preferred_element_type=F32)
        for p in range(PLANES):
            rows = []
            for i in range(SPAN_X):
                start = (i * SLOTS + level - i + 7) * 8
                rows.append(noise[p, pl.ds(start, 8, stride=9), :])
            state[p] = result[:, p * 128 : (p + 1) * 128] + jnp.concatenate(rows, 0)

    for a in range(BX):
        for b in range(BY):
            for c in range(BZ):
                i = gx * BX + a
                k = gz * BZ + c
                start = (i + k + b) * 64 + i * 8 + 7 - k
                for p in range(PLANES):
                    picked[p, pl.ds((a * BY + b) * BZ + c, 8, stride=8), :] = history[
                        p, pl.ds(start, 8, stride=128), :
                    ]
    for p in range(PLANES):
        out[:, p * 128 : (p + 1) * 128] = picked[p].astype(BF)


def natural_kernel(place, first, second, third, fourth, spread, out):
    gz = place[3]
    total = jnp.zeros((512, 512), F32)
    for back, part in enumerate((first, second, third, fourth)):
        source = lax.rem(gz - back + N_GZ, N_GZ)
        stacked = jnp.concatenate([part[:, g * 128 : (g + 1) * 128] for g in range(8)], 0)
        total += jnp.dot(stacked, spread[source], preferred_element_type=F32)
    for g in range(8):
        out[:, g * 512 : (g + 1) * 512] = total[g * 64 : (g + 1) * 64].astype(BF)


def final_kernel(faces, swap_rows, kriging, noise, out):
    upstream = jnp.dot(swap_rows[...], faces[...], preferred_element_type=F32).astype(BF)
    product = jnp.dot(upstream, kriging[...], preferred_element_type=F32)
    out[...] = product + noise[...].astype(F32)


def select_table():
    table = np.full((N_GZ, 3, N_GX * N_GY * PART), -1, np.int32)
    for s in range(N_GZ):
        for n in range(N_GX * N_GY * PART):
            i, q = n // PART, n % PART
            if i >= 30:
                table[s, 0, n] = (i - 30) * 32 + q
            if i % 2 == 1 and q >= 28:
                table[s, 1, n] = 64 + (i // 2) * 4 + q % 4
            if q % 4 == 3 and (s - q // 4) % 4 == 3:
                table[s, 2, n] = 128 + i * 2 + q // 16
    return table


def row_table():
    order = np.zeros(256, np.int32)
    for target in range(256):
        k = 7 - target % 8
        tile = (target // 8 % 4) * 2 + k % 2
        order[target] = (k // 2) * 64 + tile * 8 + target // 32
    return order


def spread_table():
    table = np.zeros((N_GZ, 128), np.int32)
    for s in range(N_GZ):
        for n in range(128):
            table[s, n] = (n // PART) * COLS_DEV + part_column(n % PART, s)
    return table


def own_table():
    return np.array([[part_column(q, s) for q in range(PART)] for s in range(N_GZ)], np.int32)


def local(factor, kriging, normals, visit_order):
    gx = lax.axis_index("gx")
    gy = lax.axis_index("gy")
    gz = lax.axis_index("gz")
    place = jnp.stack([gy // 2, (gy % 2) * 2 + gx // 2, gx % 2, gz]).astype(jnp.int32)
    sweep_place = jnp.stack([gx, gy, gx % 2, gz]).astype(jnp.int32)
    vmem = pl.BlockSpec(memory_space=pltpu.VMEM)
    smem = pl.BlockSpec(memory_space=pltpu.SMEM)
    anywhere = pl.BlockSpec(memory_space=pl.ANY)

    own_columns = jnp.asarray(own_table())[gz]
    own = one_hot(iota((PART, COLS_DEV), 1) == own_columns[:, None])
    shard = lax.dot_general(
        own, factor, (((1,), (1,)), ((), ())), preferred_element_type=F32
    ).astype(BF)
    first, second = shard[:HALF], shard[HALF:]
    along_x = jnp.concatenate([first] + [plane_shift(first, d, 0, 0) for d in (1, 2, 3)], 0)
    along_z = jnp.concatenate([second] + [plane_shift(second, 0, d, 0) for d in (1, 2, 3)], 0)

    drawn = normals.reshape(TILES, ENS, CELLS)
    ordered = drawn.at[visit_order.reshape(TILES)].get(mode="promise_in_bounds")
    ordered = ordered.reshape(TILES * ENS, CELLS)
    row_pieces = [ordered] + [line_shift(ordered, s) for s in (1, 2, 3)]

    kriging, along_x, along_z = lax.optimization_barrier((kriging, along_x, along_z))
    pieces = []
    for piece in [along_x] + [plane_shift(along_x, 0, d, 0) for d in (1, 2, 3)]:
        pieces += [piece, plane_shift(piece, 0, 0, 1)]
    for piece in [along_z] + [plane_shift(along_z, d, 0, 0) for d in (1, 2, 3)]:
        pieces += [piece, plane_shift(piece, 0, 0, 1)]

    reorder = one_hot(jnp.asarray(STATE_ROWS)[:, None] == iota((STATE, STATE), 1))
    kriging_state = to_bf16_dot(reorder, kriging)

    lane = iota((N_GX * N_GY * PART, 256), 1)
    lanes = jnp.asarray(select_table())[gz][:, :, None]
    select = one_hot(
        (lane == lanes[0]) | (lane == lanes[1]) | (lane == lanes[2])
        | ((lane - 64 == lanes[2]) & (lane >= 192))
    )
    row_order = one_hot(iota((256, 256), 1) == jnp.asarray(row_table())[:, None])

    noise_part, faces = pl.pallas_call(
        noise_kernel,
        out_shape=(
            jax.ShapeDtypeStruct((N_GZ * 64, N_GX * N_GY * PART), BF),
            jax.ShapeDtypeStruct((BX, ENS, 24, 128), BF),
        ),
        in_specs=[smem, vmem, vmem] + [anywhere] * 20,
        out_specs=(vmem, vmem),
        scratch_shapes=[
            pltpu.VMEM((N_GZ, 64, CELLS), BF),
            pltpu.VMEM((N_GX * N_GY * 2, HALF, CELLS), BF),
            pltpu.VMEM((256, 256), F32),
            pltpu.VMEM((256, 256), F32),
            pltpu.SemaphoreType.DMA,
            pltpu.SemaphoreType.DMA((N_GX,)),
        ],
        name="noise_part",
    )(place, select, row_order, *row_pieces, *pieces)

    copies = jnp.broadcast_to(
        faces[None, :, :, None], (N_GX // 2, BX, ENS, N_GZ, 24, 128)
    )
    received = lax.all_to_all(
        copies.reshape(128, 24, 128), ("gx", "gy", "gz"), 0, 0, tiled=True
    )
    other_half = plane_shift(received, 0, 0, 1)

    noise_rows = noise_part.reshape(N_GZ, 64, N_GX * N_GY * PART)
    home = []
    for d in range(N_GZ):
        part = lax.dynamic_index_in_dim(noise_rows, (gz + d) % N_GZ, 0, keepdims=False)
        home.append(part if d == 0 else line_shift(part, d))

    to_state = one_hot(iota((CELLS, STATE), 0) == jnp.asarray(STATE_CELLS)[None, :])
    step = to_bf16_dot(kriging_state, to_state)

    chosen = pl.pallas_call(
        sweep_kernel,
        out_shape=jax.ShapeDtypeStruct((64, STATE), BF),
        in_specs=[smem, vmem, vmem, vmem],
        out_specs=vmem,
        scratch_shapes=[
            pltpu.VMEM((PLANES, SPAN_X * SLOTS * 8, 128), F32),
            pltpu.VMEM((PLANES, LEVELS * 64, 128), F32),
            pltpu.VMEM((PLANES, 64, 128), F32),
            pltpu.VMEM((PLANES, 64, 128), F32),
        ],
        name="sweep",
    )(sweep_place, received, other_half, step)

    upstream = lax.all_to_all(
        chosen.reshape(N_GY, TILES, STATE), "gy", 0, 0, tiled=True
    ).reshape(ENS * TILES, STATE)

    spread = one_hot(iota((N_GZ, 128, 512), 2) == jnp.asarray(spread_table())[:, :, None])
    natural = pl.pallas_call(
        natural_kernel,
        out_shape=jax.ShapeDtypeStruct((TILES * ENS, CELLS), BF),
        in_specs=[smem] + [vmem] * 5,
        out_specs=vmem,
        name="natural",
    )(sweep_place, *home, spread)

    target, source = iota((64, 64), 0), iota((64, 64), 1)
    swap_rows = one_hot(source == (target % 8) * 8 + target // 8)
    width = 1024
    out = pl.pallas_call(
        final_kernel,
        grid=(CELLS // width,),
        out_shape=jax.ShapeDtypeStruct((TILES * ENS, CELLS), F32),
        in_specs=[
            pl.BlockSpec((64, STATE), lambda g: (0, 0)),
            pl.BlockSpec((64, 64), lambda g: (0, 0)),
            pl.BlockSpec((STATE, width), lambda g: (0, g)),
            pl.BlockSpec((64, width), lambda g: (0, g)),
        ],
        out_specs=pl.BlockSpec((64, width), lambda g: (0, g)),
        name="evolve",
    )(upstream, swap_rows, kriging_state, natural)
    return out.reshape(BX, BY, BZ, ENS, CELLS)


def solution(mesh):
    placed = (
        P(None, ("gx", "gy")),
        P(),
        P("gx", "gy", "gz", None, None, None),
        P("gx", "gy", "gz", None),
    )
    return jax.shard_map(
        local,
        mesh=mesh,
        in_specs=placed,
        out_specs=P("gx", "gy", "gz", None, None),
        check_vma=False,
    )
```

```python
import functools

import jax
import jax.numpy as jnp
import numpy as np
from jax import lax
from jax.experimental import pallas as pl
from jax.experimental.pallas import tpu as pltpu
from jax.sharding import PartitionSpec as P

TILE = 16
CELLS = 4096
FACE = 256
BX = 2
BY = 2
BZ = 2
TILES = 8
ENS = 8
N_GX = 4
N_GY = 8
N_GZ = 4
SPAN_X = N_GX * BX
SPAN_Y = N_GY * BY
SPAN_Z = N_GZ * BZ
LEVELS = SPAN_X + SPAN_Y + SPAN_Z - 2
COLS_DEV = CELLS // (N_GX * N_GY)
PART = COLS_DEV // N_GZ
HALF = PART // 2
STATE = 3 * FACE
PLANES = STATE // 128
SLOTS = SPAN_Y + SPAN_X - 1 + SPAN_Z - 1 + 14

BF = jnp.bfloat16
F32 = jnp.float32


def part_column(q, part):
    rows = q // 4
    return rows * TILE + 4 * ((part - rows) % 4) + q % 4


def state_order():
    rows = np.zeros(STATE, np.int32)
    cells = np.zeros(STATE, np.int32)
    for f in range(STATE):
        plane, lane = divmod(f, 128)
        if plane < 4:
            s, slot = plane, lane % 64
            if lane < 64:
                i, q = 30 + slot // 32, slot % 32
                v, w = 8 * (i % 2) + q // 4, 4 * ((s - q // 4) % 4) + q % 4
                rows[f], cells[f] = v * 16 + w, (15 * 16 + v) * 16 + w
            else:
                u, w = slot // 4, 4 * ((s - 15) % 4) + slot % 4
                rows[f], cells[f] = FACE + u * 16 + w, (u * 16 + 15) * 16 + w
        else:
            s, slot = 2 * (plane - 4) + lane // 64, lane % 64
            i, e = slot // 2, slot % 2
            u, v = i // 2, 8 * (i % 2) + 4 * e + (s + 1) % 4
            rows[f], cells[f] = 2 * FACE + u * 16 + v, (u * 16 + v) * 16 + 15
    return rows, cells


STATE_ROWS, STATE_CELLS = state_order()


def one_hot(condition):
    return condition.astype(BF)


def iota(shape, axis):
    return lax.broadcasted_iota(jnp.int32, shape, axis)


def to_bf16_dot(left, right):
    return jnp.dot(left, right, preferred_element_type=F32).astype(BF)


def plane_shift(value, dx, dz, dc, sends=None):
    pairs = []
    for gx in range(N_GX):
        for gy in range(N_GY):
            x, z, core = gy // 2, (gy % 2) * 2 + gx // 2, gx % 2
            if sends is not None and not sends(x, z, core):
                continue
            x, z, core = (x + dx) % 4, (z + dz) % 4, core ^ dc
            pairs.append((gx * N_GY + gy, ((z % 2) * 2 + core) * N_GY + x * 2 + z // 2))
    return lax.ppermute(value, ("gx", "gy"), pairs)


def line_shift(value, steps):
    return lax.ppermute(value, "gz", [(s, (s + steps) % N_GZ) for s in range(N_GZ)])


def noise_kernel(place, *refs):
    row_refs = refs[:4]
    piece_refs = refs[4:20]
    noise_out = refs[20]
    rows, factors, acc, sem_rows, sem_factor = refs[21:]
    x, z, core, gz = place[0], place[1], place[2], place[3]
    copies = []
    for back in range(N_GZ):
        copies.append(
            pltpu.make_async_copy(
                row_refs[back], rows.at[lax.rem(gz - back + N_GZ, N_GZ)], sem_rows
            )
        )
    for half in range(2):
        for outer in range(4):
            for swap in range(2):
                ref = piece_refs[half * 8 + outer * 2 + swap]
                for inner in range(4):
                    dx, dz = (inner, outer) if half == 0 else (outer, inner)
                    sx = lax.rem(x - dx + 4, 4)
                    sz = lax.rem(z - dz + 4, 4)
                    sc = core if swap == 0 else 1 - core
                    sgx = lax.rem(sz, 2) * 2 + sc
                    sgy = sx * 2 + sz // 2
                    copies.append(
                        pltpu.make_async_copy(
                            ref.at[pl.ds(inner * HALF, HALF)],
                            factors.at[(sgx * N_GY + sgy) * 2 + half],
                            sem_factor.at[sgx],
                        )
                    )
    for copy in copies:
        copy.start()
    pltpu.make_async_copy(rows, rows, sem_rows).wait()
    per = N_GY * 2
    wide = N_GY * PART
    for g in range(N_GX):
        block = factors.at[pl.ds(g * per, per)]
        pltpu.make_async_copy(block, block, sem_factor.at[g]).wait()
        acc[...] = jnp.zeros_like(acc)

        @pl.loop(0, g + 1)
        def _(chunk):
            span = pl.ds(pl.multiple_of(chunk * 1024, 1024), 1024)
            acc[...] += lax.dot_general(
                rows[:, :, span].reshape(N_GZ * 64, 1024),
                factors[g * per : (g + 1) * per, :, span].reshape(wide, 1024),
                (((1,), (1,)), ((), ())),
                preferred_element_type=F32,
            )

        noise_out[:, g * wide : (g + 1) * wide] = acc[...].astype(BF)


def face_kernel(place, select, row_order, *refs):
    row_refs = refs[:4]
    blocks_own, blocks_other = refs[4:6]
    line_refs, lines_other = refs[6:10], refs[10]
    face_out = refs[11]
    rows, factors, sem_rows, sem_factor = refs[12:]
    core = place[2]
    for back in range(N_GZ):
        pltpu.make_async_copy(row_refs[back], rows.at[back], sem_rows).start()
    for outer in range(4):
        pltpu.make_async_copy(
            line_refs[outer], factors.at[pl.ds(64 + outer * 32, 32)], sem_factor
        ).start()
    pltpu.make_async_copy(lines_other, factors.at[pl.ds(192, 128)], sem_factor).start()

    @pl.when(core == 1)
    def _():
        pltpu.make_async_copy(blocks_own, factors.at[pl.ds(0, 64)], sem_factor).start()

    @pl.when(core == 0)
    def _():
        pltpu.make_async_copy(blocks_other, factors.at[pl.ds(0, 64)], sem_factor).start()

    pltpu.make_async_copy(rows, rows, sem_rows).wait()
    pltpu.make_async_copy(factors, factors, sem_factor).wait()
    product = lax.dot_general(
        rows[...].reshape(N_GZ * 64, CELLS),
        factors[...],
        (((1,), (1,)), ((), ())),
        preferred_element_type=F32,
    ).astype(BF)
    sums = jnp.dot(product, select[...], preferred_element_type=F32).astype(BF)
    faces = jnp.dot(row_order[...], sums, preferred_element_type=F32)
    low = iota((8, 128), 1) < 64
    for r in range(ENS):
        for a in range(BX):
            base = r * 32 + a * 16
            face_out[a, r, 0:16, :] = faces[base : base + 16, :128].astype(BF)
            first = faces[base : base + 8, 128:]
            second = faces[base + 8 : base + 16, 128:]
            face_out[a, r, 16:24, :] = jnp.where(low, first, second).astype(BF)


def sweep_kernel(place, own_half, other_half, step, out, noise, history, state, picked):
    gx, core, gz = place[0], place[2], place[3]
    low8 = iota((8, 128), 1) < 64

    noise[...] = jnp.zeros_like(noise)

    @pl.loop(0, N_GX * N_GY)
    def _(block):
        bx = block // N_GY
        by = lax.rem(block, N_GY)
        for a, half in ((core, own_half), (1 - core, other_half)):
            planes = [half[block * N_GZ + s, 0:16, :].astype(F32) for s in range(N_GZ)]
            zs = [half[block * N_GZ + s, 16:24, :].astype(F32) for s in range(N_GZ)]
            for b in range(BY):
                start = ((bx * BX + a) * SLOTS + by * BY + b + 14) * 8
                start = pl.multiple_of(start, 8)
                for p in range(4):
                    noise[p, pl.ds(start, 8), :] = planes[p][b * 8 : (b + 1) * 8]
                for pair in range(2):
                    first, second = zs[2 * pair], zs[2 * pair + 1]
                    if b == 0:
                        second = pltpu.roll(second, 64, 1)
                    else:
                        first = pltpu.roll(first, 64, 1)
                    noise[4 + pair, pl.ds(start, 8), :] = jnp.where(low8, first, second)

    state[...] = jnp.zeros_like(state)
    low = iota((64, 128), 1) < 64
    has_below = (iota((64, 128), 0) % 8) != 7

    @pl.loop(0, LEVELS)
    def _(level):
        upstream = []
        for p in range(PLANES):
            here = state[p]
            if p < 4:
                west = jnp.concatenate([jnp.zeros((8, 128), F32), here[:56]], 0)
                value = jnp.where(low, west, here)
            else:
                value = jnp.where(has_below, pltpu.roll(here, 63, 0), 0.0)
            history[p, pl.ds(pl.multiple_of(level * 64, 64), 64), :] = value
            upstream.append(value.astype(BF))
        result = jnp.dot(jnp.concatenate(upstream, 1), step[...], preferred_element_type=F32)
        for p in range(PLANES):
            rows = []
            for i in range(SPAN_X):
                start = (i * SLOTS + level - i + 7) * 8
                rows.append(noise[p, pl.ds(start, 8, stride=9), :])
            state[p] = result[:, p * 128 : (p + 1) * 128] + jnp.concatenate(rows, 0)

    for a in range(BX):
        for b in range(BY):
            for c in range(BZ):
                i = gx * BX + a
                k = gz * BZ + c
                start = (i + k + b) * 64 + i * 8 + 7 - k
                for p in range(PLANES):
                    picked[p, pl.ds((a * BY + b) * BZ + c, 8, stride=8), :] = history[
                        p, pl.ds(start, 8, stride=128), :
                    ]
    for p in range(PLANES):
        out[:, p * 128 : (p + 1) * 128] = picked[p].astype(BF)


def natural_kernel(place, first, second, third, fourth, spread, out):
    gz = place[3]
    total = jnp.zeros((512, 512), F32)
    for back, part in enumerate((first, second, third, fourth)):
        source = lax.rem(gz - back + N_GZ, N_GZ)
        stacked = jnp.concatenate([part[:, g * 128 : (g + 1) * 128] for g in range(8)], 0)
        total += jnp.dot(stacked, spread[source], preferred_element_type=F32)
    for g in range(8):
        out[:, g * 512 : (g + 1) * 512] = total[g * 64 : (g + 1) * 64].astype(BF)


def final_kernel(faces, swap_rows, reorder, kriging, noise, out):
    upstream = jnp.dot(swap_rows[...], faces[...], preferred_element_type=F32).astype(BF)
    upstream = jnp.dot(upstream, reorder[...], preferred_element_type=F32).astype(BF)
    product = jnp.dot(upstream, kriging[...], preferred_element_type=F32)
    out[...] = product + noise[...].astype(F32)


def select_table():
    table = np.full((N_GX, N_GY, N_GZ, 3, 320), -1, np.int32)
    for gx in range(N_GX):
        for gy in range(N_GY):
            x, z, core = gy // 2, (gy % 2) * 2 + gx // 2, gx % 2
            sources = (z, z ^ 2) if z % 2 else ((z - 1) % 4, (z + 1) % 4)
            for s in range(N_GZ):
                for block, source in enumerate(sources):
                    i = 30 + source // 2
                    for q in range(32):
                        table[gx, gy, s, 0, block * 32 + q] = (i - 30) * 32 + q
                for swap in range(2):
                    for dz in range(4):
                        for dx in range(4):
                            sx, sz, sc = (x - dx) % 4, (z - dz) % 4, core ^ swap
                            i = ((sz % 2) * 2 + sc) * N_GY + sx * 2 + sz // 2
                            base = 64 + swap * 128 + dz * 32 + dx * 8
                            for e in range(2):
                                table[gx, gy, s, 2, base + e] = 128 + i * 2 + e
                            if i % 2 == 1:
                                for m in range(4):
                                    table[gx, gy, s, 1, base + 2 + m] = 64 + (i // 2) * 4 + m
    return table.reshape(-1, 3, 320)


def ahead_table():
    table = np.full((N_GZ, 8), -1, np.int32)
    for s in range(N_GZ):
        for e in range(2):
            table[s, e] = part_column(4 * ((s + 1) % 4 + 4 * e) + 3, s)
        for m in range(4):
            table[s, 2 + m] = part_column(28 + m, s)
    return table


def row_table():
    order = np.zeros((N_GZ, 256), np.int32)
    for gz in range(N_GZ):
        for target in range(256):
            k = 7 - target % 8
            tile = (target // 8 % 4) * 2 + k % 2
            order[gz, target] = ((gz - k // 2) % N_GZ) * 64 + tile * 8 + target // 32
    return order


def spread_table():
    table = np.zeros((N_GZ, 128), np.int32)
    for s in range(N_GZ):
        for n in range(128):
            table[s, n] = (n // PART) * COLS_DEV + part_column(n % PART, s)
    return table


def own_table():
    part = np.array([[part_column(q, s) for q in range(PART)] for s in range(N_GZ)], np.int32)
    return np.concatenate([part, ahead_table()], 1)


def local(factor, kriging, normals, visit_order):
    gx = lax.axis_index("gx")
    gy = lax.axis_index("gy")
    gz = lax.axis_index("gz")
    place = jnp.stack([gy // 2, (gy % 2) * 2 + gx // 2, gx % 2, gz]).astype(jnp.int32)
    sweep_place = jnp.stack([gx, gy, gx % 2, gz]).astype(jnp.int32)
    vmem = pl.BlockSpec(memory_space=pltpu.VMEM)
    smem = pl.BlockSpec(memory_space=pltpu.SMEM)
    anywhere = pl.BlockSpec(memory_space=pl.ANY)

    x, z, core = gy // 2, (gy % 2) * 2 + gx // 2, gx % 2
    own_columns = jnp.asarray(own_table())[gz]
    own = one_hot(iota((PART + 8, COLS_DEV), 1) == own_columns[:, None])
    shard = lax.dot_general(
        own, factor, (((1,), (1,)), ((), ())), preferred_element_type=F32
    ).astype(BF)
    shard, ahead = shard[:PART], shard[PART:]

    line = jnp.concatenate([ahead] + [plane_shift(ahead, d, 0, 0) for d in (1, 2, 3)], 0)
    holder = (x == 3) & (z % 2 == 1) & (core == 1)
    block = jnp.where(holder, shard, jnp.zeros_like(shard))
    for d in (1, 2, 3):
        block += plane_shift(shard, d, 0, 0, lambda x, z, c: x == 3 and z % 2 == 1 and c == 1)

    drawn = normals.reshape(TILES, ENS, CELLS)
    ordered = drawn.at[visit_order.reshape(TILES)].get(mode="promise_in_bounds")
    ordered = ordered.reshape(TILES * ENS, CELLS)
    row_pieces = [ordered] + [line_shift(ordered, s) for s in (1, 2, 3)]

    lines = [line] + [plane_shift(line, 0, d, 0) for d in (1, 2, 3)]
    moved = [plane_shift(block, 0, d, 0, lambda x, z, c: z % 2 == 1 and c == 1) for d in (1, 2, 3)]
    blocks = jnp.concatenate([block + moved[0], moved[1] + moved[2]], 0)
    lines_other = plane_shift(jnp.concatenate(lines, 0), 0, 0, 1)
    blocks_other = plane_shift(blocks, 0, 0, 1, lambda x, z, c: c == 1)

    first, second = shard[:HALF], shard[HALF:]
    along_x = jnp.concatenate([first] + [plane_shift(first, d, 0, 0) for d in (1, 2, 3)], 0)
    along_z = jnp.concatenate([second] + [plane_shift(second, 0, d, 0) for d in (1, 2, 3)], 0)
    pieces = []
    for piece in [along_x] + [plane_shift(along_x, 0, d, 0) for d in (1, 2, 3)]:
        pieces += [piece, plane_shift(piece, 0, 0, 1)]
    for piece in [along_z] + [plane_shift(along_z, d, 0, 0) for d in (1, 2, 3)]:
        pieces += [piece, plane_shift(piece, 0, 0, 1)]

    lane = iota((320, 256), 1)
    device = (gx * N_GY + gy) * N_GZ + gz
    lanes = jnp.asarray(select_table())[device][:, :, None]
    select = one_hot(
        (lane == lanes[0]) | (lane == lanes[1]) | (lane == lanes[2])
        | ((lane - 64 == lanes[2]) & (lane >= 192))
    )
    row_order = one_hot(iota((256, 256), 1) == jnp.asarray(row_table())[gz][:, None])

    faces = pl.pallas_call(
        face_kernel,
        out_shape=jax.ShapeDtypeStruct((BX, ENS, 24, 128), BF),
        in_specs=[smem, vmem, vmem] + [anywhere] * 11,
        out_specs=vmem,
        scratch_shapes=[
            pltpu.VMEM((N_GZ, 64, CELLS), BF),
            pltpu.VMEM((320, CELLS), BF),
            pltpu.SemaphoreType.DMA,
            pltpu.SemaphoreType.DMA,
        ],
        name="face_part",
    )(place, select, row_order, *row_pieces, blocks, blocks_other, *lines, lines_other)

    place, faces = lax.optimization_barrier((place, faces))
    noise_part = pl.pallas_call(
        noise_kernel,
        out_shape=jax.ShapeDtypeStruct((N_GZ * 64, N_GX * N_GY * PART), BF),
        in_specs=[smem] + [anywhere] * 20,
        out_specs=vmem,
        scratch_shapes=[
            pltpu.VMEM((N_GZ, 64, CELLS), BF),
            pltpu.VMEM((N_GX * N_GY * 2, HALF, CELLS), BF),
            pltpu.VMEM((256, 256), F32),
            pltpu.SemaphoreType.DMA,
            pltpu.SemaphoreType.DMA((N_GX,)),
        ],
        name="noise_part",
    )(place, *row_pieces, *pieces)

    copies = jnp.broadcast_to(
        faces[None, :, :, None], (N_GX // 2, BX, ENS, N_GZ, 24, 128)
    )
    received = lax.all_to_all(
        copies.reshape(128, 24, 128), ("gx", "gy", "gz"), 0, 0, tiled=True
    )
    noise_rows = noise_part.reshape(N_GZ, 64, N_GX * N_GY * PART)
    home = []
    for d in range(N_GZ):
        part = lax.dynamic_index_in_dim(noise_rows, (gz + d) % N_GZ, 0, keepdims=False)
        home.append(part if d == 0 else line_shift(part, d))

    other_half = plane_shift(received, 0, 0, 1)

    to_state = one_hot(iota((CELLS, STATE), 0) == jnp.asarray(STATE_CELLS)[None, :])
    reorder = one_hot(jnp.asarray(STATE_ROWS)[:, None] == iota((STATE, STATE), 1))
    step = to_bf16_dot(reorder, to_bf16_dot(kriging, to_state))

    chosen = pl.pallas_call(
        sweep_kernel,
        out_shape=jax.ShapeDtypeStruct((64, STATE), BF),
        in_specs=[smem, vmem, vmem, vmem],
        out_specs=vmem,
        scratch_shapes=[
            pltpu.VMEM((PLANES, SPAN_X * SLOTS * 8, 128), F32),
            pltpu.VMEM((PLANES, LEVELS * 64, 128), F32),
            pltpu.VMEM((PLANES, 64, 128), F32),
            pltpu.VMEM((PLANES, 64, 128), F32),
        ],
        name="sweep",
    )(sweep_place, received, other_half, step)

    upstream = lax.all_to_all(
        chosen.reshape(N_GY, TILES, STATE), "gy", 0, 0, tiled=True
    ).reshape(ENS * TILES, STATE)

    spread = one_hot(iota((N_GZ, 128, 512), 2) == jnp.asarray(spread_table())[:, :, None])
    natural = pl.pallas_call(
        natural_kernel,
        out_shape=jax.ShapeDtypeStruct((TILES * ENS, CELLS), BF),
        in_specs=[smem] + [vmem] * 5,
        out_specs=vmem,
        name="natural",
    )(sweep_place, *home, spread)

    target, source = iota((64, 64), 0), iota((64, 64), 1)
    swap_rows = one_hot(source == (target % 8) * 8 + target // 8)
    width = 1024
    out = pl.pallas_call(
        final_kernel,
        grid=(CELLS // width,),
        out_shape=jax.ShapeDtypeStruct((TILES * ENS, CELLS), F32),
        in_specs=[
            pl.BlockSpec((64, STATE), lambda g: (0, 0)),
            pl.BlockSpec((64, 64), lambda g: (0, 0)),
            pl.BlockSpec((STATE, STATE), lambda g: (0, 0)),
            pl.BlockSpec((STATE, width), lambda g: (0, g)),
            pl.BlockSpec((64, width), lambda g: (0, g)),
        ],
        out_specs=pl.BlockSpec((64, width), lambda g: (0, g)),
        name="evolve",
    )(upstream, swap_rows, reorder, kriging, natural)
    return out.reshape(BX, BY, BZ, ENS, CELLS)


def solution(mesh):
    placed = (
        P(None, ("gx", "gy")),
        P(),
        P("gx", "gy", "gz", None, None, None),
        P("gx", "gy", "gz", None),
    )
    return jax.shard_map(
        local,
        mesh=mesh,
        in_specs=placed,
        out_specs=P("gx", "gy", "gz", None, None),
        check_vma=False,
    )
```

```python
import functools

import jax
import jax.numpy as jnp
import numpy as np
from jax import lax
from jax.experimental import pallas as pl
from jax.experimental.pallas import tpu as pltpu
from jax.sharding import PartitionSpec as P

TILE = 16
CELLS = 4096
FACE = 256
BX = 2
BY = 2
BZ = 2
TILES = 8
ENS = 8
N_GX = 4
N_GY = 8
N_GZ = 4
SPAN_X = N_GX * BX
SPAN_Y = N_GY * BY
SPAN_Z = N_GZ * BZ
LEVELS = SPAN_X + SPAN_Y + SPAN_Z - 2
COLS_DEV = CELLS // (N_GX * N_GY)
PART = COLS_DEV // N_GZ
HALF = PART // 2
STATE = 3 * FACE
PLANES = STATE // 128
SLOTS = SPAN_Y + SPAN_X - 1 + SPAN_Z - 1 + 14

BF = jnp.bfloat16
F32 = jnp.float32


def part_column(q, part):
    rows = q // 4
    return rows * TILE + 4 * ((part - rows) % 4) + q % 4


def state_order():
    rows = np.zeros(STATE, np.int32)
    cells = np.zeros(STATE, np.int32)
    for f in range(STATE):
        plane, lane = divmod(f, 128)
        if plane < 4:
            s, slot = plane, lane % 64
            if lane < 64:
                i, q = 30 + slot // 32, slot % 32
                v, w = 8 * (i % 2) + q // 4, 4 * ((s - q // 4) % 4) + q % 4
                rows[f], cells[f] = v * 16 + w, (15 * 16 + v) * 16 + w
            else:
                u, w = slot // 4, 4 * ((s - 15) % 4) + slot % 4
                rows[f], cells[f] = FACE + u * 16 + w, (u * 16 + 15) * 16 + w
        else:
            s, slot = 2 * (plane - 4) + lane // 64, lane % 64
            i, e = slot // 2, slot % 2
            u, v = i // 2, 8 * (i % 2) + 4 * e + (s + 1) % 4
            rows[f], cells[f] = 2 * FACE + u * 16 + v, (u * 16 + v) * 16 + 15
    return rows, cells


STATE_ROWS, STATE_CELLS = state_order()


def one_hot(condition):
    return condition.astype(BF)


def iota(shape, axis):
    return lax.broadcasted_iota(jnp.int32, shape, axis)


def to_bf16_dot(left, right):
    return jnp.dot(left, right, preferred_element_type=F32).astype(BF)


def plane_shift(value, dx, dz, dc):
    pairs = []
    for gx in range(N_GX):
        for gy in range(N_GY):
            x, z, core = gy // 2, (gy % 2) * 2 + gx // 2, gx % 2
            x, z, core = (x + dx) % 4, (z + dz) % 4, core ^ dc
            pairs.append((gx * N_GY + gy, ((z % 2) * 2 + core) * N_GY + x * 2 + z // 2))
    return lax.ppermute(value, ("gx", "gy"), pairs)


def line_shift(value, steps):
    return lax.ppermute(value, "gz", [(s, (s + steps) % N_GZ) for s in range(N_GZ)])


def noise_kernel(place, select, row_order, *refs):
    row_refs = refs[:4]
    piece_refs = refs[4:20]
    noise_out, face_out = refs[20:22]
    rows, factors, acc, sums, sem_rows, sem_factor = refs[22:]
    x, z, core, gz = place[0], place[1], place[2], place[3]
    for back in range(N_GZ):
        pltpu.make_async_copy(row_refs[back], rows.at[back], sem_rows).start()
    per = N_GY * 2
    wide = N_GY * PART
    groups = [(parity, swap) for parity in range(2) for swap in range(2)]
    for number, (parity, swap) in enumerate(groups):
        for half in range(2):
            for outer in range(4):
                for inner in range(4):
                    dx, dz = (inner, outer) if half == 0 else (outer, inner)
                    if dz % 2 != parity:
                        continue
                    sx = lax.rem(x - dx + 4, 4)
                    sz = lax.rem(z - dz + 4, 4)
                    sgx = lax.rem(z + parity, 2) * 2 + (core if swap == 0 else 1 - core)
                    sgy = sx * 2 + sz // 2
                    pltpu.make_async_copy(
                        piece_refs[half * 8 + outer * 2 + swap].at[pl.ds(inner * HALF, HALF)],
                        factors.at[(sgx * N_GY + sgy) * 2 + half],
                        sem_factor.at[number],
                    ).start()
    pltpu.make_async_copy(rows, rows, sem_rows).wait()
    sums[...] = jnp.zeros_like(sums)
    for number, (parity, swap) in enumerate(groups):
        g = lax.rem(z + parity, 2) * 2 + (core if swap == 0 else 1 - core)
        block = factors.at[pl.ds(g * per, per)]
        pltpu.make_async_copy(block, block, sem_factor.at[number]).wait()
        acc[...] = jnp.zeros_like(acc)

        @pl.loop(0, g + 1)
        def _(chunk):
            span = pl.ds(pl.multiple_of(chunk * 1024, 1024), 1024)
            acc[...] += lax.dot_general(
                rows[:, :, span].reshape(N_GZ * 64, 1024),
                factors[pl.ds(g * per, per), :, span].reshape(wide, 1024),
                (((1,), (1,)), ((), ())),
                preferred_element_type=F32,
            )

        rounded = acc[...].astype(BF)
        place_g = pl.multiple_of(g * wide, wide)
        noise_out[:, pl.ds(place_g, wide)] = rounded
        sums[...] += jnp.dot(
            rounded, select[pl.ds(place_g, wide), :], preferred_element_type=F32
        )
    faces = jnp.dot(row_order[...], sums[...].astype(BF), preferred_element_type=F32)
    low = iota((8, 128), 1) < 64
    for r in range(ENS):
        for a in range(BX):
            base = r * 32 + a * 16
            face_out[a, r, 0:16, :] = faces[base : base + 16, :128].astype(BF)
            first = faces[base : base + 8, 128:]
            second = faces[base + 8 : base + 16, 128:]
            face_out[a, r, 16:24, :] = jnp.where(low, first, second).astype(BF)


def sweep_kernel(place, own_half, other_half, step, out, noise, history, state, picked):
    gx, core, gz = place[0], place[2], place[3]
    low8 = iota((8, 128), 1) < 64

    noise[...] = jnp.zeros_like(noise)

    @pl.loop(0, N_GX * N_GY)
    def _(block):
        bx = block // N_GY
        by = lax.rem(block, N_GY)
        for a, half in ((core, own_half), (1 - core, other_half)):
            planes = [half[block * N_GZ + s, 0:16, :].astype(F32) for s in range(N_GZ)]
            zs = [half[block * N_GZ + s, 16:24, :].astype(F32) for s in range(N_GZ)]
            for b in range(BY):
                start = ((bx * BX + a) * SLOTS + by * BY + b + 14) * 8
                start = pl.multiple_of(start, 8)
                for p in range(4):
                    noise[p, pl.ds(start, 8), :] = planes[p][b * 8 : (b + 1) * 8]
                for pair in range(2):
                    first, second = zs[2 * pair], zs[2 * pair + 1]
                    if b == 0:
                        second = pltpu.roll(second, 64, 1)
                    else:
                        first = pltpu.roll(first, 64, 1)
                    noise[4 + pair, pl.ds(start, 8), :] = jnp.where(low8, first, second)

    state[...] = jnp.zeros_like(state)
    low = iota((64, 128), 1) < 64
    has_below = (iota((64, 128), 0) % 8) != 7

    @pl.loop(0, LEVELS)
    def _(level):
        upstream = []
        for p in range(PLANES):
            here = state[p]
            if p < 4:
                west = jnp.concatenate([jnp.zeros((8, 128), F32), here[:56]], 0)
                value = jnp.where(low, west, here)
            else:
                value = jnp.where(has_below, pltpu.roll(here, 63, 0), 0.0)
            history[p, pl.ds(pl.multiple_of(level * 64, 64), 64), :] = value
            upstream.append(value.astype(BF))
        result = jnp.dot(jnp.concatenate(upstream, 1), step[...], preferred_element_type=F32)
        for p in range(PLANES):
            rows = []
            for i in range(SPAN_X):
                start = (i * SLOTS + level - i + 7) * 8
                rows.append(noise[p, pl.ds(start, 8, stride=9), :])
            state[p] = result[:, p * 128 : (p + 1) * 128] + jnp.concatenate(rows, 0)

    for a in range(BX):
        for b in range(BY):
            for c in range(BZ):
                i = gx * BX + a
                k = gz * BZ + c
                start = (i + k + b) * 64 + i * 8 + 7 - k
                for p in range(PLANES):
                    picked[p, pl.ds((a * BY + b) * BZ + c, 8, stride=8), :] = history[
                        p, pl.ds(start, 8, stride=128), :
                    ]
    for p in range(PLANES):
        out[:, p * 128 : (p + 1) * 128] = picked[p].astype(BF)


def natural_kernel(place, first, second, third, fourth, spread, out):
    gz = place[3]
    total = jnp.zeros((512, 512), F32)
    for back, part in enumerate((first, second, third, fourth)):
        source = lax.rem(gz + back, N_GZ)
        stacked = jnp.concatenate([part[:, g * 128 : (g + 1) * 128] for g in range(8)], 0)
        total += jnp.dot(stacked, spread[source], preferred_element_type=F32)
    for g in range(8):
        out[:, g * 512 : (g + 1) * 512] = total[g * 64 : (g + 1) * 64].astype(BF)


def final_kernel(faces, swap_rows, reorder, kriging, noise, out):
    upstream = jnp.dot(swap_rows[...], faces[...], preferred_element_type=F32).astype(BF)
    upstream = jnp.dot(upstream, reorder[...], preferred_element_type=F32).astype(BF)
    product = jnp.dot(upstream, kriging[...], preferred_element_type=F32)
    out[...] = product + noise[...].astype(F32)


def select_table():
    table = np.full((N_GZ, 3, N_GX * N_GY * PART), -1, np.int32)
    for s in range(N_GZ):
        for n in range(N_GX * N_GY * PART):
            i, q = n // PART, n % PART
            if i >= 30:
                table[s, 0, n] = (i - 30) * 32 + q
            if i % 2 == 1 and q >= 28:
                table[s, 1, n] = 64 + (i // 2) * 4 + q % 4
            if q % 4 == 3 and (s - q // 4) % 4 == 3:
                table[s, 2, n] = 128 + i * 2 + q // 16
    return table


def row_table():
    order = np.zeros((N_GZ, 256), np.int32)
    for gz in range(N_GZ):
        for target in range(256):
            k = 7 - target % 8
            tile = (target // 8 % 4) * 2 + k % 2
            order[gz, target] = ((gz - k // 2) % N_GZ) * 64 + tile * 8 + target // 32
    return order


def spread_table():
    table = np.zeros((N_GZ, 128), np.int32)
    for s in range(N_GZ):
        for n in range(128):
            table[s, n] = (n // PART) * COLS_DEV + part_column(n % PART, s)
    return table


def own_table():
    return np.array([[part_column(q, s) for q in range(PART)] for s in range(N_GZ)], np.int32)


def local(factor, kriging, normals, visit_order):
    gx = lax.axis_index("gx")
    gy = lax.axis_index("gy")
    gz = lax.axis_index("gz")
    place = jnp.stack([gy // 2, (gy % 2) * 2 + gx // 2, gx % 2, gz]).astype(jnp.int32)
    sweep_place = jnp.stack([gx, gy, gx % 2, gz]).astype(jnp.int32)
    vmem = pl.BlockSpec(memory_space=pltpu.VMEM)
    smem = pl.BlockSpec(memory_space=pltpu.SMEM)
    anywhere = pl.BlockSpec(memory_space=pl.ANY)

    own_columns = jnp.asarray(own_table())[gz]
    own = one_hot(iota((PART, COLS_DEV), 1) == own_columns[:, None])
    shard = lax.dot_general(
        own, factor, (((1,), (1,)), ((), ())), preferred_element_type=F32
    ).astype(BF)
    first, second = shard[:HALF], shard[HALF:]
    along_x = jnp.concatenate([first] + [plane_shift(first, d, 0, 0) for d in (1, 2, 3)], 0)
    along_z = jnp.concatenate([second] + [plane_shift(second, 0, d, 0) for d in (1, 2, 3)], 0)

    drawn = normals.reshape(TILES, ENS, CELLS)
    ordered = drawn.at[visit_order.reshape(TILES)].get(mode="promise_in_bounds")
    ordered = ordered.reshape(TILES * ENS, CELLS)
    row_pieces = [ordered] + [line_shift(ordered, s) for s in (1, 2, 3)]

    lane = iota((N_GX * N_GY * PART, 256), 1)
    lanes = jnp.asarray(select_table())[gz][:, :, None]
    select = one_hot(
        (lane == lanes[0]) | (lane == lanes[1]) | (lane == lanes[2])
        | ((lane - 64 == lanes[2]) & (lane >= 192))
    )
    row_order = one_hot(iota((256, 256), 1) == jnp.asarray(row_table())[gz][:, None])
    spread = one_hot(iota((N_GZ, 128, 512), 2) == jnp.asarray(spread_table())[:, :, None])
    reorder = one_hot(jnp.asarray(STATE_ROWS)[:, None] == iota((STATE, STATE), 1))
    swap_rows = one_hot(
        iota((64, 64), 1) == jnp.asarray([(r % 8) * 8 + r // 8 for r in range(64)])[:, None]
    )

    held_x = [along_x] + [plane_shift(along_x, 0, d, 0) for d in (1, 2, 3)]
    held_z = [along_z] + [plane_shift(along_z, d, 0, 0) for d in (1, 2, 3)]
    held_x[1], select, row_order, spread, reorder, swap_rows, place, sweep_place = (
        lax.optimization_barrier(
            (held_x[1], select, row_order, spread, reorder, swap_rows, place, sweep_place)
        )
    )
    pieces = []
    for piece in held_x + held_z:
        pieces += [piece, plane_shift(piece, 0, 0, 1)]

    noise_part, faces = pl.pallas_call(
        noise_kernel,
        out_shape=(
            jax.ShapeDtypeStruct((N_GZ * 64, N_GX * N_GY * PART), BF),
            jax.ShapeDtypeStruct((BX, ENS, 24, 128), BF),
        ),
        in_specs=[smem, vmem, vmem] + [anywhere] * 20,
        out_specs=(vmem, vmem),
        scratch_shapes=[
            pltpu.VMEM((N_GZ, 64, CELLS), BF),
            pltpu.VMEM((N_GX * N_GY * 2, HALF, CELLS), BF),
            pltpu.VMEM((256, 256), F32),
            pltpu.VMEM((256, 256), F32),
            pltpu.SemaphoreType.DMA,
            pltpu.SemaphoreType.DMA((N_GX,)),
        ],
        name="noise_part",
    )(place, select, row_order, *row_pieces, *pieces)

    copies = jnp.broadcast_to(
        faces[None, :, :, None], (N_GX // 2, BX, ENS, N_GZ, 24, 128)
    )
    received = lax.all_to_all(
        copies.reshape(128, 24, 128), ("gx", "gy", "gz"), 0, 0, tiled=True
    )
    home = [noise_part[:64]]
    for back in (1, 2, 3):
        home.append(line_shift(noise_part[back * 64 : (back + 1) * 64], -back))
    to_state = one_hot(iota((CELLS, STATE), 0) == jnp.asarray(STATE_CELLS)[None, :])
    step = to_bf16_dot(reorder, to_bf16_dot(kriging, to_state))
    received, step, *home = lax.optimization_barrier((received, step, *home))
    other_half = plane_shift(received, 0, 0, 1)

    chosen = pl.pallas_call(
        sweep_kernel,
        out_shape=jax.ShapeDtypeStruct((64, STATE), BF),
        in_specs=[smem, vmem, vmem, vmem],
        out_specs=vmem,
        scratch_shapes=[
            pltpu.VMEM((PLANES, SPAN_X * SLOTS * 8, 128), F32),
            pltpu.VMEM((PLANES, LEVELS * 64, 128), F32),
            pltpu.VMEM((PLANES, 64, 128), F32),
            pltpu.VMEM((PLANES, 64, 128), F32),
        ],
        name="sweep",
    )(sweep_place, received, other_half, step)

    upstream = lax.all_to_all(
        chosen.reshape(N_GY, TILES, STATE), "gy", 0, 0, tiled=True
    ).reshape(ENS * TILES, STATE)

    natural = pl.pallas_call(
        natural_kernel,
        out_shape=jax.ShapeDtypeStruct((TILES * ENS, CELLS), BF),
        in_specs=[smem] + [vmem] * 5,
        out_specs=vmem,
        name="natural",
    )(sweep_place, *home, spread)

    width = 1024
    out = pl.pallas_call(
        final_kernel,
        grid=(CELLS // width,),
        out_shape=jax.ShapeDtypeStruct((TILES * ENS, CELLS), F32),
        in_specs=[
            pl.BlockSpec((64, STATE), lambda g: (0, 0)),
            pl.BlockSpec((64, 64), lambda g: (0, 0)),
            pl.BlockSpec((STATE, STATE), lambda g: (0, 0)),
            pl.BlockSpec((STATE, width), lambda g: (0, g)),
            pl.BlockSpec((64, width), lambda g: (0, g)),
        ],
        out_specs=pl.BlockSpec((64, width), lambda g: (0, g)),
        name="evolve",
    )(upstream, swap_rows, reorder, kriging, natural)
    return out.reshape(BX, BY, BZ, ENS, CELLS)


def solution(mesh):
    placed = (
        P(None, ("gx", "gy")),
        P(),
        P("gx", "gy", "gz", None, None, None),
        P("gx", "gy", "gz", None),
    )
    return jax.shard_map(
        local,
        mesh=mesh,
        in_specs=placed,
        out_specs=P("gx", "gy", "gz", None, None),
        check_vma=False,
    )
```

```python
import functools

import jax
import jax.numpy as jnp
import numpy as np
from jax import lax
from jax.experimental import pallas as pl
from jax.experimental.pallas import tpu as pltpu
from jax.sharding import PartitionSpec as P

TILE = 16
CELLS = 4096
FACE = 256
BX = 2
BY = 2
BZ = 2
TILES = 8
ENS = 8
N_GX = 4
N_GY = 8
N_GZ = 4
SPAN_X = N_GX * BX
SPAN_Y = N_GY * BY
SPAN_Z = N_GZ * BZ
LEVELS = SPAN_X + SPAN_Y + SPAN_Z - 2
COLS_DEV = CELLS // (N_GX * N_GY)
PART = COLS_DEV // N_GZ
HALF = PART // 2
STATE = 3 * FACE
PLANES = STATE // 128
FACE_COLS = 352
SLOTS = SPAN_Y + SPAN_X - 1 + SPAN_Z - 1 + 14

BF = jnp.bfloat16
F32 = jnp.float32


def column_orders():
    orders = []
    for s in range(N_GZ):
        z_cells = [(4 * e + (s + 1) % 4) * TILE + TILE - 1 for e in range(2)]
        y_cells = [7 * TILE + 4 * ((s - 15) % 4) + m for m in range(4)]
        first = z_cells + [c for c in y_cells if c not in z_cells]
        part = [c for c in range(COLS_DEV) if (c // TILE + c % TILE // 4) % 4 == s]
        orders.append(first + [c for c in part if c not in first])
    return np.array(orders, np.int32)


ORDERS = column_orders()


def state_order():
    rows = np.zeros(STATE, np.int32)
    cells = np.zeros(STATE, np.int32)
    for f in range(STATE):
        plane, lane = divmod(f, 128)
        if plane < 4:
            s, slot = plane, lane % 64
            if lane < 64:
                i, q = 30 + slot // 32, slot % 32
                v, w = 8 * (i % 2) + ORDERS[s, q] // TILE, ORDERS[s, q] % TILE
                rows[f], cells[f] = v * 16 + w, (15 * 16 + v) * 16 + w
            else:
                u, w = slot // 4, 4 * ((s - 15) % 4) + slot % 4
                rows[f], cells[f] = FACE + u * 16 + w, (u * 16 + 15) * 16 + w
        else:
            s, slot = 2 * (plane - 4) + lane // 64, lane % 64
            i, e = slot // 2, slot % 2
            u, v = i // 2, 8 * (i % 2) + 4 * e + (s + 1) % 4
            rows[f], cells[f] = 2 * FACE + u * 16 + v, (u * 16 + v) * 16 + 15
    return rows, cells


STATE_ROWS, STATE_CELLS = state_order()


def one_hot(condition):
    return condition.astype(BF)


def iota(shape, axis):
    return lax.broadcasted_iota(jnp.int32, shape, axis)


def to_bf16_dot(left, right):
    return jnp.dot(left, right, preferred_element_type=F32).astype(BF)


def plane_shift(value, dx, dz, dc):
    pairs = []
    for gx in range(N_GX):
        for gy in range(N_GY):
            x, z, core = gy // 2, (gy % 2) * 2 + gx // 2, gx % 2
            x, z, core = (x + dx) % 4, (z + dz) % 4, core ^ dc
            pairs.append((gx * N_GY + gy, ((z % 2) * 2 + core) * N_GY + x * 2 + z // 2))
    return lax.ppermute(value, ("gx", "gy"), pairs)


def line_shift(value, steps):
    return lax.ppermute(value, "gz", [(s, (s + steps) % N_GZ) for s in range(N_GZ)])


def noise_kernel(place, *refs):
    row_refs = refs[:4]
    piece_refs = refs[4:20]
    noise_out = refs[20]
    rows, factors, acc, sem_rows, sem_factor = refs[21:]
    x, z, core = place[0], place[1], place[2]
    for back in range(N_GZ):
        pltpu.make_async_copy(row_refs[back], rows.at[back], sem_rows).start()
    groups = [(parity, swap) for parity in range(2) for swap in range(2)]
    for number, (parity, swap) in enumerate(groups):
        g = lax.rem(z + parity, 2) * 2 + (core if swap == 0 else 1 - core)
        for dz in (parity, parity + 2):
            high = lax.rem(z - dz + 4, 4) // 2
            for quarter in range(4):
                pltpu.make_async_copy(
                    piece_refs[dz * 2 + swap].at[pl.ds(quarter * 16, 16)],
                    factors.at[g, high * 4 + quarter],
                    sem_factor.at[number],
                ).start()
            for dx in range(4):
                sx = lax.rem(x - dx + 4, 4)
                pltpu.make_async_copy(
                    piece_refs[8 + dx * 2 + swap].at[pl.ds(parity * 32 + dz // 2 * 16, 16)],
                    factors.at[g, 8 + sx * 2 + high],
                    sem_factor.at[number],
                ).start()
    pltpu.make_async_copy(rows, rows, sem_rows).wait()
    wide = N_GY * PART
    for number, (parity, swap) in enumerate(groups):
        g = lax.rem(z + parity, 2) * 2 + (core if swap == 0 else 1 - core)
        block = factors.at[g]
        pltpu.make_async_copy(block, block, sem_factor.at[number]).wait()
        acc[...] = jnp.zeros_like(acc)

        @pl.loop(0, g + 1)
        def _(chunk):
            span = pl.ds(pl.multiple_of(chunk * 1024, 1024), 1024)
            acc[...] += lax.dot_general(
                rows[:, :, span].reshape(N_GZ * 64, 1024),
                factors[g, :, :, span].reshape(wide, 1024),
                (((1,), (1,)), ((), ())),
                preferred_element_type=F32,
            )

        noise_out[:, pl.ds(pl.multiple_of(g * wide, wide), wide)] = acc[...].astype(BF)


def face_kernel(place, select, row_order, *refs):
    row_refs = refs[:4]
    piece_refs = refs[4:20]
    face_out = refs[20]
    rows, factors, sem_rows, sem_factor = refs[21:]
    x, z, core = place[0], place[1], place[2]

    def load(ref, start, target):
        pltpu.make_async_copy(
            ref.at[pl.ds(start, 32)], factors.at[pl.ds(target, 32)], sem_factor
        ).start()

    for back in range(N_GZ):
        pltpu.make_async_copy(row_refs[back], rows.at[back], sem_rows).start()
    for swap in range(2):
        for dz in range(4):
            load(piece_refs[dz * 2 + swap], 0, 96 + (swap * 4 + dz) * 32)
    for parity in range(2):
        for swap in range(2):
            holds = (lax.rem(z + 1, 2) == parity) & (core == 1 - swap)

            @pl.when(holds)
            def _():
                load(piece_refs[parity * 2 + swap], 32, 0)
                load(piece_refs[(parity + 2) * 2 + swap], 32, 32)

            for dx in range(4):

                @pl.when(holds & (lax.rem(x + 1, 4) == dx))
                def _():
                    load(piece_refs[8 + dx * 2 + swap], parity * 32, 64)

    pltpu.make_async_copy(rows, rows, sem_rows).wait()
    pltpu.make_async_copy(factors, factors, sem_factor).wait()
    product = lax.dot_general(
        rows[...].reshape(N_GZ * 64, CELLS),
        factors[...],
        (((1,), (1,)), ((), ())),
        preferred_element_type=F32,
    ).astype(BF)
    sums = jnp.dot(product, select[...], preferred_element_type=F32).astype(BF)
    faces = jnp.dot(row_order[...], sums, preferred_element_type=F32)
    low = iota((8, 128), 1) < 64
    for r in range(ENS):
        for a in range(BX):
            base = r * 32 + a * 16
            face_out[a, r, 0:16, :] = faces[base : base + 16, :128].astype(BF)
            first = faces[base : base + 8, 128:]
            second = faces[base + 8 : base + 16, 128:]
            face_out[a, r, 16:24, :] = jnp.where(low, first, second).astype(BF)


def sweep_kernel(place, own_half, other_half, step, out, noise, history, state, picked):
    gx, core, gz = place[0], place[2], place[3]
    low8 = iota((8, 128), 1) < 64

    for p in range(PLANES):
        for i in range(SPAN_X):
            noise[p, i * SLOTS * 8 : (i * SLOTS + 14) * 8, :] = jnp.zeros((112, 128), F32)

    @pl.loop(0, N_GX * N_GY)
    def _(block):
        bx = block // N_GY
        by = lax.rem(block, N_GY)
        for a, half in ((core, own_half), (1 - core, other_half)):
            planes = [half[block * N_GZ + s, 0:16, :].astype(F32) for s in range(N_GZ)]
            zs = [half[block * N_GZ + s, 16:24, :].astype(F32) for s in range(N_GZ)]
            for b in range(BY):
                start = ((bx * BX + a) * SLOTS + by * BY + b + 14) * 8
                start = pl.multiple_of(start, 8)
                for p in range(4):
                    noise[p, pl.ds(start, 8), :] = planes[p][b * 8 : (b + 1) * 8]
                for pair in range(2):
                    first, second = zs[2 * pair], zs[2 * pair + 1]
                    if b == 0:
                        second = pltpu.roll(second, 64, 1)
                    else:
                        first = pltpu.roll(first, 64, 1)
                    noise[4 + pair, pl.ds(start, 8), :] = jnp.where(low8, first, second)

    state[...] = jnp.zeros_like(state)
    low = iota((64, 128), 1) < 64
    has_below = (iota((64, 128), 0) % 8) != 7

    @pl.loop(0, LEVELS)
    def _(level):
        upstream = []
        for p in range(PLANES):
            here = state[p]
            if p < 4:
                west = jnp.concatenate([jnp.zeros((8, 128), F32), here[:56]], 0)
                value = jnp.where(low, west, here)
            else:
                value = jnp.where(has_below, pltpu.roll(here, 63, 0), 0.0)
            history[p, pl.ds(pl.multiple_of(level * 64, 64), 64), :] = value
            upstream.append(value.astype(BF))
        result = jnp.dot(jnp.concatenate(upstream, 1), step[...], preferred_element_type=F32)
        for p in range(PLANES):
            rows = []
            for i in range(SPAN_X):
                start = (i * SLOTS + level - i + 7) * 8
                rows.append(noise[p, pl.ds(start, 8, stride=9), :])
            state[p] = result[:, p * 128 : (p + 1) * 128] + jnp.concatenate(rows, 0)

    for a in range(BX):
        for b in range(BY):
            for c in range(BZ):
                i = gx * BX + a
                k = gz * BZ + c
                start = (i + k + b) * 64 + i * 8 + 7 - k
                for p in range(PLANES):
                    picked[p, pl.ds((a * BY + b) * BZ + c, 8, stride=8), :] = history[
                        p, pl.ds(start, 8, stride=128), :
                    ]
    for p in range(PLANES):
        out[:, p * 128 : (p + 1) * 128] = picked[p].astype(BF)


def natural_kernel(place, first, second, third, fourth, spread, out):
    gz = place[3]
    total = jnp.zeros((256, 1024), F32)
    for back, part in enumerate((first, second, third, fourth)):
        source = lax.rem(gz + back, N_GZ)
        stacked = jnp.concatenate([part[:, g * 256 : (g + 1) * 256] for g in range(4)], 0)
        total += jnp.dot(stacked, spread[source], preferred_element_type=F32)
    for g in range(4):
        out[:, g * 1024 : (g + 1) * 1024] = total[g * 64 : (g + 1) * 64].astype(BF)


def final_kernel(faces, swap_rows, reorder, kriging, noise, out, upstream):
    @pl.when(pl.program_id(0) == 0)
    def _():
        rows = jnp.dot(swap_rows[...], faces[...], preferred_element_type=F32).astype(BF)
        upstream[...] = jnp.dot(rows, reorder[...], preferred_element_type=F32).astype(BF)

    product = jnp.dot(upstream[...], kriging[...], preferred_element_type=F32)
    out[...] = product + noise[...].astype(F32)


def select_table():
    table = np.full((N_GX, N_GY, N_GZ, 3, FACE_COLS), -1, np.int32)
    for gx in range(N_GX):
        for gy in range(N_GY):
            x, z, core = gy // 2, (gy % 2) * 2 + gx // 2, gx % 2
            parity = (z + 1) % 2
            for s in range(N_GZ):
                lanes = table[gx, gy, s]
                for j in range(2):
                    dz = parity + 2 * j
                    i = 30 + (z - dz) % 4 // 2
                    dx = (x - 3) % 4
                    for r in range(8):
                        lanes[0, j * 32 + dx * 8 + r] = (i - 30) * 32 + 8 + r
                    for r in range(16):
                        lanes[0, 64 + j * 16 + r] = (i - 30) * 32 + 16 + r
                for swap in range(2):
                    for dz in range(4):
                        for dx in range(4):
                            sx, sz, sc = (x - dx) % 4, (z - dz) % 4, core ^ swap
                            i = ((sz % 2) * 2 + sc) * N_GY + sx * 2 + sz // 2
                            base = 96 + swap * 128 + dz * 32 + dx * 8
                            for r in range(8):
                                column = ORDERS[s, r]
                                if i >= 30:
                                    lanes[0, base + r] = (i - 30) * 32 + r
                                if i % 2 == 1 and column // TILE == 7:
                                    lanes[1, base + r] = 64 + (i // 2) * 4 + column % 4
                                if r < 2:
                                    lanes[2, base + r] = 128 + i * 2 + r
    return table.reshape(-1, 3 * FACE_COLS)


def row_table():
    order = np.zeros((N_GZ, 256), np.int32)
    for gz in range(N_GZ):
        for target in range(256):
            k = 7 - target % 8
            tile = (target // 8 % 4) * 2 + k % 2
            order[gz, target] = ((gz - k // 2) % N_GZ) * 64 + tile * 8 + target // 32
    return order


def spread_table():
    table = np.zeros((4, N_GZ, 256), np.int32)
    for x in range(4):
        for s in range(N_GZ):
            for n in range(256):
                if n < 128:
                    high, q, sx = n // 64, n % 64 // 32 * 8 + n % 8, (x - n % 32 // 8) % 4
                else:
                    high, q, sx = n % 32 // 16, 16 + n % 16, (n - 128) // 32
                table[x, s, n] = (sx * 2 + high) * COLS_DEV + ORDERS[s, q]
    return table


def local(factor, kriging, normals, visit_order):
    gx = lax.axis_index("gx")
    gy = lax.axis_index("gy")
    gz = lax.axis_index("gz")
    place = jnp.stack([gy // 2, (gy % 2) * 2 + gx // 2, gx % 2, gz]).astype(jnp.int32)
    sweep_place = jnp.stack([gx, gy, gx % 2, gz]).astype(jnp.int32)
    vmem = pl.BlockSpec(memory_space=pltpu.VMEM)
    smem = pl.BlockSpec(memory_space=pltpu.SMEM)
    anywhere = pl.BlockSpec(memory_space=pl.ANY)

    own_columns = jnp.asarray(ORDERS)[gz]
    own = one_hot(iota((PART, COLS_DEV), 1) == own_columns[:, None])
    shard = lax.dot_general(
        own, factor, (((1,), (1,)), ((), ())), preferred_element_type=F32
    ).astype(BF)
    first, second = shard[:HALF], shard[HALF:]
    along_x = [first] + [plane_shift(first, d, 0, 0) for d in (1, 2, 3)]
    along_z = [second] + [plane_shift(second, 0, d, 0) for d in (1, 2, 3)]
    along_x = jnp.concatenate([t.reshape(2, 8, CELLS) for t in along_x], 1)
    along_x = along_x.reshape(4 * HALF, CELLS)
    along_z = jnp.concatenate([along_z[d] for d in (0, 2, 1, 3)], 0)

    drawn = normals.reshape(TILES, ENS, CELLS)
    ordered = drawn.at[visit_order.reshape(TILES)].get(mode="promise_in_bounds")
    ordered = ordered.reshape(TILES * ENS, CELLS)
    row_pieces = [ordered] + [line_shift(ordered, s) for s in (1, 2, 3)]

    late, kriging_late, along_x, along_z = lax.optimization_barrier(
        (gz, kriging, along_x, along_z)
    )
    lane = iota((FACE_COLS, 256), 1)
    device = (gx * N_GY + gy) * N_GZ + late
    lanes = jnp.asarray(select_table())[device].reshape(3, FACE_COLS, 1)
    select = one_hot(
        (lane == lanes[0]) | (lane == lanes[1]) | (lane == lanes[2])
        | ((lane - 64 == lanes[2]) & (lane >= 192))
    )
    row_order = one_hot(iota((256, 256), 1) == jnp.asarray(row_table())[late][:, None])
    spread = one_hot(
        iota((N_GZ, 256, 1024), 2) == jnp.asarray(spread_table())[gy // 2][:, :, None]
    )
    reorder = one_hot(jnp.asarray(STATE_ROWS)[:, None] == iota((STATE, STATE), 1))
    swap_rows = one_hot(
        iota((64, 64), 1) == jnp.asarray([(r % 8) * 8 + r // 8 for r in range(64)])[:, None]
    )
    to_state = one_hot(iota((CELLS, STATE), 0) == jnp.asarray(STATE_CELLS)[None, :])
    step = to_bf16_dot(reorder, to_bf16_dot(kriging_late, to_state))

    held_x = [along_x] + [plane_shift(along_x, 0, d, 0) for d in (1, 2, 3)]
    held_z = [along_z] + [plane_shift(along_z, d, 0, 0) for d in (1, 2, 3)]
    held_x[1], select, row_order, spread, step, place = lax.optimization_barrier(
        (held_x[1], select, row_order, spread, step, place)
    )
    pieces = []
    for piece in held_x + held_z:
        pieces += [piece, plane_shift(piece, 0, 0, 1)]

    faces = pl.pallas_call(
        face_kernel,
        out_shape=jax.ShapeDtypeStruct((BX, ENS, 24, 128), BF),
        in_specs=[smem, vmem, vmem] + [anywhere] * 20,
        out_specs=vmem,
        scratch_shapes=[
            pltpu.VMEM((N_GZ, 64, CELLS), BF),
            pltpu.VMEM((FACE_COLS, CELLS), BF),
            pltpu.SemaphoreType.DMA,
            pltpu.SemaphoreType.DMA,
        ],
        name="face_part",
    )(place, select, row_order, *row_pieces, *pieces)

    place, faces = lax.optimization_barrier((place, faces))
    noise_part = pl.pallas_call(
        noise_kernel,
        out_shape=jax.ShapeDtypeStruct((N_GZ * 64, N_GX * N_GY * PART), BF),
        in_specs=[smem] + [anywhere] * 20,
        out_specs=vmem,
        scratch_shapes=[
            pltpu.VMEM((N_GZ, 64, CELLS), BF),
            pltpu.VMEM((N_GX, 16, 16, CELLS), BF),
            pltpu.VMEM((256, 256), F32),
            pltpu.SemaphoreType.DMA,
            pltpu.SemaphoreType.DMA((N_GX,)),
        ],
        name="noise_part",
    )(place, *row_pieces, *pieces)

    copies = jnp.broadcast_to(
        faces[None, :, :, None], (N_GX // 2, BX, ENS, N_GZ, 24, 128)
    )
    received = lax.all_to_all(
        copies.reshape(128, 24, 128), ("gx", "gy", "gz"), 0, 0, tiled=True
    )
    home = [noise_part[:64]]
    for back in (1, 2, 3):
        home.append(line_shift(noise_part[back * 64 : (back + 1) * 64], -back))
    received, *home = lax.optimization_barrier((received, *home))
    other_half = plane_shift(received, 0, 0, 1)

    chosen = pl.pallas_call(
        sweep_kernel,
        out_shape=jax.ShapeDtypeStruct((64, STATE), BF),
        in_specs=[smem, vmem, vmem, vmem],
        out_specs=vmem,
        scratch_shapes=[
            pltpu.VMEM((PLANES, SPAN_X * SLOTS * 8, 128), F32),
            pltpu.VMEM((PLANES, LEVELS * 64, 128), F32),
            pltpu.VMEM((PLANES, 64, 128), F32),
            pltpu.VMEM((PLANES, 64, 128), F32),
        ],
        name="sweep",
    )(sweep_place, received, other_half, step)

    upstream = lax.all_to_all(
        chosen.reshape(N_GY, TILES, STATE), "gy", 0, 0, tiled=True
    ).reshape(ENS * TILES, STATE)

    natural = pl.pallas_call(
        natural_kernel,
        out_shape=jax.ShapeDtypeStruct((TILES * ENS, CELLS), BF),
        in_specs=[smem] + [vmem] * 5,
        out_specs=vmem,
        name="natural",
    )(sweep_place, *home, spread)

    width = 1024
    out = pl.pallas_call(
        final_kernel,
        grid=(CELLS // width,),
        out_shape=jax.ShapeDtypeStruct((TILES * ENS, CELLS), F32),
        in_specs=[
            pl.BlockSpec((64, STATE), lambda g: (0, 0)),
            pl.BlockSpec((64, 64), lambda g: (0, 0)),
            pl.BlockSpec((STATE, STATE), lambda g: (0, 0)),
            pl.BlockSpec((STATE, width), lambda g: (0, g)),
            pl.BlockSpec((64, width), lambda g: (0, g)),
        ],
        out_specs=pl.BlockSpec((64, width), lambda g: (0, g)),
        scratch_shapes=[pltpu.VMEM((64, STATE), BF)],
        name="evolve",
    )(upstream, swap_rows, reorder, kriging, natural)
    return out.reshape(BX, BY, BZ, ENS, CELLS)


def solution(mesh):
    placed = (
        P(None, ("gx", "gy")),
        P(),
        P("gx", "gy", "gz", None, None, None),
        P("gx", "gy", "gz", None),
    )
    return jax.shard_map(
        local,
        mesh=mesh,
        in_specs=placed,
        out_specs=P("gx", "gy", "gz", None, None),
        check_vma=False,
    )
```

```python
import functools

import jax
import jax.numpy as jnp
import numpy as np
from jax import lax
from jax.experimental import pallas as pl
from jax.experimental.pallas import tpu as pltpu
from jax.sharding import PartitionSpec as P

TILE = 16
CELLS = 4096
FACE = 256
BX = 2
BY = 2
BZ = 2
TILES = 8
ENS = 8
N_GX = 4
N_GY = 8
N_GZ = 4
SPAN_X = N_GX * BX
SPAN_Y = N_GY * BY
SPAN_Z = N_GZ * BZ
LEVELS = SPAN_X + SPAN_Y + SPAN_Z - 2
COLS_DEV = CELLS // (N_GX * N_GY)
PART = COLS_DEV // N_GZ
HALF = PART // 2
STATE = 3 * FACE
PLANES = STATE // 128
FACE_COLS = 352
SLOTS = SPAN_Y + SPAN_X - 1 + SPAN_Z - 1 + 14

BF = jnp.bfloat16
F32 = jnp.float32


def column_orders():
    orders = []
    for s in range(N_GZ):
        z_cells = [(4 * e + (s + 1) % 4) * TILE + TILE - 1 for e in range(2)]
        y_cells = [7 * TILE + 4 * ((s - 15) % 4) + m for m in range(4)]
        first = z_cells + [c for c in y_cells if c not in z_cells]
        part = [c for c in range(COLS_DEV) if (c // TILE + c % TILE // 4) % 4 == s]
        orders.append(first + [c for c in part if c not in first])
    return np.array(orders, np.int32)


ORDERS = column_orders()


def state_order():
    rows = np.zeros(STATE, np.int32)
    cells = np.zeros(STATE, np.int32)
    for f in range(STATE):
        plane, lane = divmod(f, 128)
        if plane < 4:
            s, slot = plane, lane % 64
            if lane < 64:
                i, q = 30 + slot // 32, slot % 32
                v, w = 8 * (i % 2) + ORDERS[s, q] // TILE, ORDERS[s, q] % TILE
                rows[f], cells[f] = v * 16 + w, (15 * 16 + v) * 16 + w
            else:
                u, w = slot // 4, 4 * ((s - 15) % 4) + slot % 4
                rows[f], cells[f] = FACE + u * 16 + w, (u * 16 + 15) * 16 + w
        else:
            s, slot = 2 * (plane - 4) + lane // 64, lane % 64
            i, e = slot // 2, slot % 2
            u, v = i // 2, 8 * (i % 2) + 4 * e + (s + 1) % 4
            rows[f], cells[f] = 2 * FACE + u * 16 + v, (u * 16 + v) * 16 + 15
    return rows, cells


STATE_ROWS, STATE_CELLS = state_order()


def one_hot(condition):
    return condition.astype(BF)


def iota(shape, axis):
    return lax.broadcasted_iota(jnp.int32, shape, axis)


def to_bf16_dot(left, right):
    return jnp.dot(left, right, preferred_element_type=F32).astype(BF)


def plane_shift(value, dx, dz, dc):
    pairs = []
    for gx in range(N_GX):
        for gy in range(N_GY):
            x, z, core = gy // 2, (gy % 2) * 2 + gx // 2, gx % 2
            x, z, core = (x + dx) % 4, (z + dz) % 4, core ^ dc
            pairs.append((gx * N_GY + gy, ((z % 2) * 2 + core) * N_GY + x * 2 + z // 2))
    return lax.ppermute(value, ("gx", "gy"), pairs)


def line_shift(value, steps):
    return lax.ppermute(value, "gz", [(s, (s + steps) % N_GZ) for s in range(N_GZ)])


def noise_kernel(place, *refs):
    row_refs = refs[:4]
    piece_refs = refs[4:20]
    noise_out = refs[20]
    rows, factors, acc, sem_rows, sem_factor = refs[21:]
    x, z, core = place[0], place[1], place[2]
    for back in range(N_GZ):
        pltpu.make_async_copy(row_refs[back], rows.at[back], sem_rows).start()
    groups = [(parity, swap) for parity in range(2) for swap in range(2)]
    for number, (parity, swap) in enumerate(groups):
        g = lax.rem(z + parity, 2) * 2 + (core if swap == 0 else 1 - core)
        for dz in (parity, parity + 2):
            high = lax.rem(z - dz + 4, 4) // 2
            for quarter in range(4):
                pltpu.make_async_copy(
                    piece_refs[dz * 2 + swap].at[pl.ds(quarter * 16, 16)],
                    factors.at[g, high * 4 + quarter],
                    sem_factor.at[number],
                ).start()
            for dx in range(4):
                sx = lax.rem(x - dx + 4, 4)
                pltpu.make_async_copy(
                    piece_refs[8 + dx * 2 + swap].at[pl.ds(parity * 32 + dz // 2 * 16, 16)],
                    factors.at[g, 8 + sx * 2 + high],
                    sem_factor.at[number],
                ).start()
    pltpu.make_async_copy(rows, rows, sem_rows).wait()
    wide = N_GY * PART
    for number, (parity, swap) in enumerate(groups):
        g = lax.rem(z + parity, 2) * 2 + (core if swap == 0 else 1 - core)
        block = factors.at[g]
        pltpu.make_async_copy(block, block, sem_factor.at[number]).wait()
        acc[...] = jnp.zeros_like(acc)

        @pl.loop(0, g + 1)
        def _(chunk):
            span = pl.ds(pl.multiple_of(chunk * 1024, 1024), 1024)
            acc[...] += lax.dot_general(
                rows[:, :, span].reshape(N_GZ * 64, 1024),
                factors[g, :, :, span].reshape(wide, 1024),
                (((1,), (1,)), ((), ())),
                preferred_element_type=F32,
            )

        noise_out[:, pl.ds(pl.multiple_of(g * wide, wide), wide)] = acc[...].astype(BF)


def face_kernel(place, select, row_order, *refs):
    row_refs = refs[:4]
    piece_refs = refs[4:20]
    copies_out = refs[20]
    rows, factors, face_out, sem_rows, sem_factor, sem_out = refs[21:]
    x, z, core = place[0], place[1], place[2]

    def load(ref, start, target):
        pltpu.make_async_copy(
            ref.at[pl.ds(start, 32)], factors.at[pl.ds(target, 32)], sem_factor
        ).start()

    for back in range(N_GZ):
        pltpu.make_async_copy(row_refs[back], rows.at[back], sem_rows).start()
    for swap in range(2):
        for dz in range(4):
            load(piece_refs[dz * 2 + swap], 0, 96 + (swap * 4 + dz) * 32)
    for parity in range(2):
        for swap in range(2):
            holds = (lax.rem(z + 1, 2) == parity) & (core == 1 - swap)

            @pl.when(holds)
            def _():
                load(piece_refs[parity * 2 + swap], 32, 0)
                load(piece_refs[(parity + 2) * 2 + swap], 32, 32)

            for dx in range(4):

                @pl.when(holds & (lax.rem(x + 1, 4) == dx))
                def _():
                    load(piece_refs[8 + dx * 2 + swap], parity * 32, 64)

    pltpu.make_async_copy(rows, rows, sem_rows).wait()
    pltpu.make_async_copy(factors, factors, sem_factor).wait()
    product = lax.dot_general(
        rows[...].reshape(N_GZ * 64, CELLS),
        factors[...],
        (((1,), (1,)), ((), ())),
        preferred_element_type=F32,
    ).astype(BF)
    sums = jnp.dot(product, select[...], preferred_element_type=F32).astype(BF)
    faces = jnp.dot(row_order[...], sums, preferred_element_type=F32)
    low = iota((8, 128), 1) < 64
    for r in range(ENS):
        for a in range(BX):
            base = r * 32 + a * 16
            face_out[a, r, 0:16, :] = faces[base : base + 16, :128].astype(BF)
            first = faces[base : base + 8, 128:]
            second = faces[base + 8 : base + 16, 128:]
            face_out[a, r, 16:24, :] = jnp.where(low, first, second).astype(BF)
    copies = [
        pltpu.make_async_copy(face_out, copies_out.at[side, :, :, k], sem_out.at[side * N_GZ + k])
        for side in range(N_GX // 2)
        for k in range(N_GZ)
    ]
    for copy in copies:
        copy.start()
    for copy in copies:
        copy.wait()


def sweep_kernel(place, own_ref, other_ref, step_ref, reorder_ref, out, *scratch):
    noise, history, state, picked, own_half, other_half, step, reorder, sems = scratch
    gx, core, gz = place[0], place[2], place[3]
    low8 = iota((8, 128), 1) < 64
    count = N_GY * N_GZ
    for bx in range(N_GX):
        chunk = pl.ds(bx * count, count)
        pltpu.make_async_copy(own_ref.at[chunk], own_half.at[chunk], sems.at[2 * bx]).start()
        pltpu.make_async_copy(other_ref.at[chunk], other_half.at[chunk], sems.at[2 * bx + 1]).start()
    load_step = pltpu.make_async_copy(step_ref, step, sems.at[8])
    load_reorder = pltpu.make_async_copy(reorder_ref, reorder, sems.at[9])
    load_step.start()
    load_reorder.start()

    for p in range(PLANES):
        for i in range(SPAN_X):
            noise[p, i * SLOTS * 8 : (i * SLOTS + 14) * 8, :] = jnp.zeros((112, 128), F32)

    def place_block(bx, by):
        block = bx * N_GY + by
        for a, half in ((core, own_half), (1 - core, other_half)):
            planes = [half[block * N_GZ + s, 0:16, :].astype(F32) for s in range(N_GZ)]
            zs = [half[block * N_GZ + s, 16:24, :].astype(F32) for s in range(N_GZ)]
            for b in range(BY):
                start = ((bx * BX + a) * SLOTS + by * BY + b + 14) * 8
                start = pl.multiple_of(start, 8)
                for p in range(4):
                    noise[p, pl.ds(start, 8), :] = planes[p][b * 8 : (b + 1) * 8]
                for pair in range(2):
                    first, second = zs[2 * pair], zs[2 * pair + 1]
                    if b == 0:
                        second = pltpu.roll(second, 64, 1)
                    else:
                        first = pltpu.roll(first, 64, 1)
                    noise[4 + pair, pl.ds(start, 8), :] = jnp.where(low8, first, second)

    for bx in range(N_GX):
        chunk = pl.ds(bx * count, count)
        pltpu.make_async_copy(own_ref.at[chunk], own_half.at[chunk], sems.at[2 * bx]).wait()
        pltpu.make_async_copy(other_ref.at[chunk], other_half.at[chunk], sems.at[2 * bx + 1]).wait()

        @pl.loop(0, N_GY)
        def _(by):
            place_block(bx, by)

    state[...] = jnp.zeros_like(state)
    low = iota((64, 128), 1) < 64
    has_below = (iota((64, 128), 0) % 8) != 7
    load_step.wait()

    @pl.loop(0, LEVELS)
    def _(level):
        upstream = []
        for p in range(PLANES):
            here = state[p]
            if p < 4:
                west = jnp.concatenate([jnp.zeros((8, 128), F32), here[:56]], 0)
                value = jnp.where(low, west, here)
            else:
                value = jnp.where(has_below, pltpu.roll(here, 63, 0), 0.0)
            history[p, pl.ds(pl.multiple_of(level * 64, 64), 64), :] = value
            upstream.append(value.astype(BF))
        result = jnp.dot(jnp.concatenate(upstream, 1), step[...], preferred_element_type=F32)
        for p in range(PLANES):
            rows = []
            for i in range(SPAN_X):
                start = (i * SLOTS + level - i + 7) * 8
                rows.append(noise[p, pl.ds(start, 8, stride=9), :])
            state[p] = result[:, p * 128 : (p + 1) * 128] + jnp.concatenate(rows, 0)

    for a in range(BX):
        for b in range(BY):
            for c in range(BZ):
                i = gx * BX + a
                k = gz * BZ + c
                start = (i + k + b) * 64 + i * 8 + 7 - k
                for p in range(PLANES):
                    picked[p, pl.ds((a * BY + b) * BZ + c, 8, stride=8), :] = history[
                        p, pl.ds(start, 8, stride=128), :
                    ]
    load_reorder.wait()
    values = jnp.concatenate([picked[p].astype(BF) for p in range(PLANES)], 1)
    out[...] = jnp.dot(values, reorder[...], preferred_element_type=F32).astype(BF)


def natural_kernel(place, first, second, third, fourth, spread, out):
    gz = place[3]
    total = jnp.zeros((256, 1024), F32)
    for back, part in enumerate((first, second, third, fourth)):
        source = lax.rem(gz + back, N_GZ)
        stacked = jnp.concatenate([part[:, g * 256 : (g + 1) * 256] for g in range(4)], 0)
        total += jnp.dot(stacked, spread[source], preferred_element_type=F32)
    for g in range(4):
        out[:, g * 1024 : (g + 1) * 1024] = total[g * 64 : (g + 1) * 64].astype(BF)


def final_kernel(faces, swap_rows, kriging, noise, out, upstream):
    @pl.when(pl.program_id(0) == 0)
    def _():
        upstream[...] = jnp.dot(swap_rows[...], faces[...], preferred_element_type=F32).astype(BF)

    product = jnp.dot(upstream[...], kriging[...], preferred_element_type=F32)
    out[...] = product + noise[...].astype(F32)


def select_table():
    table = np.full((N_GX, N_GY, N_GZ, 3, FACE_COLS), -1, np.int32)
    for gx in range(N_GX):
        for gy in range(N_GY):
            x, z, core = gy // 2, (gy % 2) * 2 + gx // 2, gx % 2
            parity = (z + 1) % 2
            for s in range(N_GZ):
                lanes = table[gx, gy, s]
                for j in range(2):
                    dz = parity + 2 * j
                    i = 30 + (z - dz) % 4 // 2
                    dx = (x - 3) % 4
                    for r in range(8):
                        lanes[0, j * 32 + dx * 8 + r] = (i - 30) * 32 + 8 + r
                    for r in range(16):
                        lanes[0, 64 + j * 16 + r] = (i - 30) * 32 + 16 + r
                for swap in range(2):
                    for dz in range(4):
                        for dx in range(4):
                            sx, sz, sc = (x - dx) % 4, (z - dz) % 4, core ^ swap
                            i = ((sz % 2) * 2 + sc) * N_GY + sx * 2 + sz // 2
                            base = 96 + swap * 128 + dz * 32 + dx * 8
                            for r in range(8):
                                column = ORDERS[s, r]
                                if i >= 30:
                                    lanes[0, base + r] = (i - 30) * 32 + r
                                if i % 2 == 1 and column // TILE == 7:
                                    lanes[1, base + r] = 64 + (i // 2) * 4 + column % 4
                                if r < 2:
                                    lanes[2, base + r] = 128 + i * 2 + r
    return table.reshape(-1, 3 * FACE_COLS)


def row_table():
    order = np.zeros((N_GZ, 256), np.int32)
    for gz in range(N_GZ):
        for target in range(256):
            k = 7 - target % 8
            tile = (target // 8 % 4) * 2 + k % 2
            order[gz, target] = ((gz - k // 2) % N_GZ) * 64 + tile * 8 + target // 32
    return order


def spread_table():
    table = np.zeros((4, N_GZ, 256), np.int32)
    for x in range(4):
        for s in range(N_GZ):
            for n in range(256):
                if n < 128:
                    high, q, sx = n // 64, n % 64 // 32 * 8 + n % 8, (x - n % 32 // 8) % 4
                else:
                    high, q, sx = n % 32 // 16, 16 + n % 16, (n - 128) // 32
                table[x, s, n] = (sx * 2 + high) * COLS_DEV + ORDERS[s, q]
    return table


def local(factor, kriging, normals, visit_order):
    gx = lax.axis_index("gx")
    gy = lax.axis_index("gy")
    gz = lax.axis_index("gz")
    place = jnp.stack([gy // 2, (gy % 2) * 2 + gx // 2, gx % 2, gz]).astype(jnp.int32)
    sweep_place = jnp.stack([gx, gy, gx % 2, gz]).astype(jnp.int32)
    vmem = pl.BlockSpec(memory_space=pltpu.VMEM)
    smem = pl.BlockSpec(memory_space=pltpu.SMEM)
    anywhere = pl.BlockSpec(memory_space=pl.ANY)

    own_columns = jnp.asarray(ORDERS)[gz]
    own = one_hot(iota((PART, COLS_DEV), 1) == own_columns[:, None])
    shard = lax.dot_general(
        own, factor, (((1,), (1,)), ((), ())), preferred_element_type=F32
    ).astype(BF)
    first, second = shard[:HALF], shard[HALF:]
    along_x = [first] + [plane_shift(first, d, 0, 0) for d in (1, 2, 3)]
    along_z = [second] + [plane_shift(second, 0, d, 0) for d in (1, 2, 3)]
    along_x = jnp.concatenate([t.reshape(2, 8, CELLS) for t in along_x], 1)
    along_x = along_x.reshape(4 * HALF, CELLS)
    along_z = jnp.concatenate([along_z[d] for d in (0, 2, 1, 3)], 0)

    drawn = normals.reshape(TILES, ENS, CELLS)
    ordered = drawn.at[visit_order.reshape(TILES)].get(mode="promise_in_bounds")
    ordered = ordered.reshape(TILES * ENS, CELLS)
    row_pieces = [ordered] + [line_shift(ordered, s) for s in (1, 2, 3)]

    late, kriging_late, along_x, along_z = lax.optimization_barrier(
        (gz, kriging, along_x, along_z)
    )
    lane = iota((FACE_COLS, 256), 1)
    device = (gx * N_GY + gy) * N_GZ + late
    lanes = jnp.asarray(select_table())[device].reshape(3, FACE_COLS, 1)
    select = one_hot(
        (lane == lanes[0]) | (lane == lanes[1]) | (lane == lanes[2])
        | ((lane - 64 == lanes[2]) & (lane >= 192))
    )
    row_order = one_hot(iota((256, 256), 1) == jnp.asarray(row_table())[late][:, None])
    spread = one_hot(
        iota((N_GZ, 256, 1024), 2) == jnp.asarray(spread_table())[gy // 2][:, :, None]
    )
    reorder = one_hot(jnp.asarray(STATE_ROWS)[:, None] == iota((STATE, STATE), 1))
    swap_rows = one_hot(
        iota((64, 64), 1) == jnp.asarray([(r % 8) * 8 + r // 8 for r in range(64)])[:, None]
    )
    to_state = one_hot(iota((CELLS, STATE), 0) == jnp.asarray(STATE_CELLS)[None, :])
    step = to_bf16_dot(reorder, to_bf16_dot(kriging_late, to_state))

    held_x = [along_x] + [plane_shift(along_x, 0, d, 0) for d in (1, 2, 3)]
    held_z = [along_z] + [plane_shift(along_z, d, 0, 0) for d in (1, 2, 3)]
    held_x[1], select, row_order, spread, step, reorder, place = lax.optimization_barrier(
        (held_x[1], select, row_order, spread, step, reorder, place)
    )
    pieces = []
    for piece in held_x + held_z:
        pieces += [piece, plane_shift(piece, 0, 0, 1)]

    copies = pl.pallas_call(
        face_kernel,
        out_shape=jax.ShapeDtypeStruct((N_GX // 2, BX, ENS, N_GZ, 24, 128), BF),
        in_specs=[smem, vmem, vmem] + [anywhere] * 20,
        out_specs=anywhere,
        scratch_shapes=[
            pltpu.VMEM((N_GZ, 64, CELLS), BF),
            pltpu.VMEM((FACE_COLS, CELLS), BF),
            pltpu.VMEM((BX, ENS, 24, 128), BF),
            pltpu.SemaphoreType.DMA,
            pltpu.SemaphoreType.DMA,
            pltpu.SemaphoreType.DMA((N_GX // 2 * N_GZ,)),
        ],
        name="face_part",
    )(place, select, row_order, *row_pieces, *pieces)

    place, copies = lax.optimization_barrier((place, copies))
    noise_part = pl.pallas_call(
        noise_kernel,
        out_shape=jax.ShapeDtypeStruct((N_GZ * 64, N_GX * N_GY * PART), BF),
        in_specs=[smem] + [anywhere] * 20,
        out_specs=vmem,
        scratch_shapes=[
            pltpu.VMEM((N_GZ, 64, CELLS), BF),
            pltpu.VMEM((N_GX, 16, 16, CELLS), BF),
            pltpu.VMEM((256, 256), F32),
            pltpu.SemaphoreType.DMA,
            pltpu.SemaphoreType.DMA((N_GX,)),
        ],
        name="noise_part",
    )(place, *row_pieces, *pieces)

    with jax.named_scope("face_exchange"):
        received = lax.all_to_all(
            copies.reshape(128, 24, 128), ("gx", "gy", "gz"), 0, 0, tiled=True
        )
    parts = [noise_part[back * 64 : (back + 1) * 64] for back in range(N_GZ)]
    received, *parts = lax.optimization_barrier((received, *parts))
    home = [parts[0]] + [line_shift(parts[back], -back) for back in (1, 2, 3)]
    other_half = plane_shift(received, 0, 0, 1)

    chosen = pl.pallas_call(
        sweep_kernel,
        out_shape=jax.ShapeDtypeStruct((64, STATE), BF),
        in_specs=[smem] + [anywhere] * 4,
        out_specs=vmem,
        scratch_shapes=[
            pltpu.VMEM((PLANES, SPAN_X * SLOTS * 8, 128), F32),
            pltpu.VMEM((PLANES, LEVELS * 64, 128), F32),
            pltpu.VMEM((PLANES, 64, 128), F32),
            pltpu.VMEM((PLANES, 64, 128), F32),
            pltpu.VMEM((128, 24, 128), BF),
            pltpu.VMEM((128, 24, 128), BF),
            pltpu.VMEM((STATE, STATE), BF),
            pltpu.VMEM((STATE, STATE), BF),
            pltpu.SemaphoreType.DMA((10,)),
        ],
        name="sweep",
    )(sweep_place, received, other_half, step, reorder)

    upstream = lax.all_to_all(
        chosen.reshape(N_GY, TILES, STATE), "gy", 0, 0, tiled=True
    ).reshape(ENS * TILES, STATE)

    natural = pl.pallas_call(
        natural_kernel,
        out_shape=jax.ShapeDtypeStruct((TILES * ENS, CELLS), BF),
        in_specs=[smem] + [vmem] * 5,
        out_specs=vmem,
        name="natural",
    )(sweep_place, *home, spread)

    width = 1024
    out = pl.pallas_call(
        final_kernel,
        grid=(CELLS // width,),
        out_shape=jax.ShapeDtypeStruct((TILES * ENS, CELLS), F32),
        in_specs=[
            pl.BlockSpec((64, STATE), lambda g: (0, 0)),
            pl.BlockSpec((64, 64), lambda g: (0, 0)),
            pl.BlockSpec((STATE, width), lambda g: (0, g)),
            pl.BlockSpec((64, width), lambda g: (0, g)),
        ],
        out_specs=pl.BlockSpec((64, width), lambda g: (0, g)),
        scratch_shapes=[pltpu.VMEM((64, STATE), BF)],
        name="evolve",
    )(upstream, swap_rows, kriging, natural)
    return out.reshape(BX, BY, BZ, ENS, CELLS)


def solution(mesh):
    placed = (
        P(None, ("gx", "gy")),
        P(),
        P("gx", "gy", "gz", None, None, None),
        P("gx", "gy", "gz", None),
    )
    return jax.shard_map(
        local,
        mesh=mesh,
        in_specs=placed,
        out_specs=P("gx", "gy", "gz", None, None),
        check_vma=False,
    )
```

```python
import jax
import jax.numpy as jnp
import numpy as np
from jax import lax
from jax.experimental import pallas as pl
from jax.experimental.pallas import tpu as pltpu
from jax.sharding import PartitionSpec as P


TILE = 16
CELLS = 4096
FACE = 256
BX = 2
BY = 2
BZ = 2
TILES = 8
ENS = 8
N_GX = 4
N_GY = 8
N_GZ = 4
SPAN_X = N_GX * BX
SPAN_Y = N_GY * BY
SPAN_Z = N_GZ * BZ
LEVELS = SPAN_X + SPAN_Y + SPAN_Z - 2
COLS_DEV = CELLS // (N_GX * N_GY)
PART = COLS_DEV // N_GZ
HALF = PART // 2
STATE = 3 * FACE
PLANES = STATE // 128
FACE_COLS = 352
SLOTS = SPAN_Y + SPAN_X - 1 + SPAN_Z - 1 + 14

BF = jnp.bfloat16
F32 = jnp.float32


def column_orders():
    orders = []
    for s in range(N_GZ):
        z_cells = [(4 * e + (s + 1) % 4) * TILE + TILE - 1 for e in range(2)]
        y_cells = [7 * TILE + 4 * ((s - 15) % 4) + m for m in range(4)]
        first = z_cells + [c for c in y_cells if c not in z_cells]
        part = [c for c in range(COLS_DEV) if (c // TILE + c % TILE // 4) % 4 == s]
        orders.append(first + [c for c in part if c not in first])
    return np.array(orders, np.int32)


ORDERS = column_orders()


def state_order():
    rows = np.zeros(STATE, np.int32)
    cells = np.zeros(STATE, np.int32)
    for f in range(STATE):
        plane, lane = divmod(f, 128)
        if plane < 4:
            s, slot = plane, lane % 64
            if lane < 64:
                i, q = 30 + slot // 32, slot % 32
                v, w = 8 * (i % 2) + ORDERS[s, q] // TILE, ORDERS[s, q] % TILE
                rows[f], cells[f] = v * 16 + w, (15 * 16 + v) * 16 + w
            else:
                u, w = slot // 4, 4 * ((s - 15) % 4) + slot % 4
                rows[f], cells[f] = FACE + u * 16 + w, (u * 16 + 15) * 16 + w
        else:
            s, slot = 2 * (plane - 4) + lane // 64, lane % 64
            i, e = slot // 2, slot % 2
            u, v = i // 2, 8 * (i % 2) + 4 * e + (s + 1) % 4
            rows[f], cells[f] = 2 * FACE + u * 16 + v, (u * 16 + v) * 16 + 15
    return rows, cells


STATE_ROWS, STATE_CELLS = state_order()


def one_hot(condition):
    return condition.astype(BF)


def iota(shape, axis):
    return lax.broadcasted_iota(jnp.int32, shape, axis)


def to_bf16_dot(left, right):
    return jnp.dot(left, right, preferred_element_type=F32).astype(BF)


def plane_shift(value, dx, dz, swap=0):
    pairs = []
    for gx in range(N_GX):
        for gy in range(N_GY):
            x, z, core = gy // 2, (gy % 2) * 2 + gx // 2, gx % 2
            move_x, move_z = (dx, dz) if core == 0 else (dz, dx)
            x, z, core = (x + move_x) % 4, (z + move_z) % 4, core ^ swap
            pairs.append((gx * N_GY + gy, ((z % 2) * 2 + core) * N_GY + x * 2 + z // 2))
    return lax.ppermute(value, ("gx", "gy"), pairs)


def line_shift(value, steps):
    return lax.ppermute(value, "gz", [(s, (s + steps) % N_GZ) for s in range(N_GZ)])


def slot_of(d):
    return d % 2 * 2 + d // 2


def by_core(core, refs, body):
    own, other = refs[:4], refs[4:]

    @pl.when(core == 0)
    def _():
        body(own, other)

    @pl.when(core == 1)
    def _():
        body(other, own)


def noise_kernel(place, *refs):
    row_refs = refs[:4]
    piece_refs = refs[4:12]
    noise_out = refs[12]
    rows, factors, acc, sem_rows, sem_factor = refs[13:]
    x, z, core = place[0], place[1], place[2]
    for back in range(N_GZ):
        pltpu.make_async_copy(row_refs[back], rows.at[back], sem_rows).start()

    def load_all(first_refs, second_refs):
        for parity in range(2):
            group = lax.rem(z + parity, 2)
            for dz in (parity, parity + 2):
                high = lax.rem(z - dz + 4, 4) // 2
                for dx in range(4):
                    target = (lax.rem(x - dx + 4, 4) * 2 + high) * 4
                    for t in range(2):
                        for ref, slot, kind in (
                            (first_refs[dz], slot_of(dx), 0),
                            (second_refs[dx], slot_of(dz), 2),
                        ):
                            pltpu.make_async_copy(
                                ref.at[pl.ds(t * 64 + slot * 16, 16)],
                                factors.at[group, target + kind + t],
                                sem_factor.at[parity],
                            ).start()

    by_core(core, piece_refs, load_all)
    pltpu.make_async_copy(rows, rows, sem_rows).wait()
    wide = 512
    for parity in range(2):
        group = lax.rem(z + parity, 2)
        block = factors.at[group]
        pltpu.make_async_copy(block, block, sem_factor.at[parity]).wait()
        acc[...] = jnp.zeros_like(acc)

        @pl.loop(0, 2 * group + 2)
        def _(chunk):
            span = pl.ds(pl.multiple_of(chunk * 1024, 1024), 1024)
            acc[...] += lax.dot_general(
                rows[:, :, span].reshape(N_GZ * 64, 1024),
                factors[group, :, :, span].reshape(wide, 1024),
                (((1,), (1,)), ((), ())),
                preferred_element_type=F32,
            )

        noise_out[:, pl.ds(pl.multiple_of(group * wide, wide), wide)] = acc[...].astype(BF)


def face_kernel(place, select, row_order, *refs):
    row_refs = refs[:4]
    piece_refs = refs[4:12]
    copies_out = refs[12]
    rows, factors, face_out, sem_rows, sem_factor, sem_out = refs[13:]
    x, z, core = place[0], place[1], place[2]
    odd = lax.rem(z + 1, 2)
    holder = lax.rem(x + 1, 4)

    def load(ref, start, target, count):
        pltpu.make_async_copy(
            ref.at[pl.ds(start, count)], factors.at[pl.ds(target, count)], sem_factor
        ).start()

    for back in range(N_GZ):
        pltpu.make_async_copy(row_refs[back], rows.at[back], sem_rows).start()

    def load_all(first_refs, second_refs):
        for dz in range(4):
            load(first_refs[dz], 0, 96 + dz * 64, 64)
        held = pl.multiple_of(64 + slot_of(holder) * 16, 16)
        part = pl.multiple_of(odd * 32, 32)
        for parity in range(2):

            @pl.when(odd == parity)
            def _():
                load(first_refs[parity], held, 0, 16)
                load(first_refs[parity + 2], held, 16, 16)

        for dx in range(4):

            @pl.when(holder == dx)
            def _():
                load(second_refs[dx], part, 32, 32)
                load(second_refs[dx], part + 64, 64, 32)

    by_core(core, piece_refs, load_all)
    pltpu.make_async_copy(rows, rows, sem_rows).wait()
    pltpu.make_async_copy(factors, factors, sem_factor).wait()
    product = lax.dot_general(
        rows[...].reshape(N_GZ * 64, CELLS),
        factors[...],
        (((1,), (1,)), ((), ())),
        preferred_element_type=F32,
    ).astype(BF)
    sums = jnp.dot(product, select[...], preferred_element_type=F32).astype(BF)
    faces = jnp.dot(row_order[...], sums, preferred_element_type=F32)
    low = iota((8, 128), 1) < 64
    for r in range(ENS):
        for a in range(BX):
            base = r * 32 + a * 16
            face_out[a, r, 0:16, :] = faces[base : base + 16, :128].astype(BF)
            first = faces[base : base + 8, 128:]
            second = faces[base + 8 : base + 16, 128:]
            face_out[a, r, 16:24, :] = jnp.where(low, first, second).astype(BF)
    copies = [
        pltpu.make_async_copy(face_out, copies_out.at[side, :, :, k], sem_out.at[side * N_GZ + k])
        for side in range(N_GX // 2)
        for k in range(N_GZ)
    ]
    for copy in copies:
        copy.start()
    for copy in copies:
        copy.wait()


def sweep_kernel(place, own_ref, other_ref, step_ref, reorder_ref, out, *scratch):
    noise, history, state, picked, own_half, other_half, step, reorder, sems = scratch
    gx, core, gz = place[0], place[2], place[3]
    low8 = iota((8, 128), 1) < 64
    count = N_GY * N_GZ
    for bx in range(N_GX):
        chunk = pl.ds(bx * count, count)
        pltpu.make_async_copy(own_ref.at[chunk], own_half.at[chunk], sems.at[2 * bx]).start()
        pltpu.make_async_copy(other_ref.at[chunk], other_half.at[chunk], sems.at[2 * bx + 1]).start()
    load_step = pltpu.make_async_copy(step_ref, step, sems.at[8])
    load_reorder = pltpu.make_async_copy(reorder_ref, reorder, sems.at[9])
    load_step.start()
    load_reorder.start()

    for p in range(PLANES):
        for i in range(SPAN_X):
            noise[p, i * SLOTS * 8 : (i * SLOTS + 14) * 8, :] = jnp.zeros((112, 128), F32)

    def place_block(bx, by):
        block = bx * N_GY + by
        for a, half in ((core, own_half), (1 - core, other_half)):
            planes = [half[block * N_GZ + s, 0:16, :].astype(F32) for s in range(N_GZ)]
            zs = [half[block * N_GZ + s, 16:24, :].astype(F32) for s in range(N_GZ)]
            for b in range(BY):
                start = ((bx * BX + a) * SLOTS + by * BY + b + 14) * 8
                start = pl.multiple_of(start, 8)
                for p in range(4):
                    noise[p, pl.ds(start, 8), :] = planes[p][b * 8 : (b + 1) * 8]
                for pair in range(2):
                    first, second = zs[2 * pair], zs[2 * pair + 1]
                    if b == 0:
                        second = pltpu.roll(second, 64, 1)
                    else:
                        first = pltpu.roll(first, 64, 1)
                    noise[4 + pair, pl.ds(start, 8), :] = jnp.where(low8, first, second)

    for bx in range(N_GX):
        chunk = pl.ds(bx * count, count)
        pltpu.make_async_copy(own_ref.at[chunk], own_half.at[chunk], sems.at[2 * bx]).wait()
        pltpu.make_async_copy(other_ref.at[chunk], other_half.at[chunk], sems.at[2 * bx + 1]).wait()

        @pl.loop(0, N_GY)
        def _(by):
            place_block(bx, by)

    state[...] = jnp.zeros_like(state)
    low = iota((64, 128), 1) < 64
    has_below = (iota((64, 128), 0) % 8) != 7
    load_step.wait()

    @pl.loop(0, LEVELS)
    def _(level):
        upstream = []
        for p in range(PLANES):
            here = state[p]
            if p < 4:
                west = jnp.concatenate([jnp.zeros((8, 128), F32), here[:56]], 0)
                value = jnp.where(low, west, here)
            else:
                value = jnp.where(has_below, pltpu.roll(here, 63, 0), 0.0)
            history[p, pl.ds(pl.multiple_of(level * 64, 64), 64), :] = value
            upstream.append(value.astype(BF))
        result = jnp.dot(jnp.concatenate(upstream, 1), step[...], preferred_element_type=F32)
        for p in range(PLANES):
            rows = []
            for i in range(SPAN_X):
                start = (i * SLOTS + level - i + 7) * 8
                rows.append(noise[p, pl.ds(start, 8, stride=9), :])
            state[p] = result[:, p * 128 : (p + 1) * 128] + jnp.concatenate(rows, 0)

    for a in range(BX):
        for b in range(BY):
            for c in range(BZ):
                i = gx * BX + a
                k = gz * BZ + c
                start = (i + k + b) * 64 + i * 8 + 7 - k
                for p in range(PLANES):
                    picked[p, pl.ds((a * BY + b) * BZ + c, 8, stride=8), :] = history[
                        p, pl.ds(start, 8, stride=128), :
                    ]
    load_reorder.wait()
    values = jnp.concatenate([picked[p].astype(BF) for p in range(PLANES)], 1)
    out[...] = jnp.dot(values, reorder[...], preferred_element_type=F32).astype(BF)


def natural_kernel(place, first, second, third, fourth, spread, out):
    gz = place[3]
    total = jnp.zeros((512, 512), F32)
    for back, part in enumerate((first, second, third, fourth)):
        source = lax.rem(gz + back, N_GZ)
        stacked = jnp.concatenate([part[:, g * 128 : (g + 1) * 128] for g in range(8)], 0)
        total += jnp.dot(stacked, spread[source], preferred_element_type=F32)
    for g in range(8):
        for c in range(2):
            start = (g // 4 * 2 + c) * 1024 + g % 4 * 256
            values = total[g * 64 : (g + 1) * 64, c * 256 : (c + 1) * 256]
            out[:, start : start + 256] = values.astype(BF)


def final_kernel(faces, swap_rows, kriging, noise, out, upstream):
    @pl.when(pl.program_id(0) == 0)
    def _():
        upstream[...] = jnp.dot(swap_rows[...], faces[...], preferred_element_type=F32).astype(BF)

    product = jnp.dot(upstream[...], kriging[...], preferred_element_type=F32)
    out[...] = product + noise[...].astype(F32)


def select_table():
    table = np.full((N_GX, N_GY, N_GZ, 3, FACE_COLS), -1, np.int32)
    for gx in range(N_GX):
        for gy in range(N_GY):
            x, z = gy // 2, (gy % 2) * 2 + gx // 2
            parity = (z + 1) % 2
            for s in range(N_GZ):
                lanes = table[gx, gy, s]
                for j in range(2):
                    start = (z - parity - 2 * j) % 4 // 2 * 32
                    for r in range(8):
                        lanes[0, j * 16 + 8 + r] = start + 8 + r
                        lanes[0, 32 + j * 16 + 8 + r] = start + 16 + r
                        lanes[0, 64 + j * 16 + 8 + r] = start + 24 + r
                for dz in range(4):
                    for dx in range(4):
                        for sc in range(2):
                            sx, sz = (x - dx) % 4, (z - dz) % 4
                            i = ((sz % 2) * 2 + sc) * N_GY + sx * 2 + sz // 2
                            base = 96 + dz * 64 + slot_of(dx) * 16 + sc * 8
                            for r in range(8):
                                column = ORDERS[s, r]
                                if i >= 30:
                                    lanes[0, base + r] = (i - 30) * 32 + r
                                if i % 2 == 1 and column // TILE == 7:
                                    lanes[1, base + r] = 64 + (i // 2) * 4 + column % 4
                                if r < 2:
                                    lanes[2, base + r] = 128 + i * 2 + r
    return table.reshape(-1, 3 * FACE_COLS)


def row_table():
    order = np.zeros((N_GZ, 256), np.int32)
    for gz in range(N_GZ):
        for target in range(256):
            k = 7 - target % 8
            tile = (target // 8 % 4) * 2 + k % 2
            order[gz, target] = ((gz - k // 2) % N_GZ) * 64 + tile * 8 + target // 32
    return order


def spread_table():
    table = np.zeros((N_GZ, 128), np.int32)
    for s in range(N_GZ):
        for n in range(128):
            device, q, core = n // 64, n % 64 // 16 * 8 + n % 8, n % 16 // 8
            table[s, n] = core * 256 + device * COLS_DEV + ORDERS[s, q]
    return table


def own_table():
    swapped = np.concatenate([ORDERS[:, HALF:], ORDERS[:, :HALF]], 1)
    return np.stack([ORDERS, swapped], 1).reshape(-1, PART)


def local(factor, kriging, normals, visit_order):
    gx = lax.axis_index("gx")
    gy = lax.axis_index("gy")
    gz = lax.axis_index("gz")
    place = jnp.stack([gy // 2, (gy % 2) * 2 + gx // 2, gx % 2, gz]).astype(jnp.int32)
    sweep_place = jnp.stack([gx, gy, gx % 2, gz]).astype(jnp.int32)
    vmem = pl.BlockSpec(memory_space=pltpu.VMEM)
    smem = pl.BlockSpec(memory_space=pltpu.SMEM)
    anywhere = pl.BlockSpec(memory_space=pl.ANY)

    core = gx % 2
    own_columns = jnp.asarray(own_table())[gz * 2 + core]
    own = one_hot(iota((PART, COLS_DEV), 1) == own_columns[:, None])
    shard = lax.dot_general(
        own, factor, (((1,), (1,)), ((), ())), preferred_element_type=F32
    ).astype(BF)
    mine = shard[:HALF].reshape(2, 8, CELLS)
    given = plane_shift(shard[HALF:], 0, 0, 1).reshape(2, 8, CELLS)
    is_first = core == 0
    both = jnp.concatenate([jnp.where(is_first, mine, given), jnp.where(is_first, given, mine)], 1)
    line = [both]
    for d in (1, 2, 3):
        line.append(plane_shift(both, d, 0))
    line = jnp.concatenate([line[d] for d in (0, 2, 1, 3)], 1).reshape(8 * HALF, CELLS)

    drawn = normals.reshape(TILES, ENS, CELLS)
    ordered = drawn.at[visit_order.reshape(TILES)].get(mode="promise_in_bounds")
    ordered = ordered.reshape(TILES * ENS, CELLS)
    row_pieces = [ordered]
    for s in (1, 2, 3):
        row_pieces.append(line_shift(ordered, s))

    late, kriging_late, line, spread_places, state_rows = lax.optimization_barrier(
        (gz, kriging, line, jnp.asarray(spread_table()), jnp.asarray(STATE_ROWS))
    )
    lane = iota((FACE_COLS, 256), 1)
    device = (gx * N_GY + gy) * N_GZ + late
    lanes = jnp.asarray(select_table())[device].reshape(3, FACE_COLS, 1)
    select = one_hot(
        (lane == lanes[0]) | (lane == lanes[1]) | (lane == lanes[2])
        | ((lane - 64 == lanes[2]) & (lane >= 192))
    )
    row_order = one_hot(iota((256, 256), 1) == jnp.asarray(row_table())[late][:, None])
    spread = one_hot(iota((N_GZ, 128, 512), 2) == spread_places[:, :, None])
    reorder = one_hot(state_rows[:, None] == iota((STATE, STATE), 1))
    swap_rows = one_hot(
        iota((64, 64), 1) == jnp.asarray([(r % 8) * 8 + r // 8 for r in range(64)])[:, None]
    )
    to_state = one_hot(iota((CELLS, STATE), 0) == jnp.asarray(STATE_CELLS)[None, :])
    step = to_bf16_dot(reorder, to_bf16_dot(kriging_late, to_state))

    held = [line]
    for d in (1, 2, 3):
        held.append(plane_shift(line, 0, d))
    held[1], select, row_order, spread, step, reorder, place = lax.optimization_barrier(
        (held[1], select, row_order, spread, step, reorder, place)
    )
    pieces = held + [plane_shift(line, 0, 0, 1)]
    pieces += [plane_shift(piece, 0, 0, 1) for piece in held[1:]]

    copies = pl.pallas_call(
        face_kernel,
        out_shape=jax.ShapeDtypeStruct((N_GX // 2, BX, ENS, N_GZ, 24, 128), BF),
        in_specs=[smem, vmem, vmem] + [anywhere] * 12,
        out_specs=anywhere,
        scratch_shapes=[
            pltpu.VMEM((N_GZ, 64, CELLS), BF),
            pltpu.VMEM((FACE_COLS, CELLS), BF),
            pltpu.VMEM((BX, ENS, 24, 128), BF),
            pltpu.SemaphoreType.DMA,
            pltpu.SemaphoreType.DMA,
            pltpu.SemaphoreType.DMA((N_GX // 2 * N_GZ,)),
        ],
        name="face_part",
    )(place, select, row_order, *row_pieces, *pieces)

    place, copies = lax.optimization_barrier((place, copies))
    noise_part = pl.pallas_call(
        noise_kernel,
        out_shape=jax.ShapeDtypeStruct((N_GZ * 64, N_GX * N_GY * PART), BF),
        in_specs=[smem] + [anywhere] * 12,
        out_specs=vmem,
        scratch_shapes=[
            pltpu.VMEM((N_GZ, 64, CELLS), BF),
            pltpu.VMEM((2, 32, 16, CELLS), BF),
            pltpu.VMEM((256, 512), F32),
            pltpu.SemaphoreType.DMA,
            pltpu.SemaphoreType.DMA((2,)),
        ],
        name="noise_part",
    )(place, *row_pieces, *pieces)

    received = lax.all_to_all(copies.reshape(128, 24, 128), ("gx", "gy", "gz"), 0, 0, tiled=True)
    parts = [noise_part[back * 64 : (back + 1) * 64] for back in range(N_GZ)]
    received, *parts = lax.optimization_barrier((received, *parts))
    home = [parts[0]] + [line_shift(parts[back], -back) for back in (1, 2, 3)]
    other_half = plane_shift(received, 0, 0, 1)

    chosen = pl.pallas_call(
        sweep_kernel,
        out_shape=jax.ShapeDtypeStruct((64, STATE), BF),
        in_specs=[smem] + [anywhere] * 4,
        out_specs=vmem,
        scratch_shapes=[
            pltpu.VMEM((PLANES, SPAN_X * SLOTS * 8, 128), F32),
            pltpu.VMEM((PLANES, LEVELS * 64, 128), F32),
            pltpu.VMEM((PLANES, 64, 128), F32),
            pltpu.VMEM((PLANES, 64, 128), F32),
            pltpu.VMEM((128, 24, 128), BF),
            pltpu.VMEM((128, 24, 128), BF),
            pltpu.VMEM((STATE, STATE), BF),
            pltpu.VMEM((STATE, STATE), BF),
            pltpu.SemaphoreType.DMA((10,)),
        ],
        name="sweep",
    )(sweep_place, received, other_half, step, reorder)

    upstream = lax.all_to_all(
        chosen.reshape(N_GY, TILES, STATE), "gy", 0, 0, tiled=True
    ).reshape(ENS * TILES, STATE)

    natural = pl.pallas_call(
        natural_kernel,
        out_shape=jax.ShapeDtypeStruct((TILES * ENS, CELLS), BF),
        in_specs=[smem] + [vmem] * 5,
        out_specs=vmem,
        name="natural",
    )(sweep_place, *home, spread)

    width = 1024
    out = pl.pallas_call(
        final_kernel,
        grid=(CELLS // width,),
        out_shape=jax.ShapeDtypeStruct((TILES * ENS, CELLS), F32),
        in_specs=[
            pl.BlockSpec((64, STATE), lambda g: (0, 0)),
            pl.BlockSpec((64, 64), lambda g: (0, 0)),
            pl.BlockSpec((STATE, width), lambda g: (0, g)),
            pl.BlockSpec((64, width), lambda g: (0, g)),
        ],
        out_specs=pl.BlockSpec((64, width), lambda g: (0, g)),
        scratch_shapes=[pltpu.VMEM((64, STATE), BF)],
        name="evolve",
    )(upstream, swap_rows, kriging, natural)
    return out.reshape(BX, BY, BZ, ENS, CELLS)


def solution(mesh):
    placed = (
        P(None, ("gx", "gy")),
        P(),
        P("gx", "gy", "gz", None, None, None),
        P("gx", "gy", "gz", None),
    )

    return jax.shard_map(
        local,
        mesh=mesh,
        in_specs=placed,
        out_specs=P("gx", "gy", "gz", None, None),
        check_vma=False,
    )
```

```python
import functools

import jax
import jax.numpy as jnp
import numpy as np
from jax import lax
from jax.experimental import pallas as pl
from jax.experimental.pallas import tpu as pltpu
from jax.sharding import PartitionSpec as P


TILE = 16
CELLS = 4096
FACE = 256
BX = 2
BY = 2
BZ = 2
TILES = 8
ENS = 8
N_GX = 4
N_GY = 8
N_GZ = 4
SPAN_X = N_GX * BX
SPAN_Y = N_GY * BY
SPAN_Z = N_GZ * BZ
LEVELS = SPAN_X + SPAN_Y + SPAN_Z - 2
COLS_DEV = CELLS // (N_GX * N_GY)
PART = COLS_DEV // N_GZ
HALF = PART // 2
STATE = 3 * FACE
PLANES = STATE // 128
FACE_COLS = 352
SLOTS = SPAN_Y + SPAN_X - 1 + SPAN_Z - 1 + 14

BF = jnp.bfloat16
F32 = jnp.float32


def column_orders():
    orders = []
    for s in range(N_GZ):
        z_cells = [(4 * e + (s + 1) % 4) * TILE + TILE - 1 for e in range(2)]
        y_cells = [7 * TILE + 4 * ((s - 15) % 4) + m for m in range(4)]
        first = z_cells + [c for c in y_cells if c not in z_cells]
        part = [c for c in range(COLS_DEV) if (c // TILE + c % TILE // 4) % 4 == s]
        orders.append(first + [c for c in part if c not in first])
    return np.array(orders, np.int32)


ORDERS = column_orders()


def state_order():
    rows = np.zeros(STATE, np.int32)
    cells = np.zeros(STATE, np.int32)
    for f in range(STATE):
        plane, lane = divmod(f, 128)
        if plane < 4:
            s, slot = plane, lane % 64
            if lane < 64:
                i, q = 30 + slot // 32, slot % 32
                v, w = 8 * (i % 2) + ORDERS[s, q] // TILE, ORDERS[s, q] % TILE
                rows[f], cells[f] = v * 16 + w, (15 * 16 + v) * 16 + w
            else:
                u, w = slot // 4, 4 * ((s - 15) % 4) + slot % 4
                rows[f], cells[f] = FACE + u * 16 + w, (u * 16 + 15) * 16 + w
        else:
            s, slot = 2 * (plane - 4) + lane // 64, lane % 64
            i, e = slot // 2, slot % 2
            u, v = i // 2, 8 * (i % 2) + 4 * e + (s + 1) % 4
            rows[f], cells[f] = 2 * FACE + u * 16 + v, (u * 16 + v) * 16 + 15
    return rows, cells


STATE_ROWS, STATE_CELLS = state_order()


def one_hot(condition):
    return condition.astype(BF)


def iota(shape, axis):
    return lax.broadcasted_iota(jnp.int32, shape, axis)


def to_bf16_dot(left, right):
    return jnp.dot(left, right, preferred_element_type=F32).astype(BF)


def plane_shift(value, dx, dz, swap=0):
    pairs = []
    for gx in range(N_GX):
        for gy in range(N_GY):
            x, z, core = gy // 2, (gy % 2) * 2 + gx // 2, gx % 2
            move_x, move_z = (dx, dz) if core == 0 else (dz, dx)
            x, z, core = (x + move_x) % 4, (z + move_z) % 4, core ^ swap
            pairs.append((gx * N_GY + gy, ((z % 2) * 2 + core) * N_GY + x * 2 + z // 2))
    return lax.ppermute(value, ("gx", "gy"), pairs)


def line_shift(value, steps):
    return lax.ppermute(value, "gz", [(s, (s + steps) % N_GZ) for s in range(N_GZ)])


def slot_of(d):
    return d % 2 * 2 + d // 2


def by_core(core, refs, body):
    own, other = refs[:4], refs[4:]

    @pl.when(core == 0)
    def _():
        body(own, other)

    @pl.when(core == 1)
    def _():
        body(other, own)


def noise_kernel(place, *refs):
    row_refs = refs[:4]
    piece_refs = refs[4:12]
    noise_out = refs[12]
    rows, factors, acc, sem_rows, sem_factor = refs[13:]
    x, z, core = place[0], place[1], place[2]
    for back in range(N_GZ):
        pltpu.make_async_copy(row_refs[back], rows.at[back], sem_rows).start()

    def load_all(first_refs, second_refs):
        for parity in range(2):
            group = lax.rem(z + parity, 2)
            for dz in (parity, parity + 2):
                high = lax.rem(z - dz + 4, 4) // 2
                for dx in range(4):
                    target = (lax.rem(x - dx + 4, 4) * 2 + high) * 4
                    for t in range(2):
                        for ref, slot, kind in (
                            (first_refs[dz], slot_of(dx), 0),
                            (second_refs[dx], slot_of(dz), 2),
                        ):
                            pltpu.make_async_copy(
                                ref.at[pl.ds(t * 64 + slot * 16, 16)],
                                factors.at[group, target + kind + t],
                                sem_factor.at[parity],
                            ).start()

    by_core(core, piece_refs, load_all)
    pltpu.make_async_copy(rows, rows, sem_rows).wait()
    wide = 512
    for parity in range(2):
        group = lax.rem(z + parity, 2)
        block = factors.at[group]
        pltpu.make_async_copy(block, block, sem_factor.at[parity]).wait()
        acc[...] = jnp.zeros_like(acc)

        @pl.loop(0, 2 * group + 2)
        def _(chunk):
            span = pl.ds(pl.multiple_of(chunk * 1024, 1024), 1024)
            acc[...] += lax.dot_general(
                rows[:, :, span].reshape(N_GZ * 64, 1024),
                factors[group, :, :, span].reshape(wide, 1024),
                (((1,), (1,)), ((), ())),
                preferred_element_type=F32,
            )

        noise_out[:, pl.ds(pl.multiple_of(group * wide, wide), wide)] = acc[...].astype(BF)


def face_kernel(place, select, row_order, *refs):
    row_refs = refs[:4]
    piece_refs = refs[4:12]
    copies_out = refs[12]
    rows, factors, face_out, sem_rows, sem_factor, sem_out = refs[13:]
    x, z, core = place[0], place[1], place[2]
    odd = lax.rem(z + 1, 2)
    holder = lax.rem(x + 1, 4)

    def load(chunk, ref, start, target, count):
        span = pl.ds(chunk * 1024, 1024)
        pltpu.make_async_copy(
            ref.at[pl.ds(start, count), span],
            factors.at[chunk, pl.ds(target, count)],
            sem_factor.at[chunk],
        ).start()

    def load_rows(chunk):
        for back in range(N_GZ):
            pltpu.make_async_copy(
                row_refs[back].at[:, pl.ds(chunk * 1024, 1024)],
                rows.at[chunk, back],
                sem_rows.at[chunk],
            ).start()

    def load_all(first_refs, second_refs):
        for chunk in range(4):
            load_rows(chunk)
            load_chunk(functools.partial(load, chunk), first_refs, second_refs)

    def load_chunk(load, first_refs, second_refs):
        for dz in range(4):
            load(first_refs[dz], 0, 96 + dz * 64, 64)
        held = pl.multiple_of(64 + slot_of(holder) * 16, 16)
        part = pl.multiple_of(odd * 32, 32)
        for parity in range(2):

            @pl.when(odd == parity)
            def _():
                load(first_refs[parity], held, 0, 16)
                load(first_refs[parity + 2], held, 16, 16)

        for dx in range(4):

            @pl.when(holder == dx)
            def _():
                load(second_refs[dx], part, 32, 32)
                load(second_refs[dx], part + 64, 64, 32)

    by_core(core, piece_refs, load_all)
    product = jnp.zeros((N_GZ * 64, FACE_COLS), F32)
    for chunk in range(4):
        row_block, factor_block = rows.at[chunk], factors.at[chunk]
        pltpu.make_async_copy(row_block, row_block, sem_rows.at[chunk]).wait()
        pltpu.make_async_copy(factor_block, factor_block, sem_factor.at[chunk]).wait()
        product += lax.dot_general(
            rows[chunk].reshape(N_GZ * 64, 1024),
            factors[chunk],
            (((1,), (1,)), ((), ())),
            preferred_element_type=F32,
        )
    product = product.astype(BF)
    sums = jnp.dot(product, select[...], preferred_element_type=F32).astype(BF)
    faces = jnp.dot(row_order[...], sums, preferred_element_type=F32)
    low = iota((8, 128), 1) < 64
    for r in range(ENS):
        for a in range(BX):
            base = r * 32 + a * 16
            face_out[a, r, 0:16, :] = faces[base : base + 16, :128].astype(BF)
            first = faces[base : base + 8, 128:]
            second = faces[base + 8 : base + 16, 128:]
            face_out[a, r, 16:24, :] = jnp.where(low, first, second).astype(BF)
    copies = [
        pltpu.make_async_copy(face_out, copies_out.at[side, :, :, k], sem_out.at[side * N_GZ + k])
        for side in range(N_GX // 2)
        for k in range(N_GZ)
    ]
    for copy in copies:
        copy.start()
    for copy in copies:
        copy.wait()


def sweep_kernel(place, own_ref, other_ref, step_ref, reorder_ref, out, *scratch):
    noise, history, state, picked, own_half, other_half, step, reorder, sems = scratch
    gx, core, gz = place[0], place[2], place[3]
    low8 = iota((8, 128), 1) < 64
    count = N_GY * N_GZ
    for bx in range(N_GX):
        chunk = pl.ds(bx * count, count)
        pltpu.make_async_copy(own_ref.at[chunk], own_half.at[chunk], sems.at[2 * bx]).start()
        pltpu.make_async_copy(other_ref.at[chunk], other_half.at[chunk], sems.at[2 * bx + 1]).start()
    load_step = pltpu.make_async_copy(step_ref, step, sems.at[8])
    load_reorder = pltpu.make_async_copy(reorder_ref, reorder, sems.at[9])
    load_step.start()
    load_reorder.start()

    for p in range(PLANES):
        for i in range(SPAN_X):
            noise[p, i * SLOTS * 8 : (i * SLOTS + 14) * 8, :] = jnp.zeros((112, 128), F32)

    def place_block(bx, by):
        block = bx * N_GY + by
        for a, half in ((core, own_half), (1 - core, other_half)):
            planes = [half[block * N_GZ + s, 0:16, :].astype(F32) for s in range(N_GZ)]
            zs = [half[block * N_GZ + s, 16:24, :].astype(F32) for s in range(N_GZ)]
            for b in range(BY):
                start = ((bx * BX + a) * SLOTS + by * BY + b + 14) * 8
                start = pl.multiple_of(start, 8)
                for p in range(4):
                    noise[p, pl.ds(start, 8), :] = planes[p][b * 8 : (b + 1) * 8]
                for pair in range(2):
                    first, second = zs[2 * pair], zs[2 * pair + 1]
                    if b == 0:
                        second = pltpu.roll(second, 64, 1)
                    else:
                        first = pltpu.roll(first, 64, 1)
                    noise[4 + pair, pl.ds(start, 8), :] = jnp.where(low8, first, second)

    for bx in range(N_GX):
        chunk = pl.ds(bx * count, count)
        pltpu.make_async_copy(own_ref.at[chunk], own_half.at[chunk], sems.at[2 * bx]).wait()
        pltpu.make_async_copy(other_ref.at[chunk], other_half.at[chunk], sems.at[2 * bx + 1]).wait()

        @pl.loop(0, N_GY)
        def _(by):
            place_block(bx, by)

    state[...] = jnp.zeros_like(state)
    low = iota((64, 128), 1) < 64
    has_below = (iota((64, 128), 0) % 8) != 7
    load_step.wait()

    @pl.loop(0, LEVELS)
    def _(level):
        upstream = []
        for p in range(PLANES):
            here = state[p]
            if p < 4:
                west = jnp.concatenate([jnp.zeros((8, 128), F32), here[:56]], 0)
                value = jnp.where(low, west, here)
            else:
                value = jnp.where(has_below, pltpu.roll(here, 63, 0), 0.0)
            history[p, pl.ds(pl.multiple_of(level * 64, 64), 64), :] = value
            upstream.append(value.astype(BF))
        result = jnp.dot(jnp.concatenate(upstream, 1), step[...], preferred_element_type=F32)
        for p in range(PLANES):
            rows = []
            for i in range(SPAN_X):
                start = (i * SLOTS + level - i + 7) * 8
                rows.append(noise[p, pl.ds(start, 8, stride=9), :])
            state[p] = result[:, p * 128 : (p + 1) * 128] + jnp.concatenate(rows, 0)

    for a in range(BX):
        for b in range(BY):
            for c in range(BZ):
                i = gx * BX + a
                k = gz * BZ + c
                start = (i + k + b) * 64 + i * 8 + 7 - k
                for p in range(PLANES):
                    picked[p, pl.ds((a * BY + b) * BZ + c, 8, stride=8), :] = history[
                        p, pl.ds(start, 8, stride=128), :
                    ]
    load_reorder.wait()
    values = jnp.concatenate([picked[p].astype(BF) for p in range(PLANES)], 1)
    out[...] = jnp.dot(values, reorder[...], preferred_element_type=F32).astype(BF)


def natural_kernel(place, first, second, third, fourth, spread, out):
    gz = place[3]
    total = jnp.zeros((512, 512), F32)
    for back, part in enumerate((first, second, third, fourth)):
        source = lax.rem(gz + back, N_GZ)
        stacked = jnp.concatenate([part[:, g * 128 : (g + 1) * 128] for g in range(8)], 0)
        total += jnp.dot(stacked, spread[source], preferred_element_type=F32)
    for g in range(8):
        for c in range(2):
            start = (g // 4 * 2 + c) * 1024 + g % 4 * 256
            values = total[g * 64 : (g + 1) * 64, c * 256 : (c + 1) * 256]
            out[:, start : start + 256] = values.astype(BF)


def final_kernel(faces, swap_rows, kriging, noise, out, upstream):
    @pl.when(pl.program_id(0) == 0)
    def _():
        upstream[...] = jnp.dot(swap_rows[...], faces[...], preferred_element_type=F32).astype(BF)

    product = jnp.dot(upstream[...], kriging[...], preferred_element_type=F32)
    out[...] = product + noise[...].astype(F32)


def select_table():
    table = np.full((N_GX, N_GY, N_GZ, 3, FACE_COLS), -1, np.int32)
    for gx in range(N_GX):
        for gy in range(N_GY):
            x, z = gy // 2, (gy % 2) * 2 + gx // 2
            parity = (z + 1) % 2
            for s in range(N_GZ):
                lanes = table[gx, gy, s]
                for j in range(2):
                    start = (z - parity - 2 * j) % 4 // 2 * 32
                    for r in range(8):
                        lanes[0, j * 16 + 8 + r] = start + 8 + r
                        lanes[0, 32 + j * 16 + 8 + r] = start + 16 + r
                        lanes[0, 64 + j * 16 + 8 + r] = start + 24 + r
                for dz in range(4):
                    for dx in range(4):
                        for sc in range(2):
                            sx, sz = (x - dx) % 4, (z - dz) % 4
                            i = ((sz % 2) * 2 + sc) * N_GY + sx * 2 + sz // 2
                            base = 96 + dz * 64 + slot_of(dx) * 16 + sc * 8
                            for r in range(8):
                                column = ORDERS[s, r]
                                if i >= 30:
                                    lanes[0, base + r] = (i - 30) * 32 + r
                                if i % 2 == 1 and column // TILE == 7:
                                    lanes[1, base + r] = 64 + (i // 2) * 4 + column % 4
                                if r < 2:
                                    lanes[2, base + r] = 128 + i * 2 + r
    return table.reshape(-1, 3 * FACE_COLS)


def row_table():
    order = np.zeros((N_GZ, 256), np.int32)
    for gz in range(N_GZ):
        for target in range(256):
            k = 7 - target % 8
            tile = (target // 8 % 4) * 2 + k % 2
            order[gz, target] = ((gz - k // 2) % N_GZ) * 64 + tile * 8 + target // 32
    return order


def spread_table():
    table = np.zeros((N_GZ, 128), np.int32)
    for s in range(N_GZ):
        for n in range(128):
            device, q, core = n // 64, n % 64 // 16 * 8 + n % 8, n % 16 // 8
            table[s, n] = core * 256 + device * COLS_DEV + ORDERS[s, q]
    return table


def own_table():
    swapped = np.concatenate([ORDERS[:, HALF:], ORDERS[:, :HALF]], 1)
    return np.stack([ORDERS, swapped], 1).reshape(-1, PART)


def local(factor, kriging, normals, visit_order):
    gx = lax.axis_index("gx")
    gy = lax.axis_index("gy")
    gz = lax.axis_index("gz")
    place = jnp.stack([gy // 2, (gy % 2) * 2 + gx // 2, gx % 2, gz]).astype(jnp.int32)
    sweep_place = jnp.stack([gx, gy, gx % 2, gz]).astype(jnp.int32)
    vmem = pl.BlockSpec(memory_space=pltpu.VMEM)
    smem = pl.BlockSpec(memory_space=pltpu.SMEM)
    anywhere = pl.BlockSpec(memory_space=pl.ANY)

    core = gx % 2
    own_columns = jnp.asarray(own_table())[gz * 2 + core]
    own = one_hot(iota((PART, COLS_DEV), 1) == own_columns[:, None])
    shard = lax.dot_general(
        own, factor, (((1,), (1,)), ((), ())), preferred_element_type=F32
    ).astype(BF)
    mine = shard[:HALF].reshape(2, 8, CELLS)
    given = plane_shift(shard[HALF:], 0, 0, 1).reshape(2, 8, CELLS)
    is_first = core == 0
    both = jnp.concatenate([jnp.where(is_first, mine, given), jnp.where(is_first, given, mine)], 1)
    line = [both]
    for d in (1, 2, 3):
        line.append(plane_shift(both, d, 0))
    line = jnp.concatenate([line[d] for d in (0, 2, 1, 3)], 1).reshape(8 * HALF, CELLS)

    drawn = normals.reshape(TILES, ENS, CELLS)
    ordered = drawn.at[visit_order.reshape(TILES)].get(mode="promise_in_bounds")
    ordered = ordered.reshape(TILES * ENS, CELLS)
    row_pieces = [ordered]
    for s in (1, 2, 3):
        row_pieces.append(line_shift(ordered, s))

    late, kriging_late, line, spread_places, state_rows = lax.optimization_barrier(
        (gz, kriging, line, jnp.asarray(spread_table()), jnp.asarray(STATE_ROWS))
    )
    lane = iota((FACE_COLS, 256), 1)
    device = (gx * N_GY + gy) * N_GZ + late
    lanes = jnp.asarray(select_table())[device].reshape(3, FACE_COLS, 1)
    select = one_hot(
        (lane == lanes[0]) | (lane == lanes[1]) | (lane == lanes[2])
        | ((lane - 64 == lanes[2]) & (lane >= 192))
    )
    row_order = one_hot(iota((256, 256), 1) == jnp.asarray(row_table())[late][:, None])
    spread = one_hot(iota((N_GZ, 128, 512), 2) == spread_places[:, :, None])
    reorder = one_hot(state_rows[:, None] == iota((STATE, STATE), 1))
    swap_rows = one_hot(
        iota((64, 64), 1) == jnp.asarray([(r % 8) * 8 + r // 8 for r in range(64)])[:, None]
    )
    to_state = one_hot(iota((CELLS, STATE), 0) == jnp.asarray(STATE_CELLS)[None, :])
    step = to_bf16_dot(reorder, to_bf16_dot(kriging_late, to_state))

    held = [line]
    for d in (1, 2, 3):
        held.append(plane_shift(line, 0, d))
    held[1], select, row_order, spread, step, reorder, place = lax.optimization_barrier(
        (held[1], select, row_order, spread, step, reorder, place)
    )
    pieces = held + [plane_shift(line, 0, 0, 1)]
    pieces += [plane_shift(piece, 0, 0, 1) for piece in held[1:]]

    copies = pl.pallas_call(
        face_kernel,
        out_shape=jax.ShapeDtypeStruct((N_GX // 2, BX, ENS, N_GZ, 24, 128), BF),
        in_specs=[smem, vmem, vmem] + [anywhere] * 12,
        out_specs=anywhere,
        scratch_shapes=[
            pltpu.VMEM((4, N_GZ, 64, 1024), BF),
            pltpu.VMEM((4, FACE_COLS, 1024), BF),
            pltpu.VMEM((BX, ENS, 24, 128), BF),
            pltpu.SemaphoreType.DMA((4,)),
            pltpu.SemaphoreType.DMA((4,)),
            pltpu.SemaphoreType.DMA((N_GX // 2 * N_GZ,)),
        ],
        compiler_params=pltpu.CompilerParams(vmem_limit_bytes=16 << 20),
        name="face_part",
    )(place, select, row_order, *row_pieces, *pieces)

    place, copies = lax.optimization_barrier((place, copies))
    noise_part = pl.pallas_call(
        noise_kernel,
        out_shape=jax.ShapeDtypeStruct((N_GZ * 64, N_GX * N_GY * PART), BF),
        in_specs=[smem] + [anywhere] * 12,
        out_specs=vmem,
        scratch_shapes=[
            pltpu.VMEM((N_GZ, 64, CELLS), BF),
            pltpu.VMEM((2, 32, 16, CELLS), BF),
            pltpu.VMEM((256, 512), F32),
            pltpu.SemaphoreType.DMA,
            pltpu.SemaphoreType.DMA((2,)),
        ],
        name="noise_part",
    )(place, *row_pieces, *pieces)

    received = lax.all_to_all(copies.reshape(128, 24, 128), ("gx", "gy", "gz"), 0, 0, tiled=True)
    parts = [noise_part[back * 64 : (back + 1) * 64] for back in range(N_GZ)]
    received, *parts = lax.optimization_barrier((received, *parts))
    home = [parts[0]] + [line_shift(parts[back], -back) for back in (1, 2, 3)]
    other_half = plane_shift(received, 0, 0, 1)

    chosen = pl.pallas_call(
        sweep_kernel,
        out_shape=jax.ShapeDtypeStruct((64, STATE), BF),
        in_specs=[smem] + [anywhere] * 4,
        out_specs=vmem,
        scratch_shapes=[
            pltpu.VMEM((PLANES, SPAN_X * SLOTS * 8, 128), F32),
            pltpu.VMEM((PLANES, LEVELS * 64, 128), F32),
            pltpu.VMEM((PLANES, 64, 128), F32),
            pltpu.VMEM((PLANES, 64, 128), F32),
            pltpu.VMEM((128, 24, 128), BF),
            pltpu.VMEM((128, 24, 128), BF),
            pltpu.VMEM((STATE, STATE), BF),
            pltpu.VMEM((STATE, STATE), BF),
            pltpu.SemaphoreType.DMA((10,)),
        ],
        name="sweep",
    )(sweep_place, received, other_half, step, reorder)

    upstream = lax.all_to_all(
        chosen.reshape(N_GY, TILES, STATE), "gy", 0, 0, tiled=True
    ).reshape(ENS * TILES, STATE)

    natural = pl.pallas_call(
        natural_kernel,
        out_shape=jax.ShapeDtypeStruct((TILES * ENS, CELLS), BF),
        in_specs=[smem] + [vmem] * 5,
        out_specs=vmem,
        name="natural",
    )(sweep_place, *home, spread)

    width = 1024
    out = pl.pallas_call(
        final_kernel,
        grid=(CELLS // width,),
        out_shape=jax.ShapeDtypeStruct((TILES * ENS, CELLS), F32),
        in_specs=[
            pl.BlockSpec((64, STATE), lambda g: (0, 0)),
            pl.BlockSpec((64, 64), lambda g: (0, 0)),
            pl.BlockSpec((STATE, width), lambda g: (0, g)),
            pl.BlockSpec((64, width), lambda g: (0, g)),
        ],
        out_specs=pl.BlockSpec((64, width), lambda g: (0, g)),
        scratch_shapes=[pltpu.VMEM((64, STATE), BF)],
        name="evolve",
    )(upstream, swap_rows, kriging, natural)
    return out.reshape(BX, BY, BZ, ENS, CELLS)


def solution(mesh):
    placed = (
        P(None, ("gx", "gy")),
        P(),
        P("gx", "gy", "gz", None, None, None),
        P("gx", "gy", "gz", None),
    )

    return jax.shard_map(
        local,
        mesh=mesh,
        in_specs=placed,
        out_specs=P("gx", "gy", "gz", None, None),
        check_vma=False,
    )
```

```python
import functools

import jax
import jax.numpy as jnp
import numpy as np
from jax import lax
from jax.experimental import pallas as pl
from jax.experimental.pallas import tpu as pltpu
from jax.sharding import PartitionSpec as P


TILE = 16
CELLS = 4096
FACE = 256
BX = 2
BY = 2
BZ = 2
TILES = 8
ENS = 8
N_GX = 4
N_GY = 8
N_GZ = 4
SPAN_X = N_GX * BX
SPAN_Y = N_GY * BY
SPAN_Z = N_GZ * BZ
LEVELS = SPAN_X + SPAN_Y + SPAN_Z - 2
COLS_DEV = CELLS // (N_GX * N_GY)
PART = COLS_DEV // N_GZ
HALF = PART // 2
STATE = 3 * FACE
PLANES = STATE // 128
FACE_COLS = 352
SLOTS = SPAN_Y + SPAN_X - 1 + SPAN_Z - 1 + 14

BF = jnp.bfloat16
F32 = jnp.float32


def column_orders():
    orders = []
    for s in range(N_GZ):
        z_cells = [(4 * e + (s + 1) % 4) * TILE + TILE - 1 for e in range(2)]
        y_cells = [7 * TILE + 4 * ((s - 15) % 4) + m for m in range(4)]
        first = z_cells + [c for c in y_cells if c not in z_cells]
        part = [c for c in range(COLS_DEV) if (c // TILE + c % TILE // 4) % 4 == s]
        orders.append(first + [c for c in part if c not in first])
    return np.array(orders, np.int32)


ORDERS = column_orders()


def state_order():
    rows = np.zeros(STATE, np.int32)
    cells = np.zeros(STATE, np.int32)
    for f in range(STATE):
        plane, lane = divmod(f, 128)
        if plane < 4:
            s, slot = plane, lane % 64
            if lane < 64:
                i, q = 30 + slot // 32, slot % 32
                v, w = 8 * (i % 2) + ORDERS[s, q] // TILE, ORDERS[s, q] % TILE
                rows[f], cells[f] = v * 16 + w, (15 * 16 + v) * 16 + w
            else:
                u, w = slot // 4, 4 * ((s - 15) % 4) + slot % 4
                rows[f], cells[f] = FACE + u * 16 + w, (u * 16 + 15) * 16 + w
        else:
            s, slot = 2 * (plane - 4) + lane // 64, lane % 64
            i, e = slot // 2, slot % 2
            u, v = i // 2, 8 * (i % 2) + 4 * e + (s + 1) % 4
            rows[f], cells[f] = 2 * FACE + u * 16 + v, (u * 16 + v) * 16 + 15
    return rows, cells


STATE_ROWS, STATE_CELLS = state_order()


def one_hot(condition):
    return condition.astype(BF)


def iota(shape, axis):
    return lax.broadcasted_iota(jnp.int32, shape, axis)


def to_bf16_dot(left, right):
    return jnp.dot(left, right, preferred_element_type=F32).astype(BF)


def plane_shift(value, dx, dz, swap=0):
    pairs = []
    for gx in range(N_GX):
        for gy in range(N_GY):
            x, z, core = gy // 2, (gy % 2) * 2 + gx // 2, gx % 2
            move_x, move_z = (dx, dz) if core == 0 else (dz, dx)
            x, z, core = (x + move_x) % 4, (z + move_z) % 4, core ^ swap
            pairs.append((gx * N_GY + gy, ((z % 2) * 2 + core) * N_GY + x * 2 + z // 2))
    return lax.ppermute(value, ("gx", "gy"), pairs)


def line_shift(value, steps):
    return lax.ppermute(value, "gz", [(s, (s + steps) % N_GZ) for s in range(N_GZ)])


def slot_of(d):
    return d % 2 * 2 + d // 2


def by_core(core, refs, body):
    own, other = refs[:4], refs[4:]

    @pl.when(core == 0)
    def _():
        body(own, other)

    @pl.when(core == 1)
    def _():
        body(other, own)


def noise_kernel(place, *refs):
    row_refs = refs[:4]
    piece_refs = refs[4:12]
    noise_out = refs[12]
    rows, factors, acc, sem_rows, sem_factor = refs[13:]
    x, z, core = place[0], place[1], place[2]
    for back in range(N_GZ):
        pltpu.make_async_copy(row_refs[back], rows.at[back], sem_rows).start()

    def load_all(first_refs, second_refs):
        for parity in range(2):
            group = lax.rem(z + parity, 2)
            for dz in (parity, parity + 2):
                high = lax.rem(z - dz + 4, 4) // 2
                for dx in range(4):
                    target = (lax.rem(x - dx + 4, 4) * 2 + high) * 4
                    for t in range(2):
                        for ref, slot, kind in (
                            (first_refs[dz], slot_of(dx), 0),
                            (second_refs[dx], slot_of(dz), 2),
                        ):
                            pltpu.make_async_copy(
                                ref.at[pl.ds(t * 64 + slot * 16, 16)],
                                factors.at[group, target + kind + t],
                                sem_factor.at[parity],
                            ).start()

    by_core(core, piece_refs, load_all)
    pltpu.make_async_copy(rows, rows, sem_rows).wait()
    wide = 512
    for parity in range(2):
        group = lax.rem(z + parity, 2)
        block = factors.at[group]
        pltpu.make_async_copy(block, block, sem_factor.at[parity]).wait()
        acc[...] = jnp.zeros_like(acc)

        @pl.loop(0, 2 * group + 2)
        def _(chunk):
            span = pl.ds(pl.multiple_of(chunk * 1024, 1024), 1024)
            acc[...] += lax.dot_general(
                rows[:, :, span].reshape(N_GZ * 64, 1024),
                factors[group, :, :, span].reshape(wide, 1024),
                (((1,), (1,)), ((), ())),
                preferred_element_type=F32,
            )

        noise_out[:, pl.ds(pl.multiple_of(group * wide, wide), wide)] = acc[...].astype(BF)


def face_kernel(place, select, row_order, *refs):
    row_refs = refs[:4]
    piece_refs = refs[4:12]
    copies_out = refs[12]
    rows, factors, face_out, sem_rows, sem_factor, sem_out = refs[13:]
    x, z, core = place[0], place[1], place[2]
    odd = lax.rem(z + 1, 2)
    holder = lax.rem(x + 1, 4)

    def load(chunk, ref, start, target, count):
        span = pl.ds(chunk * 1024, 1024)
        pltpu.make_async_copy(
            ref.at[pl.ds(start, count), span],
            factors.at[chunk, pl.ds(target, count)],
            sem_factor.at[chunk],
        ).start()

    def load_rows(chunk):
        for back in range(N_GZ):
            pltpu.make_async_copy(
                row_refs[back].at[:, pl.ds(chunk * 1024, 1024)],
                rows.at[chunk, back],
                sem_rows.at[chunk],
            ).start()

    def load_all(first_refs, second_refs):
        for chunk in range(4):
            load_rows(chunk)
            load_chunk(functools.partial(load, chunk), first_refs, second_refs)

    def load_chunk(load, first_refs, second_refs):
        for dz in range(4):
            load(first_refs[dz], 0, 96 + dz * 64, 64)
        held = pl.multiple_of(64 + slot_of(holder) * 16, 16)
        part = pl.multiple_of(odd * 32, 32)
        for parity in range(2):

            @pl.when(odd == parity)
            def _():
                load(first_refs[parity], held, 0, 16)
                load(first_refs[parity + 2], held, 16, 16)

        for dx in range(4):

            @pl.when(holder == dx)
            def _():
                load(second_refs[dx], part, 32, 32)
                load(second_refs[dx], part + 64, 64, 32)

    by_core(core, piece_refs, load_all)
    product = jnp.zeros((N_GZ * 64, FACE_COLS), F32)
    for chunk in range(4):
        row_block, factor_block = rows.at[chunk], factors.at[chunk]
        pltpu.make_async_copy(row_block, row_block, sem_rows.at[chunk]).wait()
        pltpu.make_async_copy(factor_block, factor_block, sem_factor.at[chunk]).wait()
        product += lax.dot_general(
            rows[chunk].reshape(N_GZ * 64, 1024),
            factors[chunk],
            (((1,), (1,)), ((), ())),
            preferred_element_type=F32,
        )
    product = product.astype(BF)
    sums = jnp.dot(product, select[...], preferred_element_type=F32).astype(BF)
    faces = jnp.dot(row_order[...], sums, preferred_element_type=F32)
    low = iota((8, 128), 1) < 64
    for r in range(ENS):
        for a in range(BX):
            base = r * 32 + a * 16
            face_out[a, r, 0:16, :] = faces[base : base + 16, :128].astype(BF)
            first = faces[base : base + 8, 128:]
            second = faces[base + 8 : base + 16, 128:]
            face_out[a, r, 16:24, :] = jnp.where(low, first, second).astype(BF)
    copies = [
        pltpu.make_async_copy(face_out, copies_out.at[side, :, :, k], sem_out.at[side * N_GZ + k])
        for side in range(N_GX // 2)
        for k in range(N_GZ)
    ]
    for copy in copies:
        copy.start()
    for copy in copies:
        copy.wait()


def sweep_kernel(place, own_ref, other_ref, step_ref, reorder_ref, out, *scratch):
    noise, history, state, picked, own_half, other_half, step, reorder, sems = scratch
    core, gz = place[2], place[3]
    gx = lax.rem(place[1], 2) * 2 + core
    low8 = iota((8, 128), 1) < 64
    count = N_GY * N_GZ
    for bx in range(N_GX):
        chunk = pl.ds(bx * count, count)
        pltpu.make_async_copy(own_ref.at[chunk], own_half.at[chunk], sems.at[2 * bx]).start()
        pltpu.make_async_copy(other_ref.at[chunk], other_half.at[chunk], sems.at[2 * bx + 1]).start()
    load_step = pltpu.make_async_copy(step_ref, step, sems.at[8])
    load_reorder = pltpu.make_async_copy(reorder_ref, reorder, sems.at[9])
    load_step.start()
    load_reorder.start()

    for p in range(PLANES):
        for i in range(SPAN_X):
            noise[p, i * SLOTS * 8 : (i * SLOTS + 14) * 8, :] = jnp.zeros((112, 128), F32)

    def place_block(bx, by):
        block = bx * N_GY + by
        for a, half in ((core, own_half), (1 - core, other_half)):
            planes = [half[block * N_GZ + s, 0:16, :].astype(F32) for s in range(N_GZ)]
            zs = [half[block * N_GZ + s, 16:24, :].astype(F32) for s in range(N_GZ)]
            for b in range(BY):
                start = ((bx * BX + a) * SLOTS + by * BY + b + 14) * 8
                start = pl.multiple_of(start, 8)
                for p in range(4):
                    noise[p, pl.ds(start, 8), :] = planes[p][b * 8 : (b + 1) * 8]
                for pair in range(2):
                    first, second = zs[2 * pair], zs[2 * pair + 1]
                    if b == 0:
                        second = pltpu.roll(second, 64, 1)
                    else:
                        first = pltpu.roll(first, 64, 1)
                    noise[4 + pair, pl.ds(start, 8), :] = jnp.where(low8, first, second)

    for bx in range(N_GX):
        chunk = pl.ds(bx * count, count)
        pltpu.make_async_copy(own_ref.at[chunk], own_half.at[chunk], sems.at[2 * bx]).wait()
        pltpu.make_async_copy(other_ref.at[chunk], other_half.at[chunk], sems.at[2 * bx + 1]).wait()

        @pl.loop(0, N_GY)
        def _(by):
            place_block(bx, by)

    state[...] = jnp.zeros_like(state)
    low = iota((64, 128), 1) < 64
    has_below = (iota((64, 128), 0) % 8) != 7
    load_step.wait()

    @pl.loop(0, LEVELS)
    def _(level):
        upstream = []
        for p in range(PLANES):
            here = state[p]
            if p < 4:
                west = jnp.concatenate([jnp.zeros((8, 128), F32), here[:56]], 0)
                value = jnp.where(low, west, here)
            else:
                value = jnp.where(has_below, pltpu.roll(here, 63, 0), 0.0)
            history[p, pl.ds(pl.multiple_of(level * 64, 64), 64), :] = value
            upstream.append(value.astype(BF))
        result = jnp.dot(jnp.concatenate(upstream, 1), step[...], preferred_element_type=F32)
        for p in range(PLANES):
            rows = []
            for i in range(SPAN_X):
                start = (i * SLOTS + level - i + 7) * 8
                rows.append(noise[p, pl.ds(start, 8, stride=9), :])
            state[p] = result[:, p * 128 : (p + 1) * 128] + jnp.concatenate(rows, 0)

    for a in range(BX):
        for b in range(BY):
            for c in range(BZ):
                i = gx * BX + a
                k = gz * BZ + c
                start = (i + k + b) * 64 + i * 8 + 7 - k
                for p in range(PLANES):
                    picked[p, pl.ds((a * BY + b) * BZ + c, 8, stride=8), :] = history[
                        p, pl.ds(start, 8, stride=128), :
                    ]
    load_reorder.wait()
    values = jnp.concatenate([picked[p].astype(BF) for p in range(PLANES)], 1)
    out[...] = jnp.dot(values, reorder[...], preferred_element_type=F32).astype(BF)


def natural_kernel(place, first, second, third, fourth, spread, out):
    gz = place[3]
    total = jnp.zeros((512, 512), F32)
    for back, part in enumerate((first, second, third, fourth)):
        source = lax.rem(gz + back, N_GZ)
        stacked = jnp.concatenate([part[:, g * 128 : (g + 1) * 128] for g in range(8)], 0)
        total += jnp.dot(stacked, spread[source], preferred_element_type=F32)
    for g in range(8):
        for c in range(2):
            start = (g // 4 * 2 + c) * 1024 + g % 4 * 256
            values = total[g * 64 : (g + 1) * 64, c * 256 : (c + 1) * 256]
            out[:, start : start + 256] = values.astype(BF)


def final_kernel(faces, swap_rows, kriging, noise, out, upstream):
    @pl.when(pl.program_id(0) == 0)
    def _():
        upstream[...] = jnp.dot(swap_rows[...], faces[...], preferred_element_type=F32).astype(BF)

    product = jnp.dot(upstream[...], kriging[...], preferred_element_type=F32)
    out[...] = product + noise[...].astype(F32)


def select_table():
    table = np.full((N_GX, N_GY, N_GZ, 3, FACE_COLS), -1, np.int32)
    for gx in range(N_GX):
        for gy in range(N_GY):
            x, z = gy // 2, (gy % 2) * 2 + gx // 2
            parity = (z + 1) % 2
            for s in range(N_GZ):
                lanes = table[gx, gy, s]
                for j in range(2):
                    start = (z - parity - 2 * j) % 4 // 2 * 32
                    for r in range(8):
                        lanes[0, j * 16 + 8 + r] = start + 8 + r
                        lanes[0, 32 + j * 16 + 8 + r] = start + 16 + r
                        lanes[0, 64 + j * 16 + 8 + r] = start + 24 + r
                for dz in range(4):
                    for dx in range(4):
                        for sc in range(2):
                            sx, sz = (x - dx) % 4, (z - dz) % 4
                            i = ((sz % 2) * 2 + sc) * N_GY + sx * 2 + sz // 2
                            base = 96 + dz * 64 + slot_of(dx) * 16 + sc * 8
                            for r in range(8):
                                column = ORDERS[s, r]
                                if i >= 30:
                                    lanes[0, base + r] = (i - 30) * 32 + r
                                if i % 2 == 1 and column // TILE == 7:
                                    lanes[1, base + r] = 64 + (i // 2) * 4 + column % 4
                                if r < 2:
                                    lanes[2, base + r] = 128 + i * 2 + r
    return table.reshape(-1, 3 * FACE_COLS)


def row_table():
    order = np.zeros((N_GZ, 256), np.int32)
    for gz in range(N_GZ):
        for target in range(256):
            k = 7 - target % 8
            tile = (target // 8 % 4) * 2 + k % 2
            order[gz, target] = ((gz - k // 2) % N_GZ) * 64 + tile * 8 + target // 32
    return order


def spread_table():
    table = np.zeros((N_GZ, 128), np.int32)
    for s in range(N_GZ):
        for n in range(128):
            device, q, core = n // 64, n % 64 // 16 * 8 + n % 8, n % 16 // 8
            table[s, n] = core * 256 + device * COLS_DEV + ORDERS[s, q]
    return table


def own_table():
    swapped = np.concatenate([ORDERS[:, HALF:], ORDERS[:, :HALF]], 1)
    return np.stack([ORDERS, swapped], 1).reshape(-1, PART)


def local(factor, kriging, normals, visit_order):
    gx = lax.axis_index("gx")
    gy = lax.axis_index("gy")
    gz = lax.axis_index("gz")
    place = jnp.stack([gy // 2, (gy % 2) * 2 + gx // 2, gx % 2, gz]).astype(jnp.int32)
    vmem = pl.BlockSpec(memory_space=pltpu.VMEM)
    smem = pl.BlockSpec(memory_space=pltpu.SMEM)
    anywhere = pl.BlockSpec(memory_space=pl.ANY)

    core = gx % 2
    own_columns = jnp.asarray(own_table())[gz * 2 + core]
    own = one_hot(iota((PART, COLS_DEV), 1) == own_columns[:, None])
    shard = lax.dot_general(
        own, factor, (((1,), (1,)), ((), ())), preferred_element_type=F32
    ).astype(BF)
    mine = shard[:HALF].reshape(2, 8, CELLS)
    given = plane_shift(shard[HALF:], 0, 0, 1).reshape(2, 8, CELLS)
    is_first = core == 0
    both = jnp.concatenate([jnp.where(is_first, mine, given), jnp.where(is_first, given, mine)], 1)
    line = [both]
    for d in (1, 2, 3):
        line.append(plane_shift(both, d, 0))
    line = jnp.concatenate([line[d] for d in (0, 2, 1, 3)], 1).reshape(8 * HALF, CELLS)

    drawn = normals.reshape(TILES, ENS, CELLS)
    ordered = drawn.at[visit_order.reshape(TILES)].get(mode="promise_in_bounds")
    ordered = ordered.reshape(TILES * ENS, CELLS)
    row_pieces = [ordered]
    for s in (1, 2, 3):
        row_pieces.append(line_shift(ordered, s))

    late, kriging_late, line, spread_places, state_rows = lax.optimization_barrier(
        (gz, kriging, line, jnp.asarray(spread_table()), jnp.asarray(STATE_ROWS))
    )
    lane = iota((FACE_COLS, 256), 1)
    device = (gx * N_GY + gy) * N_GZ + late
    lanes = jnp.asarray(select_table())[device].reshape(3, FACE_COLS, 1)
    select = one_hot(
        (lane == lanes[0]) | (lane == lanes[1]) | (lane == lanes[2])
        | ((lane - 64 == lanes[2]) & (lane >= 192))
    )
    row_order = one_hot(iota((256, 256), 1) == jnp.asarray(row_table())[late][:, None])
    spread = one_hot(iota((N_GZ, 128, 512), 2) == spread_places[:, :, None])
    reorder = one_hot(state_rows[:, None] == iota((STATE, STATE), 1))
    swap_rows = one_hot(
        iota((64, 64), 1) == jnp.asarray([(r % 8) * 8 + r // 8 for r in range(64)])[:, None]
    )
    to_state = one_hot(iota((CELLS, STATE), 0) == jnp.asarray(STATE_CELLS)[None, :])
    step = to_bf16_dot(reorder, to_bf16_dot(kriging_late, to_state))

    held = [line]
    for d in (1, 2, 3):
        held.append(plane_shift(line, 0, d))
    held[1], select, row_order, spread, step, reorder, place = lax.optimization_barrier(
        (held[1], select, row_order, spread, step, reorder, place)
    )
    pieces = held + [plane_shift(line, 0, 0, 1)]
    pieces += [plane_shift(piece, 0, 0, 1) for piece in held[1:]]

    copies = pl.pallas_call(
        face_kernel,
        out_shape=jax.ShapeDtypeStruct((N_GX // 2, BX, ENS, N_GZ, 24, 128), BF),
        in_specs=[smem, vmem, vmem] + [anywhere] * 12,
        out_specs=anywhere,
        scratch_shapes=[
            pltpu.VMEM((4, N_GZ, 64, 1024), BF),
            pltpu.VMEM((4, FACE_COLS, 1024), BF),
            pltpu.VMEM((BX, ENS, 24, 128), BF),
            pltpu.SemaphoreType.DMA((4,)),
            pltpu.SemaphoreType.DMA((4,)),
            pltpu.SemaphoreType.DMA((N_GX // 2 * N_GZ,)),
        ],
        compiler_params=pltpu.CompilerParams(vmem_limit_bytes=16 << 20),
        name="face_part",
    )(place, select, row_order, *row_pieces, *pieces)

    place, copies = lax.optimization_barrier((place, copies))
    noise_part = pl.pallas_call(
        noise_kernel,
        out_shape=jax.ShapeDtypeStruct((N_GZ * 64, N_GX * N_GY * PART), BF),
        in_specs=[smem] + [anywhere] * 12,
        out_specs=vmem,
        scratch_shapes=[
            pltpu.VMEM((N_GZ, 64, CELLS), BF),
            pltpu.VMEM((2, 32, 16, CELLS), BF),
            pltpu.VMEM((256, 512), F32),
            pltpu.SemaphoreType.DMA,
            pltpu.SemaphoreType.DMA((2,)),
        ],
        name="noise_part",
    )(place, *row_pieces, *pieces)

    received = lax.all_to_all(copies.reshape(128, 24, 128), ("gx", "gy", "gz"), 0, 0, tiled=True)
    parts = [noise_part[back * 64 : (back + 1) * 64] for back in range(N_GZ)]
    home = [parts[0]]
    for back in (1, 2, 3):
        home.append(line_shift(parts[back], -back))
    other_half = plane_shift(received, 0, 0, 1)

    chosen = pl.pallas_call(
        sweep_kernel,
        out_shape=jax.ShapeDtypeStruct((64, STATE), BF),
        in_specs=[smem] + [anywhere] * 4,
        out_specs=vmem,
        scratch_shapes=[
            pltpu.VMEM((PLANES, SPAN_X * SLOTS * 8, 128), F32),
            pltpu.VMEM((PLANES, LEVELS * 64, 128), F32),
            pltpu.VMEM((PLANES, 64, 128), F32),
            pltpu.VMEM((PLANES, 64, 128), F32),
            pltpu.VMEM((128, 24, 128), BF),
            pltpu.VMEM((128, 24, 128), BF),
            pltpu.VMEM((STATE, STATE), BF),
            pltpu.VMEM((STATE, STATE), BF),
            pltpu.SemaphoreType.DMA((10,)),
        ],
        name="sweep",
    )(place, received, other_half, step, reorder)

    upstream = lax.all_to_all(
        chosen.reshape(N_GY, TILES, STATE), "gy", 0, 0, tiled=True
    ).reshape(ENS * TILES, STATE)

    natural = pl.pallas_call(
        natural_kernel,
        out_shape=jax.ShapeDtypeStruct((TILES * ENS, CELLS), BF),
        in_specs=[smem] + [vmem] * 5,
        out_specs=vmem,
        name="natural",
    )(place, *home, spread)

    width = 1024
    out = pl.pallas_call(
        final_kernel,
        grid=(CELLS // width,),
        out_shape=jax.ShapeDtypeStruct((TILES * ENS, CELLS), F32),
        in_specs=[
            pl.BlockSpec((64, STATE), lambda g: (0, 0)),
            pl.BlockSpec((64, 64), lambda g: (0, 0)),
            pl.BlockSpec((STATE, width), lambda g: (0, g)),
            pl.BlockSpec((64, width), lambda g: (0, g)),
        ],
        out_specs=pl.BlockSpec((64, width), lambda g: (0, g)),
        scratch_shapes=[pltpu.VMEM((64, STATE), BF)],
        name="evolve",
    )(upstream, swap_rows, kriging, natural)
    return out.reshape(BX, BY, BZ, ENS, CELLS)


def solution(mesh):
    placed = (
        P(None, ("gx", "gy")),
        P(),
        P("gx", "gy", "gz", None, None, None),
        P("gx", "gy", "gz", None),
    )

    return jax.shard_map(
        local,
        mesh=mesh,
        in_specs=placed,
        out_specs=P("gx", "gy", "gz", None, None),
        check_vma=False,
    )
```

```python
import functools

import jax
import jax.numpy as jnp
import numpy as np
from jax import lax
from jax.experimental import pallas as pl
from jax.experimental.pallas import tpu as pltpu
from jax.sharding import PartitionSpec as P


TILE = 16
CELLS = 4096
FACE = 256
BX = 2
BY = 2
BZ = 2
TILES = 8
ENS = 8
N_GX = 4
N_GY = 8
N_GZ = 4
SPAN_X = N_GX * BX
SPAN_Y = N_GY * BY
SPAN_Z = N_GZ * BZ
LEVELS = SPAN_X + SPAN_Y + SPAN_Z - 2
COLS_DEV = CELLS // (N_GX * N_GY)
PART = COLS_DEV // N_GZ
HALF = PART // 2
STATE = 3 * FACE
PLANES = STATE // 128
FACE_COLS = 352
PARTS = 8
SLOTS = SPAN_Y + SPAN_X - 1 + SPAN_Z - 1 + 14

BF = jnp.bfloat16
F32 = jnp.float32


def column_orders():
    orders = []
    for s in range(N_GZ):
        z_cells = [(4 * e + (s + 1) % 4) * TILE + TILE - 1 for e in range(2)]
        y_cells = [7 * TILE + 4 * ((s - 15) % 4) + m for m in range(4)]
        first = z_cells + [c for c in y_cells if c not in z_cells]
        part = [c for c in range(COLS_DEV) if (c // TILE + c % TILE // 4) % 4 == s]
        orders.append(first + [c for c in part if c not in first])
    return np.array(orders, np.int32)


ORDERS = column_orders()


def state_order():
    rows = np.zeros(STATE, np.int32)
    cells = np.zeros(STATE, np.int32)
    for f in range(STATE):
        plane, lane = divmod(f, 128)
        if plane < 4:
            s, slot = plane, lane % 64
            if lane < 64:
                i, q = 30 + slot // 32, slot % 32
                v, w = 8 * (i % 2) + ORDERS[s, q] // TILE, ORDERS[s, q] % TILE
                rows[f], cells[f] = v * 16 + w, (15 * 16 + v) * 16 + w
            else:
                u, w = slot // 4, 4 * ((s - 15) % 4) + slot % 4
                rows[f], cells[f] = FACE + u * 16 + w, (u * 16 + 15) * 16 + w
        else:
            s, slot = 2 * (plane - 4) + lane // 64, lane % 64
            i, e = slot // 2, slot % 2
            u, v = i // 2, 8 * (i % 2) + 4 * e + (s + 1) % 4
            rows[f], cells[f] = 2 * FACE + u * 16 + v, (u * 16 + v) * 16 + 15
    return rows, cells


STATE_ROWS, STATE_CELLS = state_order()


def one_hot(condition):
    return condition.astype(BF)


def iota(shape, axis):
    return lax.broadcasted_iota(jnp.int32, shape, axis)


def to_bf16_dot(left, right):
    return jnp.dot(left, right, preferred_element_type=F32).astype(BF)


def plane_shift(value, dx, dz, swap=0):
    pairs = []
    for gx in range(N_GX):
        for gy in range(N_GY):
            x, z, core = gy // 2, (gy % 2) * 2 + gx // 2, gx % 2
            move_x, move_z = (dx, dz) if core == 0 else (dz, dx)
            x, z, core = (x + move_x) % 4, (z + move_z) % 4, core ^ swap
            pairs.append((gx * N_GY + gy, ((z % 2) * 2 + core) * N_GY + x * 2 + z // 2))
    return lax.ppermute(value, ("gx", "gy"), pairs)


def line_shift(value, steps):
    return lax.ppermute(value, "gz", [(s, (s + steps) % N_GZ) for s in range(N_GZ)])


def slot_of(d):
    return d % 2 * 2 + d // 2


def by_core(core, refs, body):
    own, other = refs[:4], refs[4:]

    @pl.when(core == 0)
    def _():
        body(own, other)

    @pl.when(core == 1)
    def _():
        body(other, own)


def noise_kernel(place, *refs):
    row_refs = refs[:4]
    piece_refs = refs[4:12]
    noise_out = refs[12]
    rows, factors, acc, sem_rows, sem_factor = refs[13:]
    x, z, core = place[0], place[1], place[2]
    for back in range(N_GZ):
        pltpu.make_async_copy(row_refs[back], rows.at[back], sem_rows).start()

    def load_all(first_refs, second_refs):
        for parity in range(2):
            group = lax.rem(z + parity, 2)
            for dz in (parity, parity + 2):
                high = lax.rem(z - dz + 4, 4) // 2
                for dx in range(4):
                    target = (lax.rem(x - dx + 4, 4) * 2 + high) * 4
                    for t in range(2):
                        for ref, slot, kind in (
                            (first_refs[dz], slot_of(dx), 0),
                            (second_refs[dx], slot_of(dz), 2),
                        ):
                            pltpu.make_async_copy(
                                ref.at[pl.ds(t * 64 + slot * 16, 16)],
                                factors.at[group, target + kind + t],
                                sem_factor.at[parity],
                            ).start()

    by_core(core, piece_refs, load_all)
    pltpu.make_async_copy(rows, rows, sem_rows).wait()
    wide = 512
    for parity in range(2):
        group = lax.rem(z + parity, 2)
        block = factors.at[group]
        pltpu.make_async_copy(block, block, sem_factor.at[parity]).wait()
        acc[...] = jnp.zeros_like(acc)

        @pl.loop(0, 2 * group + 2)
        def _(chunk):
            span = pl.ds(pl.multiple_of(chunk * 1024, 1024), 1024)
            acc[...] += lax.dot_general(
                rows[:, :, span].reshape(N_GZ * 64, 1024),
                factors[group, :, :, span].reshape(wide, 1024),
                (((1,), (1,)), ((), ())),
                preferred_element_type=F32,
            )

        noise_out[:, pl.ds(pl.multiple_of(group * wide, wide), wide)] = acc[...].astype(BF)


def face_kernel(place, select, row_order, *refs):
    row_refs = refs[:4]
    piece_refs = refs[4:12]
    copies_out = refs[12]
    rows, factors, face_out, sem_rows, sem_factor, sem_out = refs[13:]
    x, z, core = place[0], place[1], place[2]
    odd = lax.rem(z + 1, 2)
    holder = lax.rem(x + 1, 4)

    def load(chunk, ref, start, target, count):
        span = pl.ds(chunk * 1024, 1024)
        pltpu.make_async_copy(
            ref.at[pl.ds(start, count), span],
            factors.at[chunk, pl.ds(target, count)],
            sem_factor.at[chunk],
        ).start()

    def load_rows(chunk):
        for back in range(N_GZ):
            pltpu.make_async_copy(
                row_refs[back].at[:, pl.ds(chunk * 1024, 1024)],
                rows.at[chunk, back],
                sem_rows.at[chunk],
            ).start()

    def load_all(first_refs, second_refs):
        for chunk in range(4):
            load_rows(chunk)
            load_chunk(functools.partial(load, chunk), first_refs, second_refs)

    def load_chunk(load, first_refs, second_refs):
        for dz in range(4):
            load(first_refs[dz], 0, 96 + dz * 64, 64)
        held = pl.multiple_of(64 + slot_of(holder) * 16, 16)
        part = pl.multiple_of(odd * 32, 32)
        for parity in range(2):

            @pl.when(odd == parity)
            def _():
                load(first_refs[parity], held, 0, 16)
                load(first_refs[parity + 2], held, 16, 16)

        for dx in range(4):

            @pl.when(holder == dx)
            def _():
                load(second_refs[dx], part, 32, 32)
                load(second_refs[dx], part + 64, 64, 32)

    by_core(core, piece_refs, load_all)
    product = jnp.zeros((N_GZ * 64, FACE_COLS), F32)
    for chunk in range(4):
        row_block, factor_block = rows.at[chunk], factors.at[chunk]
        pltpu.make_async_copy(row_block, row_block, sem_rows.at[chunk]).wait()
        pltpu.make_async_copy(factor_block, factor_block, sem_factor.at[chunk]).wait()
        product += lax.dot_general(
            rows[chunk].reshape(N_GZ * 64, 1024),
            factors[chunk],
            (((1,), (1,)), ((), ())),
            preferred_element_type=F32,
        )
    product = product.astype(BF)
    sums = jnp.dot(product, select[...], preferred_element_type=F32).astype(BF)
    faces = jnp.dot(row_order[...], sums, preferred_element_type=F32)
    low = iota((8, 128), 1) < 64
    for r in range(ENS):
        for a in range(BX):
            base = r * 32 + a * 16
            face_out[a, r, 0:16, :] = faces[base : base + 16, :128].astype(BF)
            first = faces[base : base + 8, 128:]
            second = faces[base + 8 : base + 16, 128:]
            face_out[a, r, 16:24, :] = jnp.where(low, first, second).astype(BF)
    copies = [
        pltpu.make_async_copy(face_out, copies_out.at[side, :, :, k], sem_out.at[side * N_GZ + k])
        for side in range(N_GX // 2)
        for k in range(N_GZ)
    ]
    for copy in copies:
        copy.start()
    for copy in copies:
        copy.wait()


def sweep_kernel(place, own_ref, other_ref, step_ref, reorder_ref, out, *scratch):
    noise, history, state, picked, own_half, other_half, step, reorder, sems = scratch
    core, gz = place[2], place[3]
    gx = lax.rem(place[1], 2) * 2 + core
    low8 = iota((8, 128), 1) < 64
    count = N_GY * N_GZ
    for bx in range(N_GX):
        chunk = pl.ds(bx * count, count)
        pltpu.make_async_copy(own_ref.at[chunk], own_half.at[chunk], sems.at[2 * bx]).start()
        pltpu.make_async_copy(other_ref.at[chunk], other_half.at[chunk], sems.at[2 * bx + 1]).start()
    load_step = pltpu.make_async_copy(step_ref, step, sems.at[8])
    load_reorder = pltpu.make_async_copy(reorder_ref, reorder, sems.at[9])
    load_step.start()
    load_reorder.start()

    for p in range(PLANES):
        for i in range(SPAN_X):
            noise[p, i * SLOTS * 8 : (i * SLOTS + 14) * 8, :] = jnp.zeros((112, 128), F32)

    def place_block(bx, by):
        block = bx * N_GY + by
        for a, half in ((core, own_half), (1 - core, other_half)):
            planes = [half[block * N_GZ + s, 0:16, :].astype(F32) for s in range(N_GZ)]
            zs = [half[block * N_GZ + s, 16:24, :].astype(F32) for s in range(N_GZ)]
            for b in range(BY):
                start = ((bx * BX + a) * SLOTS + by * BY + b + 14) * 8
                start = pl.multiple_of(start, 8)
                for p in range(4):
                    noise[p, pl.ds(start, 8), :] = planes[p][b * 8 : (b + 1) * 8]
                for pair in range(2):
                    first, second = zs[2 * pair], zs[2 * pair + 1]
                    if b == 0:
                        second = pltpu.roll(second, 64, 1)
                    else:
                        first = pltpu.roll(first, 64, 1)
                    noise[4 + pair, pl.ds(start, 8), :] = jnp.where(low8, first, second)

    for bx in range(N_GX):
        chunk = pl.ds(bx * count, count)
        pltpu.make_async_copy(own_ref.at[chunk], own_half.at[chunk], sems.at[2 * bx]).wait()
        pltpu.make_async_copy(other_ref.at[chunk], other_half.at[chunk], sems.at[2 * bx + 1]).wait()

        @pl.loop(0, N_GY)
        def _(by):
            place_block(bx, by)

    state[...] = jnp.zeros_like(state)
    low = iota((64, 128), 1) < 64
    has_below = (iota((64, 128), 0) % 8) != 7
    load_step.wait()

    @pl.loop(0, LEVELS, unroll=3)
    def _(level):
        upstream = []
        for p in range(PLANES):
            here = state[p]
            if p < 4:
                west = jnp.concatenate([jnp.zeros((8, 128), F32), here[:56]], 0)
                value = jnp.where(low, west, here)
            else:
                value = jnp.where(has_below, pltpu.roll(here, 63, 0), 0.0)
            history[p, pl.ds(pl.multiple_of(level * 64, 64), 64), :] = value
            upstream.append(value.astype(BF))
        joined = jnp.concatenate(upstream, 1)
        first = jnp.dot(joined, step[:, :256], preferred_element_type=F32)
        second = jnp.dot(joined, step[:, 256:512], preferred_element_type=F32)
        third = jnp.dot(joined[:, :384], step[:384, 512:], preferred_element_type=F32)
        third += jnp.dot(joined[:, 384:], step[384:, 512:], preferred_element_type=F32)
        result = jnp.concatenate([first, second, third], 1)
        for p in range(PLANES):
            rows = []
            for i in range(SPAN_X):
                start = (i * SLOTS + level - i + 7) * 8
                rows.append(noise[p, pl.ds(start, 8, stride=9), :])
            state[p] = result[:, p * 128 : (p + 1) * 128] + jnp.concatenate(rows, 0)

    for a in range(BX):
        for b in range(BY):
            for c in range(BZ):
                i = gx * BX + a
                k = gz * BZ + c
                start = (i + k + b) * 64 + i * 8 + 7 - k
                for p in range(PLANES):
                    picked[p, pl.ds((a * BY + b) * BZ + c, 8, stride=8), :] = history[
                        p, pl.ds(start, 8, stride=128), :
                    ]
    load_reorder.wait()
    values = jnp.concatenate([picked[p].astype(BF) for p in range(PLANES)], 1)
    out[...] = jnp.dot(values, reorder[...], preferred_element_type=F32).astype(BF)


def natural_kernel(place, first, second, third, fourth, spread, out):
    gz = place[3]
    total = jnp.zeros((512, 512), F32)
    for back, part in enumerate((first, second, third, fourth)):
        source = lax.rem(gz + back, N_GZ)
        stacked = jnp.concatenate([part[:, g * 128 : (g + 1) * 128] for g in range(8)], 0)
        total += jnp.dot(stacked, spread[source], preferred_element_type=F32)
    for g in range(8):
        for c in range(2):
            start = (g // 4 * 2 + c) * 1024 + g % 4 * 256
            values = total[g * 64 : (g + 1) * 64, c * 256 : (c + 1) * 256]
            out[:, start : start + 256] = values.astype(BF)


def final_kernel(faces, swap_rows, kriging, noise, out, weights, values, loads, stores):
    width = CELLS // PARTS
    copies = []
    for g in range(PARTS):
        source = kriging.at[:, pl.ds(g * width, width)]
        copies.append(pltpu.make_async_copy(source, weights.at[g], loads.at[g]))
        copies[g].start()
    upstream = jnp.dot(swap_rows[...], faces[...], preferred_element_type=F32).astype(BF)
    results = []
    for g in range(PARTS):
        span = slice(g * width, (g + 1) * width)
        copies[g].wait()
        product = jnp.dot(upstream, weights[g], preferred_element_type=F32)
        values[g] = product + noise[:, span].astype(F32)
        results.append(pltpu.make_async_copy(values.at[g], out.at[:, span], stores.at[g]))
        results[g].start()
    for result in results:
        result.wait()


def select_table():
    table = np.full((N_GX, N_GY, N_GZ, 3, FACE_COLS), -1, np.int32)
    for gx in range(N_GX):
        for gy in range(N_GY):
            x, z = gy // 2, (gy % 2) * 2 + gx // 2
            parity = (z + 1) % 2
            for s in range(N_GZ):
                lanes = table[gx, gy, s]
                for j in range(2):
                    start = (z - parity - 2 * j) % 4 // 2 * 32
                    for r in range(8):
                        lanes[0, j * 16 + 8 + r] = start + 8 + r
                        lanes[0, 32 + j * 16 + 8 + r] = start + 16 + r
                        lanes[0, 64 + j * 16 + 8 + r] = start + 24 + r
                for dz in range(4):
                    for dx in range(4):
                        for sc in range(2):
                            sx, sz = (x - dx) % 4, (z - dz) % 4
                            i = ((sz % 2) * 2 + sc) * N_GY + sx * 2 + sz // 2
                            base = 96 + dz * 64 + slot_of(dx) * 16 + sc * 8
                            for r in range(8):
                                column = ORDERS[s, r]
                                if i >= 30:
                                    lanes[0, base + r] = (i - 30) * 32 + r
                                if i % 2 == 1 and column // TILE == 7:
                                    lanes[1, base + r] = 64 + (i // 2) * 4 + column % 4
                                if r < 2:
                                    lanes[2, base + r] = 128 + i * 2 + r
    return table.reshape(-1, 3 * FACE_COLS)


def row_table():
    order = np.zeros((N_GZ, 256), np.int32)
    for gz in range(N_GZ):
        for target in range(256):
            k = 7 - target % 8
            tile = (target // 8 % 4) * 2 + k % 2
            order[gz, target] = ((gz - k // 2) % N_GZ) * 64 + tile * 8 + target // 32
    return order


def spread_table():
    table = np.zeros((N_GZ, 128), np.int32)
    for s in range(N_GZ):
        for n in range(128):
            device, q, core = n // 64, n % 64 // 16 * 8 + n % 8, n % 16 // 8
            table[s, n] = core * 256 + device * COLS_DEV + ORDERS[s, q]
    return table


def own_table():
    swapped = np.concatenate([ORDERS[:, HALF:], ORDERS[:, :HALF]], 1)
    return np.stack([ORDERS, swapped], 1).reshape(-1, PART)


def local(factor, kriging, normals, visit_order):
    gx = lax.axis_index("gx")
    gy = lax.axis_index("gy")
    gz = lax.axis_index("gz")
    place = jnp.stack([gy // 2, (gy % 2) * 2 + gx // 2, gx % 2, gz]).astype(jnp.int32)
    vmem = pl.BlockSpec(memory_space=pltpu.VMEM)
    smem = pl.BlockSpec(memory_space=pltpu.SMEM)
    anywhere = pl.BlockSpec(memory_space=pl.ANY)

    core = gx % 2
    own_columns = jnp.asarray(own_table())[gz * 2 + core]
    own = one_hot(iota((PART, COLS_DEV), 1) == own_columns[:, None])
    shard = lax.dot_general(
        own, factor, (((1,), (1,)), ((), ())), preferred_element_type=F32
    ).astype(BF)
    mine = shard[:HALF].reshape(2, 8, CELLS)
    given = plane_shift(shard[HALF:], 0, 0, 1).reshape(2, 8, CELLS)
    is_first = core == 0
    both = jnp.concatenate([jnp.where(is_first, mine, given), jnp.where(is_first, given, mine)], 1)
    line = [both]
    for d in (1, 2, 3):
        line.append(plane_shift(both, d, 0))
    line = jnp.concatenate([line[d] for d in (0, 2, 1, 3)], 1).reshape(8 * HALF, CELLS)

    drawn = normals.reshape(TILES, ENS, CELLS)
    ordered = drawn.at[visit_order.reshape(TILES)].get(mode="promise_in_bounds")
    ordered = ordered.reshape(TILES * ENS, CELLS)
    row_pieces = [ordered]
    for s in (1, 2, 3):
        row_pieces.append(line_shift(ordered, s))

    late, kriging_late, line, spread_places, state_rows = lax.optimization_barrier(
        (gz, kriging, line, jnp.asarray(spread_table()), jnp.asarray(STATE_ROWS))
    )
    lane = iota((FACE_COLS, 256), 1)
    device = (gx * N_GY + gy) * N_GZ + late
    lanes = jnp.asarray(select_table())[device].reshape(3, FACE_COLS, 1)
    select = one_hot(
        (lane == lanes[0]) | (lane == lanes[1]) | (lane == lanes[2])
        | ((lane - 64 == lanes[2]) & (lane >= 192))
    )
    row_order = one_hot(iota((256, 256), 1) == jnp.asarray(row_table())[late][:, None])
    spread = one_hot(iota((N_GZ, 128, 512), 2) == spread_places[:, :, None])
    reorder = one_hot(state_rows[:, None] == iota((STATE, STATE), 1))
    swap_rows = one_hot(
        iota((64, 64), 1) == jnp.asarray([(r % 8) * 8 + r // 8 for r in range(64)])[:, None]
    )
    to_state = one_hot(iota((CELLS, STATE), 0) == jnp.asarray(STATE_CELLS)[None, :])
    step = to_bf16_dot(reorder, to_bf16_dot(kriging_late, to_state))

    held = [line]
    for d in (1, 2, 3):
        held.append(plane_shift(line, 0, d))
    held[1], select, row_order, spread, step, reorder, place = lax.optimization_barrier(
        (held[1], select, row_order, spread, step, reorder, place)
    )
    pieces = held + [plane_shift(line, 0, 0, 1)]
    pieces += [plane_shift(piece, 0, 0, 1) for piece in held[1:]]

    copies = pl.pallas_call(
        face_kernel,
        out_shape=jax.ShapeDtypeStruct((N_GX // 2, BX, ENS, N_GZ, 24, 128), BF),
        in_specs=[smem, vmem, vmem] + [anywhere] * 12,
        out_specs=anywhere,
        scratch_shapes=[
            pltpu.VMEM((4, N_GZ, 64, 1024), BF),
            pltpu.VMEM((4, FACE_COLS, 1024), BF),
            pltpu.VMEM((BX, ENS, 24, 128), BF),
            pltpu.SemaphoreType.DMA((4,)),
            pltpu.SemaphoreType.DMA((4,)),
            pltpu.SemaphoreType.DMA((N_GX // 2 * N_GZ,)),
        ],
        compiler_params=pltpu.CompilerParams(vmem_limit_bytes=16 << 20),
        name="face_part",
    )(place, select, row_order, *row_pieces, *pieces)

    place, copies = lax.optimization_barrier((place, copies))
    noise_part = pl.pallas_call(
        noise_kernel,
        out_shape=jax.ShapeDtypeStruct((N_GZ * 64, N_GX * N_GY * PART), BF),
        in_specs=[smem] + [anywhere] * 12,
        out_specs=vmem,
        scratch_shapes=[
            pltpu.VMEM((N_GZ, 64, CELLS), BF),
            pltpu.VMEM((2, 32, 16, CELLS), BF),
            pltpu.VMEM((256, 512), F32),
            pltpu.SemaphoreType.DMA,
            pltpu.SemaphoreType.DMA((2,)),
        ],
        name="noise_part",
    )(place, *row_pieces, *pieces)

    received = lax.all_to_all(copies.reshape(128, 24, 128), ("gx", "gy", "gz"), 0, 0, tiled=True)
    parts = [noise_part[back * 64 : (back + 1) * 64] for back in range(N_GZ)]
    home = [parts[0]]
    for back in (1, 2, 3):
        home.append(line_shift(parts[back], -back))
    other_half = plane_shift(received, 0, 0, 1)

    chosen = pl.pallas_call(
        sweep_kernel,
        out_shape=jax.ShapeDtypeStruct((64, STATE), BF),
        in_specs=[smem] + [anywhere] * 4,
        out_specs=vmem,
        scratch_shapes=[
            pltpu.VMEM((PLANES, SPAN_X * SLOTS * 8, 128), F32),
            pltpu.VMEM((PLANES, LEVELS * 64, 128), F32),
            pltpu.VMEM((PLANES, 64, 128), F32),
            pltpu.VMEM((PLANES, 64, 128), F32),
            pltpu.VMEM((128, 24, 128), BF),
            pltpu.VMEM((128, 24, 128), BF),
            pltpu.VMEM((STATE, STATE), BF),
            pltpu.VMEM((STATE, STATE), BF),
            pltpu.SemaphoreType.DMA((10,)),
        ],
        name="sweep",
    )(place, received, other_half, step, reorder)

    upstream = lax.all_to_all(
        chosen.reshape(N_GY, TILES, STATE), "gy", 0, 0, tiled=True
    ).reshape(ENS * TILES, STATE)

    natural = pl.pallas_call(
        natural_kernel,
        out_shape=jax.ShapeDtypeStruct((TILES * ENS, CELLS), BF),
        in_specs=[smem] + [vmem] * 5,
        out_specs=vmem,
        name="natural",
    )(place, *home, spread)

    out = pl.pallas_call(
        final_kernel,
        out_shape=jax.ShapeDtypeStruct((TILES * ENS, CELLS), F32),
        in_specs=[vmem, vmem, anywhere, vmem],
        out_specs=anywhere,
        scratch_shapes=[
            pltpu.VMEM((PARTS, STATE, CELLS // PARTS), BF),
            pltpu.VMEM((PARTS, TILES * ENS, CELLS // PARTS), F32),
            pltpu.SemaphoreType.DMA((PARTS,)),
            pltpu.SemaphoreType.DMA((PARTS,)),
        ],
        name="evolve",
    )(upstream, swap_rows, kriging, natural)
    return out.reshape(BX, BY, BZ, ENS, CELLS)


def solution(mesh):
    placed = (
        P(None, ("gx", "gy")),
        P(),
        P("gx", "gy", "gz", None, None, None),
        P("gx", "gy", "gz", None),
    )

    return jax.shard_map(
        local,
        mesh=mesh,
        in_specs=placed,
        out_specs=P("gx", "gy", "gz", None, None),
        check_vma=False,
    )
```

```python
import functools

import jax
import jax.numpy as jnp
import numpy as np
from jax import lax
from jax.experimental import pallas as pl
from jax.experimental.pallas import tpu as pltpu
from jax.sharding import PartitionSpec as P


TILE = 16
CELLS = 4096
FACE = 256
BX = 2
BY = 2
BZ = 2
TILES = 8
ENS = 8
N_GX = 4
N_GY = 8
N_GZ = 4
SPAN_X = N_GX * BX
SPAN_Y = N_GY * BY
SPAN_Z = N_GZ * BZ
LEVELS = SPAN_X + SPAN_Y + SPAN_Z - 2
COLS_DEV = CELLS // (N_GX * N_GY)
PART = COLS_DEV // N_GZ
HALF = PART // 2
STATE = 3 * FACE
PLANES = STATE // 128
FACE_COLS = 352
PARTS = 8
DEPTH = 2048
SLOTS = SPAN_Y + SPAN_X - 1 + SPAN_Z - 1 + 14

BF = jnp.bfloat16
F32 = jnp.float32


def column_orders():
    orders = []
    for s in range(N_GZ):
        z_cells = [(4 * e + (s + 1) % 4) * TILE + TILE - 1 for e in range(2)]
        y_cells = [7 * TILE + 4 * ((s - 15) % 4) + m for m in range(4)]
        first = z_cells + [c for c in y_cells if c not in z_cells]
        part = [c for c in range(COLS_DEV) if (c // TILE + c % TILE // 4) % 4 == s]
        orders.append(first + [c for c in part if c not in first])
    return np.array(orders, np.int32)


ORDERS = column_orders()


def state_order():
    rows = np.zeros(STATE, np.int32)
    cells = np.zeros(STATE, np.int32)
    for f in range(STATE):
        plane, lane = divmod(f, 128)
        if plane < 4:
            s, slot = plane, lane % 64
            if lane < 64:
                i, q = 30 + slot // 32, slot % 32
                v, w = 8 * (i % 2) + ORDERS[s, q] // TILE, ORDERS[s, q] % TILE
                rows[f], cells[f] = v * 16 + w, (15 * 16 + v) * 16 + w
            else:
                u, w = slot // 4, 4 * ((s - 15) % 4) + slot % 4
                rows[f], cells[f] = FACE + u * 16 + w, (u * 16 + 15) * 16 + w
        else:
            s, slot = 2 * (plane - 4) + lane // 64, lane % 64
            i, e = slot // 2, slot % 2
            u, v = i // 2, 8 * (i % 2) + 4 * e + (s + 1) % 4
            rows[f], cells[f] = 2 * FACE + u * 16 + v, (u * 16 + v) * 16 + 15
    return rows, cells


STATE_ROWS, STATE_CELLS = state_order()


def one_hot(condition):
    return condition.astype(BF)


def iota(shape, axis):
    return lax.broadcasted_iota(jnp.int32, shape, axis)


def to_bf16_dot(left, right):
    return jnp.dot(left, right, preferred_element_type=F32).astype(BF)


def plane_shift(value, dx, dz, swap=0):
    pairs = []
    for gx in range(N_GX):
        for gy in range(N_GY):
            x, z, core = gy // 2, (gy % 2) * 2 + gx // 2, gx % 2
            move_x, move_z = (dx, dz) if core == 0 else (dz, dx)
            x, z, core = (x + move_x) % 4, (z + move_z) % 4, core ^ swap
            pairs.append((gx * N_GY + gy, ((z % 2) * 2 + core) * N_GY + x * 2 + z // 2))
    return lax.ppermute(value, ("gx", "gy"), pairs)


def line_shift(value, steps):
    return lax.ppermute(value, "gz", [(s, (s + steps) % N_GZ) for s in range(N_GZ)])


def slot_of(d):
    return d % 2 * 2 + d // 2


def by_core(core, refs, body):
    own, other = refs[:4], refs[4:]

    @pl.when(core == 0)
    def _():
        body(own, other)

    @pl.when(core == 1)
    def _():
        body(other, own)


def noise_kernel(place, *refs):
    row_refs = refs[:4]
    piece_refs = refs[4:12]
    noise_out = refs[12]
    rows, factors, acc, sem_rows, sem_factor = refs[13:]
    x, z, core = place[0], place[1], place[2]
    for back in range(N_GZ):
        pltpu.make_async_copy(row_refs[back], rows.at[back], sem_rows).start()

    def load_all(first_refs, second_refs):
        for parity in range(2):
            group = lax.rem(z + parity, 2)
            for dz in (parity, parity + 2):
                high = lax.rem(z - dz + 4, 4) // 2
                for dx in range(4):
                    target = (lax.rem(x - dx + 4, 4) * 2 + high) * 4
                    for t in range(2):
                        for ref, slot, kind in (
                            (first_refs[dz], slot_of(dx), 0),
                            (second_refs[dx], slot_of(dz), 2),
                        ):
                            pltpu.make_async_copy(
                                ref.at[pl.ds(t * 64 + slot * 16, 16)],
                                factors.at[group, target + kind + t],
                                sem_factor.at[parity],
                            ).start()

    by_core(core, piece_refs, load_all)
    pltpu.make_async_copy(rows, rows, sem_rows).wait()
    wide = 512
    for parity in range(2):
        group = lax.rem(z + parity, 2)
        block = factors.at[group]
        pltpu.make_async_copy(block, block, sem_factor.at[parity]).wait()
        acc[...] = jnp.zeros_like(acc)

        @pl.loop(0, 2 * group + 2)
        def _(chunk):
            span = pl.ds(pl.multiple_of(chunk * 1024, 1024), 1024)
            acc[...] += lax.dot_general(
                rows[:, :, span].reshape(N_GZ * 64, 1024),
                factors[group, :, :, span].reshape(wide, 1024),
                (((1,), (1,)), ((), ())),
                preferred_element_type=F32,
            )

        noise_out[:, pl.ds(pl.multiple_of(group * wide, wide), wide)] = acc[...].astype(BF)


def face_kernel(place, select, row_order, *refs):
    row_refs = refs[:4]
    piece_refs = refs[4:12]
    copies_out = refs[12]
    rows, factors, face_out, sem_rows, sem_factor, sem_out = refs[13:]
    x, z, core = place[0], place[1], place[2]
    odd = lax.rem(z + 1, 2)
    holder = lax.rem(x + 1, 4)

    def load(chunk, ref, start, target, count):
        span = pl.ds(chunk * DEPTH, DEPTH)
        pltpu.make_async_copy(
            ref.at[pl.ds(start, count), span],
            factors.at[chunk, pl.ds(target, count)],
            sem_factor.at[chunk],
        ).start()

    def load_rows(chunk):
        for back in range(N_GZ):
            pltpu.make_async_copy(
                row_refs[back].at[:, pl.ds(chunk * DEPTH, DEPTH)],
                rows.at[chunk, back],
                sem_rows.at[chunk],
            ).start()

    def load_all(first_refs, second_refs):
        for chunk in range(CELLS // DEPTH):
            load_rows(chunk)
            load_chunk(functools.partial(load, chunk), first_refs, second_refs)

    def load_chunk(load, first_refs, second_refs):
        for dz in range(4):
            load(first_refs[dz], 0, 96 + dz * 64, 64)
        held = pl.multiple_of(64 + slot_of(holder) * 16, 16)
        part = pl.multiple_of(odd * 32, 32)
        for parity in range(2):

            @pl.when(odd == parity)
            def _():
                load(first_refs[parity], held, 0, 16)
                load(first_refs[parity + 2], held, 16, 16)

        for dx in range(4):

            @pl.when(holder == dx)
            def _():
                load(second_refs[dx], part, 32, 32)
                load(second_refs[dx], part + 64, 64, 32)

    by_core(core, piece_refs, load_all)
    product = jnp.zeros((N_GZ * 64, FACE_COLS), F32)
    for chunk in range(CELLS // DEPTH):
        row_block, factor_block = rows.at[chunk], factors.at[chunk]
        pltpu.make_async_copy(row_block, row_block, sem_rows.at[chunk]).wait()
        pltpu.make_async_copy(factor_block, factor_block, sem_factor.at[chunk]).wait()
        product += lax.dot_general(
            rows[chunk].reshape(N_GZ * 64, DEPTH),
            factors[chunk],
            (((1,), (1,)), ((), ())),
            preferred_element_type=F32,
        )
    product = product.astype(BF)
    sums = jnp.dot(product, select[...], preferred_element_type=F32).astype(BF)
    faces = jnp.dot(row_order[...], sums, preferred_element_type=F32)
    low = iota((8, 128), 1) < 64
    for r in range(ENS):
        for a in range(BX):
            base = r * 32 + a * 16
            face_out[a, r, 0:16, :] = faces[base : base + 16, :128].astype(BF)
            first = faces[base : base + 8, 128:]
            second = faces[base + 8 : base + 16, 128:]
            face_out[a, r, 16:24, :] = jnp.where(low, first, second).astype(BF)
    copies = [
        pltpu.make_async_copy(face_out, copies_out.at[side, :, :, k], sem_out.at[side * N_GZ + k])
        for side in range(N_GX // 2)
        for k in range(N_GZ)
    ]
    for copy in copies:
        copy.start()
    for copy in copies:
        copy.wait()


def sweep_kernel(place, own_ref, other_ref, step_ref, reorder_ref, out, *scratch):
    noise, history, state, picked, own_half, other_half, step, reorder, sems = scratch
    core, gz = place[2], place[3]
    gx = lax.rem(place[1], 2) * 2 + core
    low8 = iota((8, 128), 1) < 64
    count = N_GY * N_GZ
    for bx in range(N_GX):
        chunk = pl.ds(bx * count, count)
        pltpu.make_async_copy(own_ref.at[chunk], own_half.at[chunk], sems.at[2 * bx]).start()
        pltpu.make_async_copy(other_ref.at[chunk], other_half.at[chunk], sems.at[2 * bx + 1]).start()
    load_step = pltpu.make_async_copy(step_ref, step, sems.at[8])
    load_reorder = pltpu.make_async_copy(reorder_ref, reorder, sems.at[9])
    load_step.start()
    load_reorder.start()

    for p in range(PLANES):
        for i in range(SPAN_X):
            noise[p, i * SLOTS * 8 : (i * SLOTS + 14) * 8, :] = jnp.zeros((112, 128), F32)

    def place_block(bx, by):
        block = bx * N_GY + by
        for a, half in ((core, own_half), (1 - core, other_half)):
            planes = [half[block * N_GZ + s, 0:16, :].astype(F32) for s in range(N_GZ)]
            zs = [half[block * N_GZ + s, 16:24, :].astype(F32) for s in range(N_GZ)]
            for b in range(BY):
                start = ((bx * BX + a) * SLOTS + by * BY + b + 14) * 8
                start = pl.multiple_of(start, 8)
                for p in range(4):
                    noise[p, pl.ds(start, 8), :] = planes[p][b * 8 : (b + 1) * 8]
                for pair in range(2):
                    first, second = zs[2 * pair], zs[2 * pair + 1]
                    if b == 0:
                        second = pltpu.roll(second, 64, 1)
                    else:
                        first = pltpu.roll(first, 64, 1)
                    noise[4 + pair, pl.ds(start, 8), :] = jnp.where(low8, first, second)

    for bx in range(N_GX):
        chunk = pl.ds(bx * count, count)
        pltpu.make_async_copy(own_ref.at[chunk], own_half.at[chunk], sems.at[2 * bx]).wait()
        pltpu.make_async_copy(other_ref.at[chunk], other_half.at[chunk], sems.at[2 * bx + 1]).wait()

        @pl.loop(0, N_GY, unroll=2)
        def _(by):
            place_block(bx, by)

    state[...] = jnp.zeros_like(state)
    low = iota((64, 128), 1) < 64
    has_below = (iota((64, 128), 0) % 8) != 7
    load_step.wait()

    @pl.loop(0, LEVELS, unroll=3)
    def _(level):
        upstream = []
        for p in range(PLANES):
            here = state[p]
            if p < 4:
                west = jnp.concatenate([jnp.zeros((8, 128), F32), here[:56]], 0)
                value = jnp.where(low, west, here)
            else:
                value = jnp.where(has_below, pltpu.roll(here, 63, 0), 0.0)
            history[p, pl.ds(pl.multiple_of(level * 64, 64), 64), :] = value
            upstream.append(value.astype(BF))
        joined = jnp.concatenate(upstream, 1)
        first = jnp.dot(joined, step[:, :256], preferred_element_type=F32)
        second = jnp.dot(joined, step[:, 256:512], preferred_element_type=F32)
        third = jnp.dot(joined[:, :384], step[:384, 512:], preferred_element_type=F32)
        third += jnp.dot(joined[:, 384:], step[384:, 512:], preferred_element_type=F32)
        result = jnp.concatenate([first, second, third], 1)
        for p in range(PLANES):
            rows = []
            for i in range(SPAN_X):
                start = (i * SLOTS + level - i + 7) * 8
                rows.append(noise[p, pl.ds(start, 8, stride=9), :])
            state[p] = result[:, p * 128 : (p + 1) * 128] + jnp.concatenate(rows, 0)

    for a in range(BX):
        for b in range(BY):
            for c in range(BZ):
                i = gx * BX + a
                k = gz * BZ + c
                start = (i + k + b) * 64 + i * 8 + 7 - k
                for p in range(PLANES):
                    picked[p, pl.ds((a * BY + b) * BZ + c, 8, stride=8), :] = history[
                        p, pl.ds(start, 8, stride=128), :
                    ]
    load_reorder.wait()
    values = jnp.concatenate([picked[p].astype(BF) for p in range(PLANES)], 1)
    out[...] = jnp.dot(values, reorder[...], preferred_element_type=F32).astype(BF)


def natural_kernel(place, first, second, third, fourth, spread, out):
    gz = place[3]
    total = jnp.zeros((512, 512), F32)
    for back, part in enumerate((first, second, third, fourth)):
        source = lax.rem(gz + back, N_GZ)
        stacked = jnp.concatenate([part[:, g * 128 : (g + 1) * 128] for g in range(8)], 0)
        total += jnp.dot(stacked, spread[source], preferred_element_type=F32)
    for g in range(8):
        for c in range(2):
            start = (g // 4 * 2 + c) * 1024 + g % 4 * 256
            values = total[g * 64 : (g + 1) * 64, c * 256 : (c + 1) * 256]
            out[:, start : start + 256] = values.astype(BF)


def swap_kernel(out):
    target, source = iota((64, 64), 0), iota((64, 64), 1)
    out[...] = one_hot(source == (target & 7) * 8 + (target >> 3))


def final_kernel(faces, swap_rows, kriging, noise, out, weights, values, loads, stores):
    width = CELLS // PARTS
    copies = []
    for g in range(PARTS):
        source = kriging.at[:, pl.ds(g * width, width)]
        copies.append(pltpu.make_async_copy(source, weights.at[g], loads.at[g]))
        copies[g].start()
    upstream = jnp.dot(swap_rows[...], faces[...], preferred_element_type=F32).astype(BF)
    results = []
    for g in range(PARTS):
        span = slice(g * width, (g + 1) * width)
        copies[g].wait()
        product = jnp.dot(upstream, weights[g], preferred_element_type=F32)
        values[g] = product + noise[:, span].astype(F32)
        results.append(pltpu.make_async_copy(values.at[g], out.at[:, span], stores.at[g]))
        results[g].start()
    for result in results:
        result.wait()


def select_table():
    table = np.full((N_GX, N_GY, N_GZ, 3, FACE_COLS), -1, np.int32)
    for gx in range(N_GX):
        for gy in range(N_GY):
            x, z = gy // 2, (gy % 2) * 2 + gx // 2
            parity = (z + 1) % 2
            for s in range(N_GZ):
                lanes = table[gx, gy, s]
                for j in range(2):
                    start = (z - parity - 2 * j) % 4 // 2 * 32
                    for r in range(8):
                        lanes[0, j * 16 + 8 + r] = start + 8 + r
                        lanes[0, 32 + j * 16 + 8 + r] = start + 16 + r
                        lanes[0, 64 + j * 16 + 8 + r] = start + 24 + r
                for dz in range(4):
                    for dx in range(4):
                        for sc in range(2):
                            sx, sz = (x - dx) % 4, (z - dz) % 4
                            i = ((sz % 2) * 2 + sc) * N_GY + sx * 2 + sz // 2
                            base = 96 + dz * 64 + slot_of(dx) * 16 + sc * 8
                            for r in range(8):
                                column = ORDERS[s, r]
                                if i >= 30:
                                    lanes[0, base + r] = (i - 30) * 32 + r
                                if i % 2 == 1 and column // TILE == 7:
                                    lanes[1, base + r] = 64 + (i // 2) * 4 + column % 4
                                if r < 2:
                                    lanes[2, base + r] = 128 + i * 2 + r
    return table.reshape(-1, 3 * FACE_COLS)


def row_table():
    order = np.zeros((N_GZ, 256), np.int32)
    for gz in range(N_GZ):
        for target in range(256):
            k = 7 - target % 8
            tile = (target // 8 % 4) * 2 + k % 2
            order[gz, target] = ((gz - k // 2) % N_GZ) * 64 + tile * 8 + target // 32
    return order


def spread_table():
    table = np.zeros((N_GZ, 128), np.int32)
    for s in range(N_GZ):
        for n in range(128):
            device, q, core = n // 64, n % 64 // 16 * 8 + n % 8, n % 16 // 8
            table[s, n] = core * 256 + device * COLS_DEV + ORDERS[s, q]
    return table


def own_table():
    swapped = np.concatenate([ORDERS[:, HALF:], ORDERS[:, :HALF]], 1)
    return np.stack([ORDERS, swapped], 1).reshape(-1, PART)


def local(factor, kriging, normals, visit_order):
    gx = lax.axis_index("gx")
    gy = lax.axis_index("gy")
    gz = lax.axis_index("gz")
    place = jnp.stack([gy // 2, (gy % 2) * 2 + gx // 2, gx % 2, gz]).astype(jnp.int32)
    vmem = pl.BlockSpec(memory_space=pltpu.VMEM)
    smem = pl.BlockSpec(memory_space=pltpu.SMEM)
    anywhere = pl.BlockSpec(memory_space=pl.ANY)

    core = gx % 2
    own_columns = jnp.asarray(own_table())[gz * 2 + core]
    own = one_hot(iota((PART, COLS_DEV), 1) == own_columns[:, None])
    shard = lax.dot_general(
        own, factor, (((1,), (1,)), ((), ())), preferred_element_type=F32
    ).astype(BF)
    mine = shard[:HALF].reshape(2, 8, CELLS)
    given = plane_shift(shard[HALF:], 0, 0, 1).reshape(2, 8, CELLS)
    is_first = core == 0
    both = jnp.concatenate([jnp.where(is_first, mine, given), jnp.where(is_first, given, mine)], 1)
    line = [both]
    for d in (1, 2, 3):
        line.append(plane_shift(both, d, 0))
    line = jnp.concatenate([line[d] for d in (0, 2, 1, 3)], 1).reshape(8 * HALF, CELLS)

    drawn = normals.reshape(TILES, ENS, CELLS)
    ordered = drawn.at[visit_order.reshape(TILES)].get(mode="promise_in_bounds")
    ordered = ordered.reshape(TILES * ENS, CELLS)
    row_pieces = [ordered]
    for s in (1, 2, 3):
        row_pieces.append(line_shift(ordered, s))

    late, kriging_late, line, spread_places, state_rows = lax.optimization_barrier(
        (gz, kriging, line, jnp.asarray(spread_table()), jnp.asarray(STATE_ROWS))
    )
    lane = iota((FACE_COLS, 256), 1)
    device = (gx * N_GY + gy) * N_GZ + late
    lanes = jnp.asarray(select_table())[device].reshape(3, FACE_COLS, 1)
    select = one_hot(
        (lane == lanes[0]) | (lane == lanes[1]) | (lane == lanes[2])
        | ((lane - 64 == lanes[2]) & (lane >= 192))
    )
    row_order = one_hot(iota((256, 256), 1) == jnp.asarray(row_table())[late][:, None])
    spread = one_hot(iota((N_GZ, 128, 512), 2) == spread_places[:, :, None])
    reorder = one_hot(state_rows[:, None] == iota((STATE, STATE), 1))
    swap_rows = pl.pallas_call(
        swap_kernel,
        out_shape=jax.ShapeDtypeStruct((64, 64), BF),
        out_specs=vmem,
        compiler_params=pltpu.CompilerParams(vmem_limit_bytes=67043328),
        name="swap_rows",
    )()
    to_state = one_hot(iota((CELLS, STATE), 0) == jnp.asarray(STATE_CELLS)[None, :])
    step = to_bf16_dot(reorder, to_bf16_dot(kriging_late, to_state))

    held = [line]
    for d in (1, 2, 3):
        held.append(plane_shift(line, 0, d))
    held[1], select, row_order, spread, step, reorder, place = lax.optimization_barrier(
        (held[1], select, row_order, spread, step, reorder, place)
    )
    pieces = held + [plane_shift(line, 0, 0, 1)]
    for d in (1, 2, 3):
        pieces.append(plane_shift(held[d], 0, 0, 1))

    copies = pl.pallas_call(
        face_kernel,
        out_shape=jax.ShapeDtypeStruct((N_GX // 2, BX, ENS, N_GZ, 24, 128), BF),
        in_specs=[smem, vmem, vmem] + [anywhere] * 12,
        out_specs=anywhere,
        scratch_shapes=[
            pltpu.VMEM((CELLS // DEPTH, N_GZ, 64, DEPTH), BF),
            pltpu.VMEM((CELLS // DEPTH, FACE_COLS, DEPTH), BF),
            pltpu.VMEM((BX, ENS, 24, 128), BF),
            pltpu.SemaphoreType.DMA((CELLS // DEPTH,)),
            pltpu.SemaphoreType.DMA((CELLS // DEPTH,)),
            pltpu.SemaphoreType.DMA((N_GX // 2 * N_GZ,)),
        ],
        compiler_params=pltpu.CompilerParams(vmem_limit_bytes=16 << 20),
        name="face_part",
    )(place, select, row_order, *row_pieces, *pieces)

    place, copies = lax.optimization_barrier((place, copies))
    noise_part = pl.pallas_call(
        noise_kernel,
        out_shape=jax.ShapeDtypeStruct((N_GZ * 64, N_GX * N_GY * PART), BF),
        in_specs=[smem] + [anywhere] * 12,
        out_specs=vmem,
        scratch_shapes=[
            pltpu.VMEM((N_GZ, 64, CELLS), BF),
            pltpu.VMEM((2, 32, 16, CELLS), BF),
            pltpu.VMEM((256, 512), F32),
            pltpu.SemaphoreType.DMA,
            pltpu.SemaphoreType.DMA((2,)),
        ],
        name="noise_part",
    )(place, *row_pieces, *pieces)

    received = lax.all_to_all(copies.reshape(128, 24, 128), ("gx", "gy", "gz"), 0, 0, tiled=True)
    parts = [noise_part[back * 64 : (back + 1) * 64] for back in range(N_GZ)]
    home = [parts[0]]
    for back in (1, 2, 3):
        home.append(line_shift(parts[back], -back))
    other_half = plane_shift(received, 0, 0, 1)

    chosen = pl.pallas_call(
        sweep_kernel,
        out_shape=jax.ShapeDtypeStruct((64, STATE), BF),
        in_specs=[smem] + [anywhere] * 4,
        out_specs=vmem,
        scratch_shapes=[
            pltpu.VMEM((PLANES, SPAN_X * SLOTS * 8, 128), F32),
            pltpu.VMEM((PLANES, LEVELS * 64, 128), F32),
            pltpu.VMEM((PLANES, 64, 128), F32),
            pltpu.VMEM((PLANES, 64, 128), F32),
            pltpu.VMEM((128, 24, 128), BF),
            pltpu.VMEM((128, 24, 128), BF),
            pltpu.VMEM((STATE, STATE), BF),
            pltpu.VMEM((STATE, STATE), BF),
            pltpu.SemaphoreType.DMA((10,)),
        ],
        name="sweep",
    )(place, received, other_half, step, reorder)

    upstream = lax.all_to_all(
        chosen.reshape(N_GY, TILES, STATE), "gy", 0, 0, tiled=True
    ).reshape(ENS * TILES, STATE)

    natural = pl.pallas_call(
        natural_kernel,
        out_shape=jax.ShapeDtypeStruct((TILES * ENS, CELLS), BF),
        in_specs=[smem] + [vmem] * 5,
        out_specs=vmem,
        compiler_params=pltpu.CompilerParams(vmem_limit_bytes=67043328),
        name="natural",
    )(place, *home, spread)

    out = pl.pallas_call(
        final_kernel,
        out_shape=jax.ShapeDtypeStruct((TILES * ENS, CELLS), F32),
        in_specs=[vmem, vmem, anywhere, vmem],
        out_specs=anywhere,
        scratch_shapes=[
            pltpu.VMEM((PARTS, STATE, CELLS // PARTS), BF),
            pltpu.VMEM((PARTS, TILES * ENS, CELLS // PARTS), F32),
            pltpu.SemaphoreType.DMA((PARTS,)),
            pltpu.SemaphoreType.DMA((PARTS,)),
        ],
        name="evolve",
    )(upstream, swap_rows, kriging, natural)
    return out.reshape(BX, BY, BZ, ENS, CELLS)


def solution(mesh):
    placed = (
        P(None, ("gx", "gy")),
        P(),
        P("gx", "gy", "gz", None, None, None),
        P("gx", "gy", "gz", None),
    )

    return jax.shard_map(
        local,
        mesh=mesh,
        in_specs=placed,
        out_specs=P("gx", "gy", "gz", None, None),
        check_vma=False,
    )
```

```python
import functools

import jax
import jax.numpy as jnp
import numpy as np
from jax import lax
from jax.experimental import pallas as pl
from jax.experimental.pallas import tpu as pltpu
from jax.sharding import PartitionSpec as P


TILE = 16
CELLS = 4096
FACE = 256
BX = 2
BY = 2
BZ = 2
TILES = 8
ENS = 8
N_GX = 4
N_GY = 8
N_GZ = 4
SPAN_X = N_GX * BX
SPAN_Y = N_GY * BY
SPAN_Z = N_GZ * BZ
LEVELS = SPAN_X + SPAN_Y + SPAN_Z - 2
COLS_DEV = CELLS // (N_GX * N_GY)
PART = COLS_DEV // N_GZ
HALF = PART // 2
STATE = 3 * FACE
PLANES = STATE // 128
FACE_COLS = 352
PARTS = 8
DEPTH = 2048
SLOTS = SPAN_Y + SPAN_X - 1 + SPAN_Z - 1 + 14

BF = jnp.bfloat16
F32 = jnp.float32


def column_orders():
    orders = []
    for s in range(N_GZ):
        z_cells = [(4 * e + (s + 1) % 4) * TILE + TILE - 1 for e in range(2)]
        y_cells = [7 * TILE + 4 * ((s - 15) % 4) + m for m in range(4)]
        first = z_cells + [c for c in y_cells if c not in z_cells]
        part = [c for c in range(COLS_DEV) if (c // TILE + c % TILE // 4) % 4 == s]
        orders.append(first + [c for c in part if c not in first])
    return np.array(orders, np.int32)


ORDERS = column_orders()


def state_order():
    rows = np.zeros(STATE, np.int32)
    cells = np.zeros(STATE, np.int32)
    for f in range(STATE):
        plane, lane = divmod(f, 128)
        if plane < 4:
            s, slot = plane, lane % 64
            if lane < 64:
                i, q = 30 + slot // 32, slot % 32
                v, w = 8 * (i % 2) + ORDERS[s, q] // TILE, ORDERS[s, q] % TILE
                rows[f], cells[f] = v * 16 + w, (15 * 16 + v) * 16 + w
            else:
                u, w = slot // 4, 4 * ((s - 15) % 4) + slot % 4
                rows[f], cells[f] = FACE + u * 16 + w, (u * 16 + 15) * 16 + w
        else:
            s, slot = 2 * (plane - 4) + lane // 64, lane % 64
            i, e = slot // 2, slot % 2
            u, v = i // 2, 8 * (i % 2) + 4 * e + (s + 1) % 4
            rows[f], cells[f] = 2 * FACE + u * 16 + v, (u * 16 + v) * 16 + 15
    return rows, cells


STATE_ROWS, STATE_CELLS = state_order()


def one_hot(condition):
    return condition.astype(BF)


def iota(shape, axis):
    return lax.broadcasted_iota(jnp.int32, shape, axis)


def to_bf16_dot(left, right):
    return jnp.dot(left, right, preferred_element_type=F32).astype(BF)


def plane_shift(value, dx, dz, swap=0):
    pairs = []
    for gx in range(N_GX):
        for gy in range(N_GY):
            x, z, core = gy // 2, (gy % 2) * 2 + gx // 2, gx % 2
            move_x, move_z = (dx, dz) if core == 0 else (dz, dx)
            x, z, core = (x + move_x) % 4, (z + move_z) % 4, core ^ swap
            pairs.append((gx * N_GY + gy, ((z % 2) * 2 + core) * N_GY + x * 2 + z // 2))
    return lax.ppermute(value, ("gx", "gy"), pairs)


def line_shift(value, steps):
    return lax.ppermute(value, "gz", [(s, (s + steps) % N_GZ) for s in range(N_GZ)])


def slot_of(d):
    return d % 2 * 2 + d // 2


def by_core(core, refs, body):
    own, other = refs[:4], refs[4:]

    @pl.when(core == 0)
    def _():
        body(own, other)

    @pl.when(core == 1)
    def _():
        body(other, own)


def noise_kernel(place, *refs):
    row_refs = refs[:4]
    piece_refs = refs[4:12]
    noise_out = refs[12]
    rows, factors, acc, sem_rows, sem_factor = refs[13:]
    x, z, core = place[0], place[1], place[2]
    for back in range(N_GZ):
        pltpu.make_async_copy(row_refs[back], rows.at[back], sem_rows).start()

    def load_all(first_refs, second_refs):
        for parity in range(2):
            group = lax.rem(z + parity, 2)
            for dz in (parity, parity + 2):
                high = lax.rem(z - dz + 4, 4) // 2
                for dx in range(4):
                    target = (lax.rem(x - dx + 4, 4) * 2 + high) * 4
                    for t in range(2):
                        for ref, slot, kind in (
                            (first_refs[dz], slot_of(dx), 0),
                            (second_refs[dx], slot_of(dz), 2),
                        ):
                            pltpu.make_async_copy(
                                ref.at[pl.ds(t * 64 + slot * 16, 16)],
                                factors.at[group, target + kind + t],
                                sem_factor.at[parity],
                            ).start()

    by_core(core, piece_refs, load_all)
    pltpu.make_async_copy(rows, rows, sem_rows).wait()
    wide = 512
    for parity in range(2):
        group = lax.rem(z + parity, 2)
        block = factors.at[group]
        pltpu.make_async_copy(block, block, sem_factor.at[parity]).wait()
        acc[...] = jnp.zeros_like(acc)

        @pl.loop(0, 2 * group + 2)
        def _(chunk):
            span = pl.ds(pl.multiple_of(chunk * 1024, 1024), 1024)
            acc[...] += lax.dot_general(
                rows[:, :, span].reshape(N_GZ * 64, 1024),
                factors[group, :, :, span].reshape(wide, 1024),
                (((1,), (1,)), ((), ())),
                preferred_element_type=F32,
            )

        noise_out[:, pl.ds(pl.multiple_of(group * wide, wide), wide)] = acc[...].astype(BF)


def face_kernel(place, select, row_order, *refs):
    row_refs = refs[:4]
    piece_refs = refs[4:12]
    copies_out = refs[12]
    rows, factors, face_out, sem_rows, sem_factor, sem_out = refs[13:]
    x, z, core = place[0], place[1], place[2]
    odd = lax.rem(z + 1, 2)
    holder = lax.rem(x + 1, 4)

    def load(chunk, ref, start, target, count):
        span = pl.ds(chunk * DEPTH, DEPTH)
        pltpu.make_async_copy(
            ref.at[pl.ds(start, count), span],
            factors.at[chunk, pl.ds(target, count)],
            sem_factor.at[chunk],
        ).start()

    def load_rows(chunk):
        for back in range(N_GZ):
            pltpu.make_async_copy(
                row_refs[back].at[:, pl.ds(chunk * DEPTH, DEPTH)],
                rows.at[chunk, back],
                sem_rows.at[chunk],
            ).start()

    def load_all(first_refs, second_refs):
        for chunk in range(CELLS // DEPTH):
            load_rows(chunk)
            load_chunk(functools.partial(load, chunk), first_refs, second_refs)

    def load_chunk(load, first_refs, second_refs):
        for dz in range(4):
            load(first_refs[dz], 0, 96 + dz * 64, 64)
        held = pl.multiple_of(64 + slot_of(holder) * 16, 16)
        part = pl.multiple_of(odd * 32, 32)
        for parity in range(2):

            @pl.when(odd == parity)
            def _():
                load(first_refs[parity], held, 0, 16)
                load(first_refs[parity + 2], held, 16, 16)

        for dx in range(4):

            @pl.when(holder == dx)
            def _():
                load(second_refs[dx], part, 32, 32)
                load(second_refs[dx], part + 64, 64, 32)

    by_core(core, piece_refs, load_all)
    product = jnp.zeros((N_GZ * 64, FACE_COLS), F32)
    for chunk in range(CELLS // DEPTH):
        row_block, factor_block = rows.at[chunk], factors.at[chunk]
        pltpu.make_async_copy(row_block, row_block, sem_rows.at[chunk]).wait()
        pltpu.make_async_copy(factor_block, factor_block, sem_factor.at[chunk]).wait()
        product += lax.dot_general(
            rows[chunk].reshape(N_GZ * 64, DEPTH),
            factors[chunk],
            (((1,), (1,)), ((), ())),
            preferred_element_type=F32,
        )
    product = product.astype(BF)
    sums = jnp.dot(product, select[...], preferred_element_type=F32).astype(BF)
    faces = jnp.dot(row_order[...], sums, preferred_element_type=F32)
    low = iota((8, 128), 1) < 64
    for r in range(ENS):
        for a in range(BX):
            base = r * 32 + a * 16
            face_out[a, r, 0:16, :] = faces[base : base + 16, :128].astype(BF)
            first = faces[base : base + 8, 128:]
            second = faces[base + 8 : base + 16, 128:]
            face_out[a, r, 16:24, :] = jnp.where(low, first, second).astype(BF)
    copies = [
        pltpu.make_async_copy(face_out, copies_out.at[side, :, :, k], sem_out.at[side * N_GZ + k])
        for side in range(N_GX // 2)
        for k in range(N_GZ)
    ]
    for copy in copies:
        copy.start()
    for copy in copies:
        copy.wait()


def sweep_kernel(place, own_ref, other_ref, step_ref, reorder_ref, out, *scratch):
    noise, history, state, picked, own_half, other_half, step, reorder, sems = scratch
    core, gz = place[2], place[3]
    gx = lax.rem(place[1], 2) * 2 + core
    low8 = iota((8, 128), 1) < 64
    count = N_GY * N_GZ
    for bx in range(N_GX):
        chunk = pl.ds(bx * count, count)
        pltpu.make_async_copy(own_ref.at[chunk], own_half.at[chunk], sems.at[2 * bx]).start()
        pltpu.make_async_copy(other_ref.at[chunk], other_half.at[chunk], sems.at[2 * bx + 1]).start()
    load_step = pltpu.make_async_copy(step_ref, step, sems.at[8])
    load_reorder = pltpu.make_async_copy(reorder_ref, reorder, sems.at[9])
    load_step.start()
    load_reorder.start()

    for p in range(PLANES):
        for i in range(SPAN_X):
            noise[p, i * SLOTS * 8 : (i * SLOTS + 14) * 8, :] = jnp.zeros((112, 128), F32)

    def place_block(bx, by):
        block = bx * N_GY + by
        for a, half in ((core, own_half), (1 - core, other_half)):
            planes = [half[block * N_GZ + s, 0:16, :].astype(F32) for s in range(N_GZ)]
            zs = [half[block * N_GZ + s, 16:24, :].astype(F32) for s in range(N_GZ)]
            for b in range(BY):
                start = ((bx * BX + a) * SLOTS + by * BY + b + 14) * 8
                start = pl.multiple_of(start, 8)
                for p in range(4):
                    noise[p, pl.ds(start, 8), :] = planes[p][b * 8 : (b + 1) * 8]
                for pair in range(2):
                    first, second = zs[2 * pair], zs[2 * pair + 1]
                    if b == 0:
                        second = pltpu.roll(second, 64, 1)
                    else:
                        first = pltpu.roll(first, 64, 1)
                    noise[4 + pair, pl.ds(start, 8), :] = jnp.where(low8, first, second)

    for bx in range(N_GX):
        chunk = pl.ds(bx * count, count)
        pltpu.make_async_copy(own_ref.at[chunk], own_half.at[chunk], sems.at[2 * bx]).wait()
        pltpu.make_async_copy(other_ref.at[chunk], other_half.at[chunk], sems.at[2 * bx + 1]).wait()

        @pl.loop(0, N_GY, unroll=8)
        def _(by):
            place_block(bx, by)

    state[...] = jnp.zeros_like(state)
    low = iota((64, 128), 1) < 64
    has_below = (iota((64, 128), 0) % 8) != 7
    load_step.wait()

    @pl.loop(0, LEVELS, unroll=3)
    def _(level):
        upstream = []
        for p in range(PLANES):
            here = state[p]
            if p < 4:
                west = jnp.concatenate([jnp.zeros((8, 128), F32), here[:56]], 0)
                value = jnp.where(low, west, here)
            else:
                value = jnp.where(has_below, pltpu.roll(here, 63, 0), 0.0)
            history[p, pl.ds(pl.multiple_of(level * 64, 64), 64), :] = value
            upstream.append(value.astype(BF))
        joined = jnp.concatenate(upstream, 1)
        first = jnp.dot(joined, step[:, :256], preferred_element_type=F32)
        second = jnp.dot(joined, step[:, 256:512], preferred_element_type=F32)
        third = jnp.dot(joined[:, :384], step[:384, 512:], preferred_element_type=F32)
        third += jnp.dot(joined[:, 384:], step[384:, 512:], preferred_element_type=F32)
        result = jnp.concatenate([first, second, third], 1)
        for p in range(PLANES):
            rows = []
            for i in range(SPAN_X):
                start = (i * SLOTS + level - i + 7) * 8
                rows.append(noise[p, pl.ds(start, 8, stride=9), :])
            state[p] = result[:, p * 128 : (p + 1) * 128] + jnp.concatenate(rows, 0)

    for a in range(BX):
        for b in range(BY):
            for c in range(BZ):
                i = gx * BX + a
                k = gz * BZ + c
                start = (i + k + b) * 64 + i * 8 + 7 - k
                for p in range(PLANES):
                    picked[p, pl.ds((a * BY + b) * BZ + c, 8, stride=8), :] = history[
                        p, pl.ds(start, 8, stride=128), :
                    ]
    load_reorder.wait()
    values = jnp.concatenate([picked[p].astype(BF) for p in range(PLANES)], 1)
    out[...] = jnp.dot(values, reorder[...], preferred_element_type=F32).astype(BF)


def natural_kernel(place, first, second, third, fourth, spread, out):
    gz = place[3]
    total = jnp.zeros((512, 512), F32)
    for back, part in enumerate((first, second, third, fourth)):
        source = lax.rem(gz + back, N_GZ)
        stacked = jnp.concatenate([part[:, g * 128 : (g + 1) * 128] for g in range(8)], 0)
        total += jnp.dot(stacked, spread[source], preferred_element_type=F32)
    for g in range(8):
        for c in range(2):
            start = (g // 4 * 2 + c) * 1024 + g % 4 * 256
            values = total[g * 64 : (g + 1) * 64, c * 256 : (c + 1) * 256]
            out[:, start : start + 256] = values.astype(BF)


def swap_kernel(out):
    target, source = iota((64, 64), 0), iota((64, 64), 1)
    out[...] = one_hot(source == (target & 7) * 8 + (target >> 3))


def final_kernel(faces, swap_rows, kriging, noise, out, weights, values, loads, stores):
    width = CELLS // PARTS
    copies = []
    for g in range(PARTS):
        source = kriging.at[:, pl.ds(g * width, width)]
        copies.append(pltpu.make_async_copy(source, weights.at[g], loads.at[g]))
        copies[g].start()
    upstream = jnp.dot(swap_rows[...], faces[...], preferred_element_type=F32).astype(BF)
    results = []
    for g in range(PARTS):
        span = slice(g * width, (g + 1) * width)
        copies[g].wait()
        product = jnp.dot(upstream, weights[g], preferred_element_type=F32)
        values[g] = product + noise[:, span].astype(F32)
        results.append(pltpu.make_async_copy(values.at[g], out.at[:, span], stores.at[g]))
        results[g].start()
    for result in results:
        result.wait()


def select_table():
    table = np.full((N_GX, N_GY, N_GZ, 3, FACE_COLS), -1, np.int32)
    for gx in range(N_GX):
        for gy in range(N_GY):
            x, z = gy // 2, (gy % 2) * 2 + gx // 2
            parity = (z + 1) % 2
            for s in range(N_GZ):
                lanes = table[gx, gy, s]
                for j in range(2):
                    start = (z - parity - 2 * j) % 4 // 2 * 32
                    for r in range(8):
                        lanes[0, j * 16 + 8 + r] = start + 8 + r
                        lanes[0, 32 + j * 16 + 8 + r] = start + 16 + r
                        lanes[0, 64 + j * 16 + 8 + r] = start + 24 + r
                for dz in range(4):
                    for dx in range(4):
                        for sc in range(2):
                            sx, sz = (x - dx) % 4, (z - dz) % 4
                            i = ((sz % 2) * 2 + sc) * N_GY + sx * 2 + sz // 2
                            base = 96 + dz * 64 + slot_of(dx) * 16 + sc * 8
                            for r in range(8):
                                column = ORDERS[s, r]
                                if i >= 30:
                                    lanes[0, base + r] = (i - 30) * 32 + r
                                if i % 2 == 1 and column // TILE == 7:
                                    lanes[1, base + r] = 64 + (i // 2) * 4 + column % 4
                                if r < 2:
                                    lanes[2, base + r] = 128 + i * 2 + r
    return table.reshape(-1, 3 * FACE_COLS)


def row_table():
    order = np.zeros((N_GZ, 256), np.int32)
    for gz in range(N_GZ):
        for target in range(256):
            k = 7 - target % 8
            tile = (target // 8 % 4) * 2 + k % 2
            order[gz, target] = ((gz - k // 2) % N_GZ) * 64 + tile * 8 + target // 32
    return order


def spread_table():
    table = np.zeros((N_GZ, 128), np.int32)
    for s in range(N_GZ):
        for n in range(128):
            device, q, core = n // 64, n % 64 // 16 * 8 + n % 8, n % 16 // 8
            table[s, n] = core * 256 + device * COLS_DEV + ORDERS[s, q]
    return table


def own_table():
    swapped = np.concatenate([ORDERS[:, HALF:], ORDERS[:, :HALF]], 1)
    return np.stack([ORDERS, swapped], 1).reshape(-1, PART)


def local(factor, kriging, normals, visit_order):
    gx = lax.axis_index("gx")
    gy = lax.axis_index("gy")
    gz = lax.axis_index("gz")
    place = jnp.stack([gy // 2, (gy % 2) * 2 + gx // 2, gx % 2, gz]).astype(jnp.int32)
    vmem = pl.BlockSpec(memory_space=pltpu.VMEM)
    smem = pl.BlockSpec(memory_space=pltpu.SMEM)
    anywhere = pl.BlockSpec(memory_space=pl.ANY)

    core = gx % 2
    own_columns = jnp.asarray(own_table())[gz * 2 + core]
    own = one_hot(iota((PART, COLS_DEV), 1) == own_columns[:, None])
    shard = lax.dot_general(
        own, factor, (((1,), (1,)), ((), ())), preferred_element_type=F32
    ).astype(BF)
    mine = shard[:HALF].reshape(2, 8, CELLS)
    given = plane_shift(shard[HALF:], 0, 0, 1).reshape(2, 8, CELLS)
    is_first = core == 0
    both = jnp.concatenate([jnp.where(is_first, mine, given), jnp.where(is_first, given, mine)], 1)
    line = [both]
    for d in (1, 2, 3):
        line.append(plane_shift(both, d, 0))
    line = jnp.concatenate([line[d] for d in (0, 2, 1, 3)], 1).reshape(8 * HALF, CELLS)

    drawn = normals.reshape(TILES, ENS, CELLS)
    ordered = drawn.at[visit_order.reshape(TILES)].get(mode="promise_in_bounds")
    ordered = ordered.reshape(TILES * ENS, CELLS)
    row_pieces = [ordered]
    for s in (1, 2, 3):
        row_pieces.append(line_shift(ordered, s))

    late, kriging_late, line, spread_places, state_rows = lax.optimization_barrier(
        (gz, kriging, line, jnp.asarray(spread_table()), jnp.asarray(STATE_ROWS))
    )
    lane = iota((FACE_COLS, 256), 1)
    device = (gx * N_GY + gy) * N_GZ + late
    lanes = jnp.asarray(select_table())[device].reshape(3, FACE_COLS, 1)
    select = one_hot(
        (lane == lanes[0]) | (lane == lanes[1]) | (lane == lanes[2])
        | ((lane - 64 == lanes[2]) & (lane >= 192))
    )
    row_order = one_hot(iota((256, 256), 1) == jnp.asarray(row_table())[late][:, None])
    spread = one_hot(iota((N_GZ, 128, 512), 2) == spread_places[:, :, None])
    reorder = one_hot(state_rows[:, None] == iota((STATE, STATE), 1))
    swap_rows = pl.pallas_call(
        swap_kernel,
        out_shape=jax.ShapeDtypeStruct((64, 64), BF),
        out_specs=vmem,
        compiler_params=pltpu.CompilerParams(vmem_limit_bytes=67043328),
        name="swap_rows",
    )()
    to_state = one_hot(iota((CELLS, STATE), 0) == jnp.asarray(STATE_CELLS)[None, :])
    step = to_bf16_dot(reorder, to_bf16_dot(kriging_late, to_state))

    held = [line]
    for d in (1, 2, 3):
        held.append(plane_shift(line, 0, d))
    held[1], select, row_order, spread, step, reorder, place = lax.optimization_barrier(
        (held[1], select, row_order, spread, step, reorder, place)
    )
    pieces = held + [plane_shift(line, 0, 0, 1)]
    pieces += [plane_shift(piece, 0, 0, 1) for piece in held[1:]]

    copies = pl.pallas_call(
        face_kernel,
        out_shape=jax.ShapeDtypeStruct((N_GX // 2, BX, ENS, N_GZ, 24, 128), BF),
        in_specs=[smem, vmem, vmem] + [anywhere] * 12,
        out_specs=anywhere,
        scratch_shapes=[
            pltpu.VMEM((CELLS // DEPTH, N_GZ, 64, DEPTH), BF),
            pltpu.VMEM((CELLS // DEPTH, FACE_COLS, DEPTH), BF),
            pltpu.VMEM((BX, ENS, 24, 128), BF),
            pltpu.SemaphoreType.DMA((CELLS // DEPTH,)),
            pltpu.SemaphoreType.DMA((CELLS // DEPTH,)),
            pltpu.SemaphoreType.DMA((N_GX // 2 * N_GZ,)),
        ],
        compiler_params=pltpu.CompilerParams(vmem_limit_bytes=16 << 20),
        name="face_part",
    )(place, select, row_order, *row_pieces, *pieces)

    place, copies = lax.optimization_barrier((place, copies))
    noise_part = pl.pallas_call(
        noise_kernel,
        out_shape=jax.ShapeDtypeStruct((N_GZ * 64, N_GX * N_GY * PART), BF),
        in_specs=[smem] + [anywhere] * 12,
        out_specs=vmem,
        scratch_shapes=[
            pltpu.VMEM((N_GZ, 64, CELLS), BF),
            pltpu.VMEM((2, 32, 16, CELLS), BF),
            pltpu.VMEM((256, 512), F32),
            pltpu.SemaphoreType.DMA,
            pltpu.SemaphoreType.DMA((2,)),
        ],
        name="noise_part",
    )(place, *row_pieces, *pieces)

    received = lax.all_to_all(copies.reshape(128, 24, 128), ("gx", "gy", "gz"), 0, 0, tiled=True)
    parts = [noise_part[back * 64 : (back + 1) * 64] for back in range(N_GZ)]
    home = [parts[0]]
    for back in (1, 2, 3):
        home.append(line_shift(parts[back], -back))
    other_half = plane_shift(received, 0, 0, 1)

    chosen = pl.pallas_call(
        sweep_kernel,
        out_shape=jax.ShapeDtypeStruct((64, STATE), BF),
        in_specs=[smem] + [anywhere] * 4,
        out_specs=vmem,
        scratch_shapes=[
            pltpu.VMEM((PLANES, SPAN_X * SLOTS * 8, 128), F32),
            pltpu.VMEM((PLANES, LEVELS * 64, 128), F32),
            pltpu.VMEM((PLANES, 64, 128), F32),
            pltpu.VMEM((PLANES, 64, 128), F32),
            pltpu.VMEM((128, 24, 128), BF),
            pltpu.VMEM((128, 24, 128), BF),
            pltpu.VMEM((STATE, STATE), BF),
            pltpu.VMEM((STATE, STATE), BF),
            pltpu.SemaphoreType.DMA((10,)),
        ],
        name="sweep",
    )(place, received, other_half, step, reorder)

    upstream = lax.all_to_all(
        chosen.reshape(N_GY, TILES, STATE), "gy", 0, 0, tiled=True
    ).reshape(ENS * TILES, STATE)

    natural = pl.pallas_call(
        natural_kernel,
        out_shape=jax.ShapeDtypeStruct((TILES * ENS, CELLS), BF),
        in_specs=[smem] + [vmem] * 5,
        out_specs=vmem,
        compiler_params=pltpu.CompilerParams(vmem_limit_bytes=67043328),
        name="natural",
    )(place, *home, spread)

    out = pl.pallas_call(
        final_kernel,
        out_shape=jax.ShapeDtypeStruct((TILES * ENS, CELLS), F32),
        in_specs=[vmem, vmem, anywhere, vmem],
        out_specs=anywhere,
        scratch_shapes=[
            pltpu.VMEM((PARTS, STATE, CELLS // PARTS), BF),
            pltpu.VMEM((PARTS, TILES * ENS, CELLS // PARTS), F32),
            pltpu.SemaphoreType.DMA((PARTS,)),
            pltpu.SemaphoreType.DMA((PARTS,)),
        ],
        name="evolve",
    )(upstream, swap_rows, kriging, natural)
    return out.reshape(BX, BY, BZ, ENS, CELLS)


def solution(mesh):
    placed = (
        P(None, ("gx", "gy")),
        P(),
        P("gx", "gy", "gz", None, None, None),
        P("gx", "gy", "gz", None),
    )

    return jax.shard_map(
        local,
        mesh=mesh,
        in_specs=placed,
        out_specs=P("gx", "gy", "gz", None, None),
        check_vma=False,
    )
```
